128 devices in a mesh: dp: 16 (over x, z), tensor: 8 (over y, core).
Axes of the slice: x: 4, y: 4, z: 4, core: 2. Of those that a mesh axis runs over, the one named last changes fastest.
Arguments:
- activations: bfloat16 [256, 256, 14336], P('dp', None, 'tensor'), may hold values from -6 to 6
- out_grads: bfloat16 [256, 256, 4096], P('dp', None, 'tensor'), may hold values from -0.29882812 to 0.29882812
- lengths: int32 [256], P('dp'), may hold values from 1 to 256, 49152 in all
- bank_in: bfloat16 [16, 128, 64], replicated, may hold values from -0.046875 to 0.046875
- index_in: int32 [112], P('tensor'), may hold values from 0 to 15
- bank_out: bfloat16 [16, 128, 64], replicated, may hold values from -0.09375 to 0.09375
- index_out: int32 [32], P('tensor'), may hold values from 0 to 15
- prior_cov: float32 [4096, 4096], P('dp'), may hold values from -1 to 5, as said below
- val_grads: float32 [4096, 512], P('dp', 'tensor'), may hold values from -0.3 to 0.3
Outputs:
- scores: float32 [256, 512], P('dp', 'tensor')
The draws below stay inside these ranges and needn't reach their ends.
Inputs may be any that keep to these rules, and one draw needn't show every extreme that they name: `lengths`: the longest rollout uses all 256 slots. `prior_cov`: symmetric and positive definite.
All inputs are finite; a program needn't handle non-finite values. No bound on the sum of `lengths` on one device may be relied on, other than what follows from the above.
Results may differ from the reference program's by a relative error of at most 0.0003.
Values sent between devices are 32-bit elements; how exact they have to be, the bound alone decides.
No kernel may reach another device: no remote copies, remote signals or barrier semaphores. Data moves between devices by JAX's collectives and lax.ppermute only.
A program may use at most 128 MiB of HBM per device.

```python
import math
import jax
import jax.numpy as jnp
import numpy as np
from jax import lax

D = 4096
FF = 14336
K = 64
BLK = 128
NBANK = 16
SEQ = 256
NV = 512
ITERS = 6
F = 4096
ROLLOUTS = 256


def draw_prior_cov(key, part):
    key_diag, key_off = jax.random.split(jax.random.fold_in(key, 11))
    row_index = jnp.arange(F, dtype=jnp.float32)
    ramp = 1.0 + 2.0 * row_index / F
    spread = jax.random.uniform(key_diag, (F,), jnp.float32, 0.8, 1.25)
    noise = jax.random.normal(key_off, (F, F), jnp.float32)
    offdiag = (noise + noise.T) * (0.3 / (2.0 * F) ** 0.5)
    on_diagonal = jnp.arange(F)[:, None] == jnp.arange(F)[None, :]
    return jnp.where(on_diagonal, (ramp * spread)[:, None] * jnp.ones((1, F), jnp.float32), offdiag)


def touch_ends(drawn, key, low, high):
    longest = drawn.shape.index(max(drawn.shape))
    spots = []
    for shift in (0, 1):
        where = [jax.random.randint(jax.random.fold_in(key, axis), (), 0, length) for axis, length in enumerate(drawn.shape)]
        where[longest] = (where[longest] + shift) % drawn.shape[longest]
        spots.append(tuple(where))
    return drawn.at[spots[0]].set(low).at[spots[1]].set(high)


def steps_of(stream_key, extent, cuts, low, top_value):
    factor_of = 1.0
    for position, parts in cuts:
        draws = jax.random.uniform(jax.random.fold_in(jax.random.fold_in(stream_key, 6), position), (parts,), jnp.float32, low / len(cuts), top_value / len(cuts))
        factor_of = factor_of * jnp.repeat(jnp.exp(draws), extent[position] // parts).reshape((-1,) + (1,) * (len(extent) - 1 - position))
    return factor_of


def length_profile(amount, total, limit, lean):
    portions = [(1 << 20) // math.isqrt(rank ** lean) + 1 for rank in range(2, amount + 1)]
    rest, holding = total - limit - (amount - 1), [1] * (amount - 1)
    while rest > 0:
        movable = [i for i in range(amount - 1) if holding[i] < limit]
        pool, budget = sum([portions[i] for i in movable]), rest
        for i in movable:
            more = min(limit - holding[i], max(1, budget * portions[i] // pool), rest)
            holding[i] = holding[i] + more
            rest = rest - more
    return np.array([limit] + holding)


def uneven_parts(own_key, count, total, most, lean):
    if count == 2:
        one = jax.random.randint(own_key, (), max(1, total - most), min(most, total - 1) + 1)
        return jnp.stack([one, total - one])
    tallies = jnp.asarray(length_profile(count, total, most, lean), jnp.int32)
    couples = (count - 1) // 2
    source_of, sink = tallies[1:1 + 2 * couples:2], tallies[2:2 + 2 * couples:2]
    slack = jnp.minimum(source_of - 1, most - sink)
    moved = jax.random.randint(jax.random.fold_in(own_key, 1), (couples,), 0, 1 << 20) % (slack + 1)
    tallies = tallies.at[1:1 + 2 * couples:2].set(source_of - moved).at[2:2 + 2 * couples:2].set(sink + moved)
    return tallies[jax.random.permutation(jax.random.fold_in(own_key, 2), count)]


def scatter_about(own_key, dims, scale, bound, cuts=(), held_as=jnp.bfloat16):
    level = steps_of(own_key, dims, cuts, -0.22, 0.18) if cuts else 1.0
    array = jax.random.normal(own_key, dims, jnp.float32) * scale * level
    return jnp.minimum(jnp.maximum(array, -bound), bound).astype(held_as)


def setup_inputs(seed: int = 0) -> dict:
    key_of = jax.random.split(jax.random.key(seed), 10)
    return {
        "activations": scatter_about(key_of[0], (ROLLOUTS, SEQ, FF), 1.0, 6.0, ((0, 16), (2, 8))),
        "out_grads": scatter_about(key_of[1], (ROLLOUTS, SEQ, D), 0.05, 0.29882812, ((0, 16), (2, 8))),
        "lengths": uneven_parts(key_of[2], ROLLOUTS, ROLLOUTS * SEQ * 3 // 4, SEQ, 1).astype(jnp.int32),
        "bank_in": scatter_about(key_of[3], (NBANK, BLK, K), FF ** -0.5, 0.046875),
        "index_in": touch_ends(jax.random.randint(key_of[4], (FF // BLK,), 0, NBANK), jax.random.fold_in(key_of[4], 1), 0, NBANK - 1).astype(jnp.int32),
        "bank_out": scatter_about(key_of[5], (NBANK, BLK, K), D ** -0.5, 0.09375),
        "index_out": touch_ends(jax.random.randint(key_of[6], (D // BLK,), 0, NBANK), jax.random.fold_in(key_of[6], 1), 0, NBANK - 1).astype(jnp.int32),
        "prior_cov": draw_prior_cov(jax.random.fold_in(key_of[9], 71), 0),
        "val_grads": scatter_about(key_of[8], (F, NV), 0.05, 0.3, ((0, 16), (1, 8)), jnp.float32),
    }


HIGH = lax.Precision.HIGHEST


def build_projection(bank, index_table):
    return bank[index_table].reshape(index_table.shape[0] * bank.shape[1], bank.shape[2])


def reference(activations, out_grads, lengths, bank_in, index_in, bank_out, index_out, prior_cov, val_grads):
    proj_in = build_projection(bank_in, index_in)
    proj_out = build_projection(bank_out, index_out)
    act_low = jnp.dot(activations.reshape(ROLLOUTS * SEQ, FF), proj_in, preferred_element_type=jnp.float32).reshape(ROLLOUTS, SEQ, K)
    grad_low = jnp.dot(out_grads.reshape(ROLLOUTS * SEQ, D), proj_out, preferred_element_type=jnp.float32).reshape(ROLLOUTS, SEQ, K)
    used = (jnp.arange(SEQ, dtype=jnp.int32)[None, :] < lengths[:, None]).astype(jnp.float32)
    factors = jnp.einsum("rsk,rsl->rkl", grad_low * used[:, :, None], act_low, precision=HIGH).reshape(ROLLOUTS, K * K)
    covariance = prior_cov + lax.dot_general(factors, factors, (((0,), (0,)), ((), ())), precision=HIGH) / ROLLOUTS
    damping = 0.1 * jnp.trace(covariance) / (K * K)
    solution = jnp.zeros_like(val_grads)
    residual = val_grads
    direction = residual
    norm_now = jnp.sum(residual * residual, axis=0)
    for iteration in range(ITERS):
        image = jnp.dot(covariance, direction, precision=HIGH) + damping * direction
        alpha = norm_now / jnp.sum(direction * image, axis=0)
        solution = solution + alpha * direction
        residual = residual - alpha * image
        if iteration + 1 < ITERS:
            norm_next = jnp.sum(residual * residual, axis=0)
            direction = residual + (norm_next / norm_now) * direction
            norm_now = norm_next
    return jnp.dot(factors, solution, precision=HIGH)
```

```python
import functools

import jax
import jax.numpy as jnp
from jax import lax
from jax.experimental import pallas as pl
from jax.experimental.pallas import tpu as pltpu
from jax.sharding import PartitionSpec as P

ITERS = 6
F32 = jnp.float32
BF16 = jnp.bfloat16
HIGHEST = lax.Precision.HIGHEST

NT = (((1,), (1,)), ((), ()))
NN = (((1,), (0,)), ((), ()))
TN = (((0,), (0,)), ((), ()))

SIDE = 4
CORES = 2
BLK = 256
VMEM = pl.BlockSpec(memory_space=pltpu.VMEM)
SMEM = pl.BlockSpec(memory_space=pltpu.SMEM)


def params(mib):
    return pltpu.CompilerParams(vmem_limit_bytes=mib << 20)


def split(value):
    high = value.astype(BF16)
    return high, (value - high.astype(F32)).astype(BF16)


def mm(a, b, dims):
    return lax.dot_general(a, b, dims, preferred_element_type=F32)


def mm3(a, b, dims):
    return mm(a[0], b[0], dims) + mm(a[1], b[0], dims) + mm(a[0], b[1], dims)


def along_z(step):
    return [(i, (i // SIDE) * SIDE + (i + step) % SIDE) for i in range(16)]


def along_x(step):
    return [(i, (i + step * SIDE) % 16) for i in range(16)]


def along_y(step):
    return [(i, (i + step * CORES) % 8) for i in range(8)]


def other_core():
    return [(i, i ^ 1) for i in range(8)]


def crossed(step, flip):
    pairs = []
    for dp in range(16):
        for tensor in range(8):
            table = along_x(step) if (tensor % CORES) ^ flip else along_z(step)
            pairs.append((dp * 8 + tensor, table[dp][1] * 8 + tensor))
    return pairs


def project_kernel(order, idx_in, idx_out, act, grad, bank_in, bank_out, out, proj_in, proj_out):
    @pl.when(pl.program_id(0) == 0)
    def _():
        for b in range(proj_in.shape[1] // 128):
            proj_in[:, b * 128 : (b + 1) * 128] = bank_in[idx_in[b]]
        for b in range(proj_out.shape[1] // 128):
            proj_out[:, b * 128 : (b + 1) * 128] = bank_out[idx_out[b]]

    out[0, :, 0:64] = mm(act[0], proj_in[...], NT)
    out[0, :, 64:128] = mm(grad[0], proj_out[...], NT)


def project(order, idx_in, idx_out, act, grad, bank_in_t, bank_out_t):
    count = order.shape[0]
    slots, width, model = act.shape[1], act.shape[2], grad.shape[2]
    return pl.pallas_call(
        project_kernel,
        out_shape=jax.ShapeDtypeStruct((count, slots, 128), F32),
        grid_spec=pltpu.PrefetchScalarGridSpec(
            num_scalar_prefetch=3,
            grid=(count,),
            in_specs=[
                pl.BlockSpec((1, slots, width), lambda i, o, a, b: (o[i], 0, 0)),
                pl.BlockSpec((1, slots, model), lambda i, o, a, b: (o[i], 0, 0)),
                pl.BlockSpec(bank_in_t.shape, lambda i, o, a, b: (0, 0, 0)),
                pl.BlockSpec(bank_out_t.shape, lambda i, o, a, b: (0, 0, 0)),
            ],
            out_specs=pl.BlockSpec((1, slots, 128), lambda i, o, a, b: (i, 0, 0)),
            scratch_shapes=[pltpu.VMEM((64, width), BF16), pltpu.VMEM((64, model), BF16)],
        ),
        compiler_params=params(32),
        name="project",
    )(order, idx_in, idx_out, act, grad, bank_in_t, bank_out_t)


def factor_kernel(lens, a0, a1, b1, b2, b3, out):
    slots = a0.shape[1]
    for r in range(2):
        total = (a0[r] + a1[r]) + (b1[r] + b2[r]) + b3[r]
        used = lax.broadcasted_iota(jnp.int32, (slots, 64), 0) < lens[r]
        grad = jnp.where(used, total[:, 64:128], 0.0)
        out[r] = mm3(split(grad), split(total[:, 0:64]), TN)


def factor(lens, pieces):
    return pl.pallas_call(
        factor_kernel,
        out_shape=jax.ShapeDtypeStruct((2, 64, 64), F32),
        in_specs=[SMEM] + [VMEM] * 5,
        out_specs=VMEM,
        name="factor",
    )(lens, *pieces)


def block_at(where, dx, dz):
    x = lax.rem(where[0] + (SIDE - dx), SIDE)
    z = lax.rem(where[1] + (SIDE - dz), SIDE)
    return pl.multiple_of((x * SIDE + z) * BLK, BLK)


def prior_kernel(where, g0, g1, g2, g3, prior, full, out):
    for dx, piece in enumerate((g0, g1, g2, g3)):
        for dz in range(SIDE):
            full[:, pl.ds(block_at(where, dx, dz), BLK)] = piece[:, dz * BLK : (dz + 1) * BLK]
    acc = jnp.zeros((64, BLK), F32)
    for k in range(16):
        cols = slice(k * BLK, (k + 1) * BLK)
        acc = acc + mm3(split(full[:, cols]), split(prior[:, cols]), NT)
    out[0:64, :] = acc
    own = prior[:, pl.ds(pl.multiple_of(where[2] * BLK, BLK), BLK)]
    row = lax.broadcasted_iota(jnp.int32, (BLK, BLK), 0)
    col = lax.broadcasted_iota(jnp.int32, (BLK, BLK), 1)
    out[64:72, :] = jnp.broadcast_to(jnp.sum(jnp.where(row == col, own, 0.0), axis=0, keepdims=True), (8, BLK))


def prior_image(where, pieces, prior):
    return pl.pallas_call(
        prior_kernel,
        out_shape=(
            jax.ShapeDtypeStruct((64, prior.shape[1]), F32),
            jax.ShapeDtypeStruct((72, BLK), F32),
        ),
        in_specs=[SMEM] + [VMEM] * 5,
        out_specs=(VMEM, VMEM),
        compiler_params=params(32),
        name="prior_image",
    )(where, *pieces, prior)


def rowsum(value):
    return jnp.sum(value, axis=1, keepdims=True)


def local_image(stack, cov_hi, cov_lo):
    both = mm(stack[...], cov_hi[...], NT)
    return both[0:64] + both[64:128] + mm(stack[0:64, :], cov_lo[...], NT)


def next_direction(res, direc, stack, beta, old):
    for k in range(16):
        cols = slice(k * BLK, (k + 1) * BLK)
        value = res[:, cols] + beta * old[:, cols]
        direc[:, cols] = value
        high, low = split(value)
        stack[0:64, cols] = high
        stack[64:128, cols] = low


def own_scores(stack, own_hi, own_lo):
    both = mm(stack[...], own_hi[...], NT)
    return both[0:64] + both[64:128] + mm(stack[0:64, :], own_lo[...], NT)


def first_kernel(
    where, near, far, start, image, prior,
    res, direc, rr, score, query, out, cov_hi, cov_lo, own_hi, own_lo,
    f_hi, f_lo, stack,
):
    square = jnp.zeros((64, BLK), F32)
    for part, ref in enumerate((near, far)):
        for k in range(16):
            cols = slice(k * BLK, (k + 1) * BLK)
            for half in range(2):
                rows = slice(half * 64, (half + 1) * 64)
                value = ref[rows, cols]
                square = square + value * value
                high, low = split(value)
                f_hi[part * 128 + half * 64 : part * 128 + (half + 1) * 64, cols] = high
                f_lo[part * 128 + half * 64 : part * 128 + (half + 1) * 64, cols] = low
    rollouts = 256
    diag = jnp.zeros((8, BLK), F32)
    for i in range(16):
        diag = diag + image[i, 64:72, :]
    features = prior.shape[1]
    trace = jnp.sum(diag) / 8.0 + jnp.sum(square) / rollouts
    damping = 0.1 * trace / features

    own_hi[0:8, :] = f_hi[0:8, :]
    own_hi[8:16, :] = f_hi[128:136, :]
    own_lo[0:8, :] = f_lo[0:8, :]
    own_lo[8:16, :] = f_lo[128:136, :]

    for k in range(16):
        cols = slice(k * BLK, (k + 1) * BLK)
        high, low = split(start[:, cols])
        stack[0:64, cols] = high
        stack[64:128, cols] = low
    both = mm(stack[...], f_hi[...], NT)
    q = both[0:64] + both[64:128] + mm(stack[0:64, :], f_lo[...], NT)
    q_parts = split(q * (1.0 / rollouts))
    norm = jnp.zeros((64, 1), F32)
    curve = jnp.zeros((64, 1), F32)
    for k in range(16):
        cols = slice(k * BLK, (k + 1) * BLK)
        b = start[:, cols]
        value = image[k, 0:64, :] + mm3(q_parts, (f_hi[:, cols], f_lo[:, cols]), NN) + damping * b
        res[:, cols] = value
        norm = norm + rowsum(b * b)
        curve = curve + rowsum(b * value)
    alpha = norm / curve
    fresh = jnp.zeros((64, 1), F32)
    for k in range(16):
        cols = slice(k * BLK, (k + 1) * BLK)
        value = start[:, cols] - alpha * res[:, cols]
        res[:, cols] = value
        fresh = fresh + rowsum(value * value)
    next_direction(res, direc, stack, fresh / norm, start)
    rr[...] = jnp.broadcast_to(fresh, rr.shape)
    score[:, 0:8] = alpha * q[:, 0:8]
    score[:, 8:16] = alpha * q[:, 128:136]

    first = pl.multiple_of(where[2] * BLK, BLK)
    mine = (f_hi[:, pl.ds(first, BLK)], f_lo[:, pl.ds(first, BLK)])
    row = lax.broadcasted_iota(jnp.int32, (BLK, BLK), 0)
    col = lax.broadcasted_iota(jnp.int32, (BLK, BLK), 1)
    for k in range(16):
        cols = slice(k * BLK, (k + 1) * BLK)
        value = prior[:, cols] + mm3(mine, (f_hi[:, cols], f_lo[:, cols]), TN) * (1.0 / rollouts)
        value = value + jnp.where(row + where[2] * BLK == col + k * BLK, damping, 0.0)
        high, low = split(value)
        cov_hi[:, cols] = high
        cov_lo[:, cols] = low
    out[...] = local_image(stack, cov_hi, cov_lo)
    query[...] = own_scores(stack, own_hi, own_lo)


def first_step(where, near, far, start, image, prior):
    n = prior.shape[1]
    sds = jax.ShapeDtypeStruct
    return pl.pallas_call(
        first_kernel,
        out_shape=(
            sds((64, n), F32), sds((64, n), F32), sds((64, 128), F32),
            sds((64, 16), F32), sds((64, 16), F32), sds((64, BLK), F32),
            sds((BLK, n), BF16), sds((BLK, n), BF16), sds((16, n), BF16), sds((16, n), BF16),
        ),
        in_specs=[SMEM] + [VMEM] * 5,
        out_specs=(VMEM,) * 10,
        scratch_shapes=[
            pltpu.VMEM((256, n), BF16), pltpu.VMEM((256, n), BF16), pltpu.VMEM((128, n), BF16),
        ],
        compiler_params=params(48),
        name="first_step",
    )(where, near, far, start, image, prior)


def step_kernel(
    where, g0, g1, g2, g3, res_in, direc_in, rr_in, score_in, query_in,
    cov_hi, cov_lo, own_hi, own_lo,
    res, direc, rr, score, query, out, stack, *, last,
):
    curve = jnp.zeros((64, 1), F32)
    for dx, piece in enumerate((g0, g1, g2, g3)):
        for dz in range(SIDE):
            at = pl.ds(block_at(where, dx, dz), BLK)
            curve = curve + rowsum(direc_in[:, at] * piece[:, dz * BLK : (dz + 1) * BLK])
    norm = rr_in[:, 0:1]
    alpha = norm / curve
    fresh = jnp.zeros((64, 1), F32)
    for dx, piece in enumerate((g0, g1, g2, g3)):
        for dz in range(SIDE):
            at = pl.ds(block_at(where, dx, dz), BLK)
            value = res_in[:, at] - alpha * piece[:, dz * BLK : (dz + 1) * BLK]
            res[:, at] = value
            fresh = fresh + rowsum(value * value)
    next_direction(res, direc, stack, fresh / norm, direc_in)
    rr[...] = jnp.broadcast_to(fresh, rr.shape)
    score[...] = score_in[...] + alpha * query_in[...]
    image = local_image(stack, cov_hi, cov_lo)
    query[...] = own_scores(stack, own_hi, own_lo)
    if last:
        mine = direc[:, pl.ds(pl.multiple_of(where[2] * BLK, BLK), BLK)]
        ones = jnp.ones((8, BLK), F32)
        out[0] = lax.dot_general(ones, mine * image, NT, precision=HIGHEST, preferred_element_type=F32)
        out[1] = lax.dot_general(ones, fresh * (lax.broadcasted_iota(jnp.int32, (64, BLK), 1) == 0).astype(F32), NT, precision=HIGHEST, preferred_element_type=F32)
    else:
        out[...] = image


def cg_step(where, pieces, state, cov, last):
    n = cov[0].shape[1]
    sds = jax.ShapeDtypeStruct
    return pl.pallas_call(
        functools.partial(step_kernel, last=last),
        out_shape=(
            sds((64, n), F32), sds((64, n), F32), sds((64, 128), F32),
            sds((64, 16), F32), sds((64, 16), F32),
            sds((2, 8, 64) if last else (64, BLK), F32),
        ),
        in_specs=[SMEM] + [VMEM] * 13,
        out_specs=(VMEM,) * 6,
        scratch_shapes=[pltpu.VMEM((128, n), BF16)],
        compiler_params=params(48),
        name="last_step" if last else "cg_step",
    )(where, *pieces, *state, *cov)


def finish_kernel(where, sums, norm, score, query, out):
    curve = sums[0]
    for i in range(1, 16):
        curve = curve + sums[i]
    alpha = norm[0:1, :] / curve[0:1, :]
    row = lax.broadcasted_iota(jnp.int32, (16, 16), 0)
    slot = lax.broadcasted_iota(jnp.int32, (16, 16), 1)
    core = lax.rem(slot // 8 + where[4], CORES)
    y = lax.rem(where[3] + SIDE - lax.rem(slot, 8) // 2, SIDE)
    pick = (row == core * 8 + y * 2 + lax.rem(slot, 2)).astype(F32)
    dot = functools.partial(lax.dot_general, dimension_numbers=NT, precision=HIGHEST, preferred_element_type=F32)
    out[...] = dot(pick, score[...]) + alpha * dot(pick, query[...])


def finish(where, sums, norm, score, query):
    return pl.pallas_call(
        finish_kernel,
        out_shape=jax.ShapeDtypeStruct((16, 64), F32),
        in_specs=[SMEM] + [VMEM] * 4,
        out_specs=VMEM,
        name="finish",
    )(where, sums, norm, score, query)


def gather_blocks(block):
    line = [block] + [lax.ppermute(block, "dp", along_z(d)) for d in (1, 2, 3)]
    line = jnp.concatenate(line, axis=1)
    return [line] + [lax.ppermute(line, "dp", along_x(d)) for d in (1, 2, 3)]


def per_device(
    activations, out_grads, lengths, bank_in, index_in, bank_out, index_out, prior_cov, val_grads
):
    dp = lax.axis_index("dp").astype(jnp.int32)
    tensor = lax.axis_index("tensor").astype(jnp.int32)
    y, core = tensor // CORES, tensor % CORES
    where = jnp.stack([dp // SIDE, dp % SIDE, dp, y, core])
    slot = jnp.arange(8, dtype=jnp.int32)
    line = ((y + slot // 2) % SIDE) * 2 + slot % 2

    start_pieces = gather_blocks(val_grads.T)

    banks = (bank_in.transpose(0, 2, 1), bank_out.transpose(0, 2, 1))
    theirs = project((1 - core) * 8 + line, index_in, index_out, activations, out_grads, *banks)
    from_core = lax.ppermute(theirs, "tensor", other_core())
    mine = project(core * 8 + line, index_in, index_out, activations, out_grads, *banks)
    from_y = [
        lax.ppermute(mine[2 * d : 2 * d + 2] + from_core[2 * d : 2 * d + 2], "tensor", along_y(d))
        for d in (1, 2, 3)
    ]
    lens = lax.dynamic_slice_in_dim(lengths, core * 8 + y * 2, 2)

    start, image_here = prior_image(where, start_pieces, prior_cov)
    image = lax.all_gather(image_here, "dp", axis=0)

    own = factor(lens, [mine[0:2], from_core[0:2], *from_y]).reshape(2, 4096)
    part = jnp.concatenate([own] + [lax.ppermute(own, "tensor", along_y(d)) for d in (1, 2, 3)], axis=0)
    for flip in (0, 1):
        moved = [lax.ppermute(part, ("dp", "tensor"), crossed(d, flip)) for d in (1, 2, 3)]
        part = jnp.concatenate([part] + moved, axis=0)
    far = lax.ppermute(part, "tensor", other_core())

    first = first_step(where, part, far, start, image, prior_cov)
    state, out, cov = first[0:5], first[5], first[6:10]
    for iteration in range(1, ITERS - 1):
        pieces = gather_blocks(out)
        *state, out = cg_step(where, pieces, state, cov, iteration + 2 == ITERS)
    sums = lax.all_to_all(jnp.broadcast_to(out[0], (16, 8, 64)), "dp", 0, 0)
    return finish(where, sums, out[1], state[3], state[4])


def solution(mesh):
    return jax.shard_map(
        per_device,
        mesh=mesh,
        in_specs=(
            P("dp", None, "tensor"),
            P("dp", None, "tensor"),
            P("dp"),
            P(),
            P("tensor"),
            P(),
            P("tensor"),
            P("dp", None),
            P("dp", "tensor"),
        ),
        out_specs=P("dp", "tensor"),
        check_vma=False,
    )
```

```python
import functools

import jax
import jax.numpy as jnp
from jax import lax
from jax.experimental import pallas as pl
from jax.experimental.pallas import tpu as pltpu
from jax.sharding import PartitionSpec as P

ITERS = 6
F32 = jnp.float32
BF16 = jnp.bfloat16
HIGHEST = lax.Precision.HIGHEST

NT = (((1,), (1,)), ((), ()))
NN = (((1,), (0,)), ((), ()))
TN = (((0,), (0,)), ((), ()))

SIDE = 4
CORES = 2
BLK = 256
VMEM = pl.BlockSpec(memory_space=pltpu.VMEM)
SMEM = pl.BlockSpec(memory_space=pltpu.SMEM)
HBM = pl.BlockSpec(memory_space=pltpu.HBM)


def params(mib):
    return pltpu.CompilerParams(vmem_limit_bytes=mib << 20)


def in_hbm(values):
    return [pltpu.with_memory_space_constraint(v, pltpu.HBM) for v in values]


def place():
    dp = lax.axis_index("dp").astype(jnp.int32)
    tensor = lax.axis_index("tensor").astype(jnp.int32)
    return lax.div(dp, SIDE), lax.rem(dp, SIDE), dp, lax.div(tensor, CORES), lax.rem(tensor, CORES)


def fetch(sources, targets, sems):
    copies = [pltpu.make_async_copy(a, b, sems.at[i]) for i, (a, b) in enumerate(zip(sources, targets))]
    for copy in copies:
        copy.start()
    return copies


def cost(flops, nbytes):
    return pl.CostEstimate(flops=flops, bytes_accessed=nbytes, transcendentals=0)


def split(value):
    high = value.astype(BF16)
    return high, (value - high.astype(F32)).astype(BF16)


def mm(a, b, dims):
    return lax.dot_general(a, b, dims, preferred_element_type=F32)


def mm3(a, b, dims):
    return mm(a[0], b[0], dims) + mm(a[1], b[0], dims) + mm(a[0], b[1], dims)


def along_z(step):
    return [(i, (i // SIDE) * SIDE + (i + step) % SIDE) for i in range(16)]


def along_x(step):
    return [(i, (i + step * SIDE) % 16) for i in range(16)]


def along_y(step):
    return [(i, (i + step * CORES) % 8) for i in range(8)]


def other_core():
    return [(i, i ^ 1) for i in range(8)]


def crossed(step, flip):
    pairs = []
    for dp in range(16):
        for tensor in range(8):
            table = along_x(step) if (tensor % CORES) ^ flip else along_z(step)
            pairs.append((dp * 8 + tensor, table[dp][1] * 8 + tensor))
    return pairs


def project_kernel(order, idx_in, idx_out, act, grad, bank_in, bank_out, out, proj_in, proj_out):
    @pl.when(pl.program_id(0) == 0)
    def _():
        for b in range(proj_in.shape[1] // 128):
            proj_in[:, b * 128 : (b + 1) * 128] = bank_in[idx_in[b]]
        for b in range(proj_out.shape[1] // 128):
            proj_out[:, b * 128 : (b + 1) * 128] = bank_out[idx_out[b]]

    out[0, :, 0:64] = mm(act[0], proj_in[...], NT)
    out[0, :, 64:128] = mm(grad[0], proj_out[...], NT)


def project(order, idx_in, idx_out, act, grad, bank_in_t, bank_out_t):
    idx_in, idx_out, act, grad, bank_in_t, bank_out_t = in_hbm(
        [idx_in, idx_out, act, grad, bank_in_t, bank_out_t]
    )
    count = order.shape[0]
    slots, width, model = act.shape[1], act.shape[2], grad.shape[2]
    return pl.pallas_call(
        project_kernel,
        out_shape=jax.ShapeDtypeStruct((count, slots, 128), F32),
        grid_spec=pltpu.PrefetchScalarGridSpec(
            num_scalar_prefetch=3,
            grid=(count,),
            in_specs=[
                pl.BlockSpec((1, slots, width), lambda i, o, a, b: (o[i], 0, 0)),
                pl.BlockSpec((1, slots, model), lambda i, o, a, b: (o[i], 0, 0)),
                pl.BlockSpec(bank_in_t.shape, lambda i, o, a, b: (0, 0, 0)),
                pl.BlockSpec(bank_out_t.shape, lambda i, o, a, b: (0, 0, 0)),
            ],
            out_specs=pl.BlockSpec((1, slots, 128), lambda i, o, a, b: (i, 0, 0)),
            scratch_shapes=[pltpu.VMEM((64, width), BF16), pltpu.VMEM((64, model), BF16)],
        ),
        compiler_params=params(12),
        cost_estimate=cost(2 * count * slots * (width + model) * 256, count * slots * (width + model) * 2),
        name="project",
    )(order, idx_in, idx_out, act, grad, bank_in_t, bank_out_t)


def factor_kernel(lens, a0, a1, b1, b2, b3, out, v0, v1, w1, w2, w3, sems):
    copies = fetch((a0, a1, b1, b2, b3), (v0, v1, w1, w2, w3), sems)
    _, _, _, y, core = place()
    for copy in copies:
        copy.wait()
    slots = v0.shape[1]
    for r in range(2):
        total = (v0[r] + v1[r]) + (w1[r] + w2[r]) + w3[r]
        used = lax.broadcasted_iota(jnp.int32, (slots, 64), 0) < lens[core * 8 + y * 2 + r]
        grad = jnp.where(used, total[:, 64:128], 0.0)
        out[r] = mm3(split(grad), split(total[:, 0:64]), TN)


def factor(lens, pieces):
    shape = pieces[0].shape
    return pl.pallas_call(
        factor_kernel,
        out_shape=jax.ShapeDtypeStruct((2, 64, 64), F32),
        in_specs=[SMEM] + [HBM] * 5,
        out_specs=VMEM,
        scratch_shapes=[pltpu.VMEM(shape, F32)] * 5 + [pltpu.SemaphoreType.DMA((5,))],
        name="factor",
    )(lens, *in_hbm(pieces))


def block_at(where, first, second):
    core = where[4]
    dx = core * first + (1 - core) * second
    dz = first + second - dx
    x = lax.rem(where[0] + SIDE - dx, SIDE)
    z = lax.rem(where[1] + SIDE - dz, SIDE)
    return pl.multiple_of((x * SIDE + z) * BLK, BLK)


def prior_kernel(g0, g1, g2, g3, prior_hbm, full_out, stack_out, pri_hi, pri_lo, out, g, prior, full, stack, sems):
    pieces = fetch((g0, g1, g2, g3), [g.at[i] for i in range(4)], sems)
    rows = [pl.ds(i * 64, 64) for i in range(4)]
    priors = fetch([prior_hbm.at[r] for r in rows], [prior.at[r] for r in rows], sems.at[pl.ds(4, 4)])
    where = place()
    for second in range(SIDE):
        pieces[second].wait()
        for first in range(SIDE):
            value = g[second, :, first * BLK : (first + 1) * BLK]
            at = pl.ds(block_at(where, first, second), BLK)
            full[:, at] = value
            stack[0:64, at], stack[64:128, at] = split(value)
    full_out[...] = full[...]
    stack_out[...] = stack[...]
    for i in range(4):
        priors[i].wait()
        for k in range(16):
            part = (rows[i], slice(k * BLK, (k + 1) * BLK))
            pri_hi[part], pri_lo[part] = split(prior[part])
    out[0:64, :] = local_image(stack, pri_hi, pri_lo)
    own = prior[:, pl.ds(pl.multiple_of(where[2] * BLK, BLK), BLK)]
    row = lax.broadcasted_iota(jnp.int32, (BLK, BLK), 0)
    col = lax.broadcasted_iota(jnp.int32, (BLK, BLK), 1)
    out[64:72, :] = jnp.broadcast_to(jnp.sum(jnp.where(row == col, own, 0.0), axis=0, keepdims=True), (8, BLK))


def prior_image(pieces, prior):
    n = prior.shape[1]
    sds = jax.ShapeDtypeStruct
    return pl.pallas_call(
        prior_kernel,
        out_shape=(
            pltpu.HBM((64, n), F32), pltpu.HBM((128, n), BF16), pltpu.HBM((BLK, n), BF16),
            pltpu.HBM((BLK, n), BF16), sds((72, BLK), F32),
        ),
        in_specs=[HBM] * 5,
        out_specs=(VMEM,) * 5,
        scratch_shapes=[
            pltpu.VMEM((4, 64, 4 * BLK), F32), pltpu.VMEM((BLK, n), F32),
            pltpu.VMEM((64, n), F32), pltpu.VMEM((128, n), BF16), pltpu.SemaphoreType.DMA((8,)),
        ],
        compiler_params=params(24),
        cost_estimate=cost(6 * 256 * 256 * n, 8 * 256 * n),
        name="prior_image",
    )(*in_hbm([*pieces, prior]))


def rowsum(value):
    return jnp.sum(value, axis=1, keepdims=True)


def local_image(stack, cov_hi, cov_lo):
    both = mm(stack[...], cov_hi[...], NT)
    return both[0:64] + both[64:128] + mm(stack[0:64, :], cov_lo[...], NT)


def next_direction(res, direc, stack, beta, old):
    for k in range(16):
        cols = slice(k * BLK, (k + 1) * BLK)
        value = res[:, cols] + beta * old[:, cols]
        direc[:, cols] = value
        high, low = split(value)
        stack[0:64, cols] = high
        stack[64:128, cols] = low


def own_scores(stack, own_hi, own_lo):
    both = mm(stack[...], own_hi[...], NT)
    return both[0:64] + both[64:128] + mm(stack[0:64, :], own_lo[...], NT)


def first_kernel(
    n0, n1, n2, n3, m0, m1, m2, m3, start_hbm, stack_hbm, image_hbm, pri_hi_hbm, pri_lo_hbm,
    res, direc, rr, score, query, damp, out, f_hi, f_lo, own_hi, own_lo,
    pieces, start, start_stack, image, pri_hi, pri_lo, stack, sems,
):
    begin = fetch((stack_hbm, start_hbm), (start_stack, start), sems)
    copies = fetch((n0, n1, n2, n3, m0, m1, m2, m3), [pieces.at[i] for i in range(8)], sems.at[pl.ds(5, 8)])
    later = fetch((image_hbm, pri_hi_hbm, pri_lo_hbm), (image, pri_hi, pri_lo), sems.at[pl.ds(2, 3)])
    where = place()
    square = jnp.zeros((32, BLK), F32)
    for i in range(8):
        copies[i].wait()
        rows = slice(i * 32, (i + 1) * 32)
        for k in range(16):
            cols = slice(k * BLK, (k + 1) * BLK)
            value = pieces[i, :, cols]
            square = square + value * value
            f_hi[rows, cols], f_lo[rows, cols] = split(value)
    for copy in begin:
        copy.wait()
    rollouts = f_hi.shape[0]
    half = rollouts // 2
    for ref, f in ((own_hi, f_hi), (own_lo, f_lo)):
        ref[0:8, :] = f[0:8, :]
        ref[8:16, :] = f[half : half + 8, :]

    q = local_image(start_stack, f_hi, f_lo)
    later[0].wait()
    diag = jnp.zeros((8, BLK), F32)
    for i in range(16):
        diag = diag + image[i, 64:72, :]
    features = f_hi.shape[1]
    trace = jnp.sum(diag) / 8.0 + jnp.sum(square) / rollouts
    damping = 0.1 * trace / features
    damp[...] = jnp.full(damp.shape, damping, F32)
    q_parts = split(q * (1.0 / rollouts))
    norm = jnp.zeros((64, 1), F32)
    curve = jnp.zeros((64, 1), F32)
    for k in range(16):
        cols = slice(k * BLK, (k + 1) * BLK)
        b = start[:, cols]
        value = image[k, 0:64, :] + mm3(q_parts, (f_hi[:, cols], f_lo[:, cols]), NN) + damping * b
        res[:, cols] = value
        norm = norm + rowsum(b * b)
        curve = curve + rowsum(b * value)
    alpha = norm / curve
    fresh = jnp.zeros((64, 1), F32)
    for k in range(16):
        cols = slice(k * BLK, (k + 1) * BLK)
        value = start[:, cols] - alpha * res[:, cols]
        res[:, cols] = value
        fresh = fresh + rowsum(value * value)
    next_direction(res, direc, stack, fresh / norm, start)
    rr[...] = jnp.broadcast_to(fresh, rr.shape)
    score[:, 0:8] = alpha * q[:, 0:8]
    score[:, 8:16] = alpha * q[:, half : half + 8]

    mine = pl.ds(pl.multiple_of(where[2] * BLK, BLK), BLK)
    q = local_image(stack, f_hi, f_lo)
    query[:, 0:8] = q[:, 0:8]
    query[:, 8:16] = q[:, half : half + 8]
    low_rank = mm3(split(q * (1.0 / rollouts)), (f_hi[:, mine], f_lo[:, mine]), NN)
    later[1].wait()
    later[2].wait()
    out[...] = local_image(stack, pri_hi, pri_lo) + low_rank + damping * direc[:, mine]


def first_step(pieces, start, start_stack, image, prior):
    n = start.shape[1]
    sds = jax.ShapeDtypeStruct
    return pl.pallas_call(
        first_kernel,
        out_shape=(
            sds((64, n), F32), sds((64, n), F32), sds((64, 128), F32),
            sds((64, 16), F32), sds((64, 16), F32), sds((8, 128), F32), sds((64, BLK), F32),
            sds((256, n), BF16), sds((256, n), BF16), sds((16, n), BF16), sds((16, n), BF16),
        ),
        in_specs=[HBM] * 13,
        out_specs=(VMEM,) * 11,
        scratch_shapes=[
            pltpu.VMEM((8, 32, n), F32), pltpu.VMEM((64, n), F32), pltpu.VMEM((128, n), BF16),
            pltpu.VMEM(image.shape, F32), pltpu.VMEM((BLK, n), BF16), pltpu.VMEM((BLK, n), BF16),
            pltpu.VMEM((128, n), BF16), pltpu.SemaphoreType.DMA((13,)),
        ],
        compiler_params=params(32),
        name="first_step",
    )(*in_hbm([*pieces, start, start_stack, image, *prior]))


def covariance_kernel(f_hi, f_lo, prior, damp, cov_hi, cov_lo):
    first = pl.multiple_of(place()[2] * BLK, BLK)
    mine = (f_hi[:, pl.ds(first, BLK)], f_lo[:, pl.ds(first, BLK)])
    row = lax.broadcasted_iota(jnp.int32, (BLK, BLK), 0)
    col = lax.broadcasted_iota(jnp.int32, (BLK, BLK), 1)
    for k in range(16):
        cols = slice(k * BLK, (k + 1) * BLK)
        value = prior[:, cols] + mm3(mine, (f_hi[:, cols], f_lo[:, cols]), TN) * (1.0 / f_hi.shape[0])
        value = value + jnp.where(row + first == col + k * BLK, damp[0:1, 0:1], 0.0)
        cov_hi[:, cols], cov_lo[:, cols] = split(value)


def covariance(f_hi, f_lo, prior, damp):
    n = prior.shape[1]
    return pl.pallas_call(
        covariance_kernel,
        out_shape=(jax.ShapeDtypeStruct((BLK, n), BF16),) * 2,
        in_specs=[VMEM] * 4,
        out_specs=(VMEM, VMEM),
        compiler_params=params(20),
        cost_estimate=cost(6 * 256 * 256 * n, 12 * 256 * n),
        name="covariance",
    )(f_hi, f_lo, prior, damp)


def step_kernel(
    g0, g1, g2, g3, res_in, direc_in, rr_in, score_in, query_in, cov_hi, cov_lo, own_hi, own_lo,
    rr, score, query, out, res, direc, stack, *, last,
):
    where = place()
    curve = jnp.zeros((64, 1), F32)
    for second, piece in enumerate((g0, g1, g2, g3)):
        for first in range(SIDE):
            at = pl.ds(block_at(where, first, second), BLK)
            curve = curve + rowsum(direc_in[:, at] * piece[:, first * BLK : (first + 1) * BLK])
    norm = rr_in[:, 0:1]
    alpha = norm / curve
    fresh = jnp.zeros((64, 1), F32)
    for second, piece in enumerate((g0, g1, g2, g3)):
        for first in range(SIDE):
            at = pl.ds(block_at(where, first, second), BLK)
            value = res_in[:, at] - alpha * piece[:, first * BLK : (first + 1) * BLK]
            res[:, at] = value
            fresh = fresh + rowsum(value * value)
    next_direction(res, direc, stack, fresh / norm, direc_in)
    rr[...] = jnp.broadcast_to(fresh, rr.shape)
    score[...] = score_in[...] + alpha * query_in[...]
    image = local_image(stack, cov_hi, cov_lo)
    query[...] = own_scores(stack, own_hi, own_lo)
    if last:
        mine = direc[:, pl.ds(pl.multiple_of(where[2] * BLK, BLK), BLK)]
        ones = jnp.ones((8, BLK), F32)
        curve = lax.dot_general(ones, mine * image, NT, precision=HIGHEST, preferred_element_type=F32)
        for i in range(16):
            out[i, :, 0:64] = curve
            out[i, :, 64:128] = curve
    else:
        out[...] = image


def cg_step(pieces, state, cov, last):
    n = cov[0].shape[1]
    sds = jax.ShapeDtypeStruct
    small = (
        sds((64, 128), F32), sds((64, 16), F32), sds((64, 16), F32),
        sds((16, 8, 128) if last else (64, BLK), F32),
    )
    large = [] if last else [sds((64, n), F32)] * 2
    scratch = [pltpu.VMEM((64, n), F32)] * 2 if last else []
    return pl.pallas_call(
        functools.partial(step_kernel, last=last),
        out_shape=(*small, *large),
        in_specs=[VMEM] * 13,
        out_specs=(VMEM,) * (4 + len(large)),
        scratch_shapes=[*scratch, pltpu.VMEM((128, n), BF16)],
        compiler_params=params(20),
        name="last_step" if last else "cg_step",
    )(*pieces, *state, *cov)


def finish_kernel(sums, rr, score, query, out):
    curve = sums[0]
    for i in range(1, 16):
        curve = curve + sums[i]
    dot = functools.partial(lax.dot_general, dimension_numbers=NT, precision=HIGHEST, preferred_element_type=F32)
    eye = lax.broadcasted_iota(jnp.int32, (64, 64), 0) == lax.broadcasted_iota(jnp.int32, (64, 64), 1)
    norm = jnp.sum(jnp.where(eye, jnp.broadcast_to(rr[:, 0:1], (64, 64)), 0.0), axis=0, keepdims=True)
    alpha = norm / curve[0:1, 0:64]
    _, _, _, y_here, core_here = place()
    row = lax.broadcasted_iota(jnp.int32, (16, 16), 0)
    slot = lax.broadcasted_iota(jnp.int32, (16, 16), 1)
    core = lax.rem(slot // 8 + core_here, CORES)
    y = lax.rem(y_here + SIDE - lax.rem(slot, 8) // 2, SIDE)
    pick = (row == core * 8 + y * 2 + lax.rem(slot, 2)).astype(F32)
    out[...] = dot(pick, score[...]) + alpha * dot(pick, query[...])


def finish(sums, rr, score, query):
    return pl.pallas_call(
        finish_kernel,
        out_shape=jax.ShapeDtypeStruct((16, 64), F32),
        in_specs=[VMEM] * 4,
        out_specs=VMEM,
        name="finish",
    )(sums, rr, score, query)


BOTH = ("dp", "tensor")


def first_stage(block):
    line = [block] + [lax.ppermute(block, BOTH, crossed(d, 0)) for d in (1, 2, 3)]
    return jnp.concatenate(line, axis=1)


def second_stage(line):
    return [line] + [lax.ppermute(line, BOTH, crossed(d, 1)) for d in (1, 2, 3)]


def per_device(
    activations, out_grads, lengths, bank_in, index_in, bank_out, index_out, prior_cov, val_grads
):
    _, _, _, y, core = place()
    slot = jnp.arange(8, dtype=jnp.int32)
    line = lax.rem(y + slot // 2, SIDE) * 2 + slot % 2

    banks = (bank_in.transpose(0, 2, 1), bank_out.transpose(0, 2, 1))
    start_line = first_stage(val_grads.T)
    theirs = project((1 - core) * 8 + line, index_in, index_out, activations, out_grads, *banks)
    order, start_line, theirs = lax.optimization_barrier((core * 8 + line, start_line, theirs))
    start_pieces = second_stage(start_line)
    from_core = lax.ppermute(theirs, "tensor", other_core())
    mine = project(order, index_in, index_out, activations, out_grads, *banks)
    mine, start_pieces = lax.optimization_barrier((mine, start_pieces))
    from_y = [
        lax.ppermute(mine[2 * d : 2 * d + 2] + from_core[2 * d : 2 * d + 2], "tensor", along_y(d))
        for d in (1, 2, 3)
    ]

    start, start_stack, pri_hi, pri_lo, image_here = prior_image(start_pieces, prior_cov)
    image = lax.all_gather(image_here, "dp", axis=0)
    lengths, start = lax.optimization_barrier((lengths, start))

    own = factor(lengths, [mine[0:2], from_core[0:2], *from_y]).reshape(2, 4096)
    part = jnp.concatenate([own] + [lax.ppermute(own, "tensor", along_y(d)) for d in (1, 2, 3)], axis=0)
    moved = [lax.ppermute(part, BOTH, crossed(d, 0)) for d in (1, 2, 3)]
    near = second_stage(jnp.concatenate([part] + moved, axis=0))
    far = [lax.ppermute(piece, "tensor", other_core()) for piece in near]

    first = first_step(near + far, start, start_stack, image, (pri_hi, pri_lo))
    state, damp, out, f_hi, f_lo, own_hi, own_lo = first[0:5], *first[5:11]
    cov = (*covariance(f_hi, f_lo, prior_cov, damp), own_hi, own_lo)
    for iteration in range(1, ITERS - 1):
        pieces = second_stage(first_stage(out))
        rr, score, query, out, *large = cg_step(pieces, state, cov, iteration + 2 == ITERS)
        state = (*large, rr, score, query)
    sums = lax.all_to_all(out, "dp", 0, 0, tiled=True)
    return finish(sums, rr, score, query)


def solution(mesh):
    return jax.shard_map(
        per_device,
        mesh=mesh,
        in_specs=(
            P("dp", None, "tensor"),
            P("dp", None, "tensor"),
            P("dp"),
            P(),
            P("tensor"),
            P(),
            P("tensor"),
            P("dp", None),
            P("dp", "tensor"),
        ),
        out_specs=P("dp", "tensor"),
        check_vma=False,
    )
```

```python
import functools

import jax
import jax.numpy as jnp
from jax import lax
from jax.experimental import pallas as pl
from jax.experimental.pallas import tpu as pltpu
from jax.sharding import PartitionSpec as P

ITERS = 6
F32 = jnp.float32
BF16 = jnp.bfloat16
HIGHEST = lax.Precision.HIGHEST

NT = (((1,), (1,)), ((), ()))
NN = (((1,), (0,)), ((), ()))
TN = (((0,), (0,)), ((), ()))

SIDE = 4
CORES = 2
BLK = 256
SEG = 32
OWN = 512
COLS = 32
VMEM = pl.BlockSpec(memory_space=pltpu.VMEM)
SMEM = pl.BlockSpec(memory_space=pltpu.SMEM)
HBM = pl.BlockSpec(memory_space=pltpu.HBM)


def params(mib):
    return pltpu.CompilerParams(vmem_limit_bytes=mib << 20)


def in_hbm(values):
    return [pltpu.with_memory_space_constraint(v, pltpu.HBM) for v in values]


def place():
    dp = lax.axis_index("dp").astype(jnp.int32)
    tensor = lax.axis_index("tensor").astype(jnp.int32)
    return lax.div(dp, SIDE), lax.rem(dp, SIDE), dp, lax.div(tensor, CORES), lax.rem(tensor, CORES)


def fetch(sources, targets, sems):
    copies = [pltpu.make_async_copy(a, b, sems.at[i]) for i, (a, b) in enumerate(zip(sources, targets))]
    for copy in copies:
        copy.start()
    return copies


def cost(flops, nbytes):
    return pl.CostEstimate(flops=flops, bytes_accessed=nbytes, transcendentals=0)


def split(value):
    high = value.astype(BF16)
    return high, (value - high.astype(F32)).astype(BF16)


def mm(a, b, dims):
    return lax.dot_general(a, b, dims, preferred_element_type=F32)


def mm3(a, b, dims):
    return mm(a[0], b[0], dims) + mm(a[1], b[0], dims) + mm(a[0], b[1], dims)


def along_z(step):
    return [(i, (i // SIDE) * SIDE + (i + step) % SIDE) for i in range(16)]


def along_x(step):
    return [(i, (i + step * SIDE) % 16) for i in range(16)]


def along_y(step):
    return [(i, (i + step * CORES) % 8) for i in range(8)]


def other_core():
    return [(i, i ^ 1) for i in range(8)]


def crossed(step, flip):
    pairs = []
    for dp in range(16):
        for tensor in range(8):
            table = along_x(step) if (tensor % CORES) ^ flip else along_z(step)
            pairs.append((dp * 8 + tensor, table[dp][1] * 8 + tensor))
    return pairs


def project_kernel(order, idx_in, idx_out, act, grad, bank_in, bank_out, out, proj_in, proj_out):
    @pl.when(pl.program_id(0) == 0)
    def _():
        for b in range(proj_in.shape[1] // 128):
            proj_in[:, b * 128 : (b + 1) * 128] = bank_in[idx_in[b]]
        for b in range(proj_out.shape[1] // 128):
            proj_out[:, b * 128 : (b + 1) * 128] = bank_out[idx_out[b]]

    out[0, :, 0:64] = mm(act[0], proj_in[...], NT)
    out[0, :, 64:128] = mm(grad[0], proj_out[...], NT)


def project(order, idx_in, idx_out, act, grad, bank_in_t, bank_out_t):
    idx_in, idx_out, act, grad, bank_in_t, bank_out_t = in_hbm(
        [idx_in, idx_out, act, grad, bank_in_t, bank_out_t]
    )
    count = order.shape[0]
    slots, width, model = act.shape[1], act.shape[2], grad.shape[2]
    return pl.pallas_call(
        project_kernel,
        out_shape=jax.ShapeDtypeStruct((count, slots, 128), F32),
        grid_spec=pltpu.PrefetchScalarGridSpec(
            num_scalar_prefetch=3,
            grid=(count,),
            in_specs=[
                pl.BlockSpec((1, slots, width), lambda i, o, a, b: (o[i], 0, 0)),
                pl.BlockSpec((1, slots, model), lambda i, o, a, b: (o[i], 0, 0)),
                pl.BlockSpec(bank_in_t.shape, lambda i, o, a, b: (0, 0, 0)),
                pl.BlockSpec(bank_out_t.shape, lambda i, o, a, b: (0, 0, 0)),
            ],
            out_specs=pl.BlockSpec((1, slots, 128), lambda i, o, a, b: (i, 0, 0)),
            scratch_shapes=[pltpu.VMEM((64, width), BF16), pltpu.VMEM((64, model), BF16)],
        ),
        compiler_params=params(12),
        cost_estimate=cost(2 * count * slots * (width + model) * 256, count * slots * (width + model) * 2),
        name="project",
    )(order, idx_in, idx_out, act, grad, bank_in_t, bank_out_t)


def factor_kernel(lens, a0, a1, b1, b2, b3, out, v0, v1, w1, w2, w3, sems):
    copies = fetch((a0, a1, b1, b2, b3), (v0, v1, w1, w2, w3), sems)
    _, _, _, y, core = place()
    for copy in copies:
        copy.wait()
    slots = v0.shape[1]
    for r in range(2):
        total = (v0[r] + v1[r]) + (w1[r] + w2[r]) + w3[r]
        used = lax.broadcasted_iota(jnp.int32, (slots, 64), 0) < lens[core * 8 + y * 2 + r]
        grad = jnp.where(used, total[:, 64:128], 0.0)
        out[r] = mm3(split(grad), split(total[:, 0:64]), TN)


def factor(lens, pieces):
    shape = pieces[0].shape
    return pl.pallas_call(
        factor_kernel,
        out_shape=jax.ShapeDtypeStruct((2, 64, 64), F32),
        in_specs=[SMEM] + [HBM] * 5,
        out_specs=VMEM,
        scratch_shapes=[pltpu.VMEM(shape, F32)] * 5 + [pltpu.SemaphoreType.DMA((5,))],
        name="factor",
    )(lens, *in_hbm(pieces))


def rowsum(value):
    return jnp.sum(value, axis=1, keepdims=True)


def put(stack, cols, value):
    half = stack.shape[0] // 2
    stack[0:half, cols], stack[half:, cols] = split(value)


def stacked(stack, hi, lo):
    half = stack.shape[0] // 2
    both = mm(stack[...], hi[...], NT)
    return both[0:half] + both[half:] + mm(stack[0:half, :], lo[...], NT)


BLOCKS = [slice(k * BLK, (k + 1) * BLK) for k in range(16)]


def prior_kernel(b0, b1, b2, b3, prior_hbm, start_out, stack_out, pri_hi, pri_lo, out, pieces, prior, start, stack, sems):
    begin = fetch((b0, b1, b2, b3), [pieces.at[i] for i in range(4)], sems)
    rows = [pl.ds(i * SEG, SEG) for i in range(16)]
    parts = fetch([prior_hbm.at[r] for r in rows], [prior.at[r] for r in rows], sems.at[pl.ds(4, 16)])
    _, _, _, y, core = place()
    for d in range(SIDE):
        begin[d].wait()
        at = pl.ds(pl.multiple_of(lax.rem(y + SIDE - d, SIDE) * 8, 8), 8)
        for i in range(16):
            start[at, BLOCKS[i]] = pieces[d, i]
    for cols in BLOCKS:
        put(stack, cols, start[:, cols])
    start_out[...] = start[...]
    stack_out[...] = stack[...]
    t = y * CORES + core
    diag = jnp.zeros((SEG, 128), F32)
    on_diag = lax.broadcasted_iota(jnp.int32, (SEG, 128), 1) == lax.rem(t, 4) * SEG + lax.broadcasted_iota(jnp.int32, (SEG, 128), 0)
    for i in range(16):
        parts[i].wait()
        for cols in BLOCKS:
            pri_hi[rows[i], cols], pri_lo[rows[i], cols] = split(prior[rows[i], cols])
        at = pl.ds(pl.multiple_of(i * BLK + lax.div(t, 4) * 128, 128), 128)
        diag = diag + jnp.where(on_diag, prior[rows[i], at], 0.0)
    out[0:COLS, :] = stacked(stack, pri_hi, pri_lo)
    out[COLS : COLS + 8, :] = jnp.full((8, OWN), jnp.sum(diag), F32)


def prior_image(pieces, prior):
    n = prior.shape[1]
    sds = jax.ShapeDtypeStruct
    return pl.pallas_call(
        prior_kernel,
        out_shape=(
            sds((COLS, n), F32), sds((2 * COLS, n), BF16),
            pltpu.VMEM((OWN, n), BF16), pltpu.VMEM((OWN, n), BF16), sds((COLS + 8, OWN), F32),
        ),
        in_specs=[HBM] * 5,
        out_specs=(VMEM,) * 5,
        scratch_shapes=[
            pltpu.VMEM((4, 16, 8, BLK), F32), pltpu.VMEM((OWN, n), F32),
            pltpu.VMEM((COLS, n), F32), pltpu.VMEM((2 * COLS, n), BF16), pltpu.SemaphoreType.DMA((20,)),
        ],
        compiler_params=params(28),
        cost_estimate=cost(6 * 256 * OWN * n, 8 * OWN * n),
        name="prior_image",
    )(*in_hbm([*pieces, prior]))


def low_rank(stack, f_hi, f_lo, query, low):
    q = stacked(stack, f_hi, f_lo)
    query[...] = q
    parts = split(q * (1.0 / f_hi.shape[0]))
    for cols in BLOCKS:
        low[:, cols] = mm3(parts, (f_hi[:, cols], f_lo[:, cols]), NN)


def factors_kernel(n0, n1, n2, n3, m0, m1, m2, m3, stack, f_hi, f_lo, query, low, square_out, pieces, sems):
    copies = fetch((n0, n1, n2, n3, m0, m1, m2, m3), [pieces.at[i] for i in range(8)], sems)
    square = jnp.zeros((32, BLK), F32)
    for i in range(8):
        copies[i].wait()
        rows = slice(i * 32, (i + 1) * 32)
        for cols in BLOCKS:
            value = pieces[i, :, cols]
            square = square + value * value
            f_hi[rows, cols], f_lo[rows, cols] = split(value)
    square_out[...] = jnp.full(square_out.shape, jnp.sum(square), F32)
    low_rank(stack, f_hi, f_lo, query, low)


def take_factors(pieces, stack):
    n = stack.shape[1]
    sds = jax.ShapeDtypeStruct
    return pl.pallas_call(
        factors_kernel,
        out_shape=(
            pltpu.VMEM((256, n), BF16), pltpu.VMEM((256, n), BF16),
            sds((COLS, 256), F32), sds((COLS, n), F32), sds((8, 128), F32),
        ),
        in_specs=[HBM] * 8 + [VMEM],
        out_specs=(VMEM,) * 5,
        scratch_shapes=[pltpu.VMEM((8, 32, n), F32), pltpu.SemaphoreType.DMA((8,))],
        compiler_params=params(20),
        cost_estimate=cost(12 * 256 * 256 * n, 8 * 256 * n),
        name="take_factors",
    )(*in_hbm(pieces), stack)


def low_rank_step(stack, f_hi, f_lo):
    n = stack.shape[1]
    sds = jax.ShapeDtypeStruct
    return pl.pallas_call(
        low_rank,
        out_shape=(sds((COLS, 256), F32), sds((COLS, n), F32)),
        in_specs=[VMEM] * 3,
        out_specs=(VMEM,) * 2,
        compiler_params=params(16),
        cost_estimate=cost(12 * 256 * 256 * n, 4 * 256 * n),
        name="low_rank",
    )(stack, f_hi, f_lo)


def arrange(pieces, perm, image):
    _, _, _, y, core = place()
    for d, piece in enumerate(pieces):
        chip = lax.rem(y + SIDE - d, SIDE) * CORES
        for side in range(CORES):
            t = chip + (core if side == 0 else 1 - core)
            perm[:, pl.ds(pl.multiple_of(t * OWN, OWN), OWN)] = piece[0:COLS, side * OWN : (side + 1) * OWN]
    lane = lax.broadcasted_iota(jnp.int32, (COLS, 128), 1)
    low64 = lane < 64
    even = lax.rem(lane // SEG, 2) == 0
    for high in range(2):
        for g in range(4):
            x = [perm[:, pl.ds(((4 * high + k) * 4 + g) * 128, 128)] for k in range(4)]
            rolled = [pltpu.roll(v, 64, 1) for v in x]
            a0 = jnp.where(low64, x[0], rolled[2])
            a2 = jnp.where(low64, rolled[0], x[2])
            a1 = jnp.where(low64, x[1], rolled[3])
            a3 = jnp.where(low64, rolled[1], x[3])
            result = (
                jnp.where(even, a0, pltpu.roll(a1, SEG, 1)), jnp.where(even, pltpu.roll(a0, 128 - SEG, 1), a1),
                jnp.where(even, a2, pltpu.roll(a3, SEG, 1)), jnp.where(even, pltpu.roll(a2, 128 - SEG, 1), a3),
            )
            for m in range(4):
                first = (4 * g + m) * BLK + high * 128
                image[:, first : first + 128] = result[m]


def own_part(direc):
    _, _, _, y, core = place()
    t = y * CORES + core
    group = lax.broadcasted_iota(jnp.int32, (COLS, 128), 1) // SEG
    parts = []
    for g in range(4):
        value = jnp.zeros((COLS, 128), F32)
        for m in range(4):
            at = pl.ds(pl.multiple_of((4 * g + m) * BLK + lax.div(t, 4) * 128, 128), 128)
            moved = pltpu.roll(direc[:, at], lax.rem((m + 4 - lax.rem(t, 4)) * SEG, 128), 1)
            value = jnp.where(group == m, moved, value)
        parts.append(value)
    return jnp.concatenate(parts, axis=1)


def step_body(pieces, damping, norm, res_in, direc_in, low, query, pri_hi, pri_lo, res, direc, stack, perm, image):
    arrange(pieces, perm, image)
    curve = jnp.zeros((COLS, 1), F32)
    for cols in BLOCKS:
        old = direc_in[:, cols]
        value = image[:, cols] + low[:, cols] + damping * old
        image[:, cols] = value
        curve = curve + rowsum(old * value)
    if norm is None:
        norm = jnp.zeros((COLS, 1), F32)
        for cols in BLOCKS:
            norm = norm + rowsum(res_in[:, cols] * res_in[:, cols])
    alpha = norm / curve
    fresh = jnp.zeros((COLS, 1), F32)
    for cols in BLOCKS:
        value = res_in[:, cols] - alpha * image[:, cols]
        res[:, cols] = value
        fresh = fresh + rowsum(value * value)
    beta = fresh / norm
    for cols in BLOCKS:
        value = res[:, cols] + beta * direc_in[:, cols]
        direc[:, cols] = value
        put(stack, cols, value)
    return alpha, fresh, stacked(stack, pri_hi, pri_lo)


def first_kernel(
    g0, g1, g2, g3, start, low, query, square, pri_hi, pri_lo,
    res, direc, stack_out, rr, score, damp, out, stack, perm, image,
):
    pieces = (g0, g1, g2, g3)
    trace = square[0:1, 0:1] * (1.0 / query.shape[1])
    for piece in pieces:
        trace = trace + piece[COLS : COLS + 1, 0:1] + piece[COLS : COLS + 1, OWN : OWN + 1]
    damping = 0.1 * trace / start.shape[1]
    damp[...] = jnp.broadcast_to(damping, damp.shape)
    alpha, fresh, out[...] = step_body(
        pieces, damping, None, start, start, low, query, pri_hi, pri_lo, res, direc, stack, perm, image
    )
    stack_out[...] = stack[...]
    rr[...] = jnp.broadcast_to(fresh, rr.shape)
    score[...] = alpha * query[...]


def step_kernel(
    g0, g1, g2, g3, res_in, direc_in, rr_in, score_in, damp, low, query, pri_hi, pri_lo,
    res, direc, stack_out, rr, score, out, stack, perm, image,
):
    alpha, fresh, out[...] = step_body(
        (g0, g1, g2, g3), damp[0:1, 0:1], rr_in[:, 0:1], res_in, direc_in, low, query, pri_hi, pri_lo,
        res, direc, stack, perm, image,
    )
    stack_out[...] = stack[...]
    rr[...] = jnp.broadcast_to(fresh, rr.shape)
    score[...] = score_in[...] + alpha * query[...]


def last_kernel(
    g0, g1, g2, g3, res_in, direc_in, rr_in, score_in, damp, low, query, pri_hi, pri_lo,
    stack_out, rr, score, known, out, res, direc, stack, perm, image,
):
    alpha, fresh, own_image = step_body(
        (g0, g1, g2, g3), damp[0:1, 0:1], rr_in[:, 0:1], res_in, direc_in, low, query, pri_hi, pri_lo,
        res, direc, stack, perm, image,
    )
    out[...] = jnp.broadcast_to(rowsum(own_part(direc) * own_image), out.shape)
    stack_out[...] = stack[...]
    size = jnp.zeros((COLS, 1), F32)
    for cols in BLOCKS:
        size = size + rowsum(direc[:, cols] * direc[:, cols])
    known[...] = jnp.broadcast_to(damp[0:1, 0:1] * size, known.shape)
    rr[...] = jnp.broadcast_to(fresh, rr.shape)
    score[...] = score_in[...] + alpha * query[...]


def cg_call(kernel, operands, outs, extra):
    n = operands[-1].shape[1]
    scratch = [pltpu.VMEM((COLS, n), F32)] * extra + [
        pltpu.VMEM((2 * COLS, n), BF16), pltpu.VMEM((COLS, n), F32), pltpu.VMEM((COLS, n), F32)
    ]
    return pl.pallas_call(
        kernel,
        out_shape=outs,
        in_specs=[VMEM] * len(operands),
        out_specs=(VMEM,) * len(outs),
        scratch_shapes=scratch,
        compiler_params=params(24),
        name=kernel.__name__[:-7],
    )(*operands)


def finish_kernel(sums0, sums1, sums2, sums3, known, rr, score, query, out):
    x, z, _, y, core = place()
    q = query[...]
    rollouts = q.shape[1]
    curve = (sums0[:, 0:1] + sums1[:, 0:1]) + (sums2[:, 0:1] + sums3[:, 0:1])
    curve = curve + known[:, 0:1] + rowsum(q * q) * (1.0 / rollouts)
    total = score[...] + (rr[:, 0:1] / curve) * q
    iota = lambda shape, axis: lax.broadcasted_iota(jnp.int32, shape, axis)
    dot = functools.partial(lax.dot_general, precision=HIGHEST, preferred_element_type=F32)
    pick = (iota((8, COLS), 1) == iota((8, COLS), 0) + 4 * (y * CORES + core)).astype(F32)
    mine = dot(pick, total, NN)
    row = iota((rollouts, rollouts), 0)
    side = lax.rem(core + row // 128, CORES)
    second, first, back, last = row // 32 % 4, row // 8 % 4, row // 2 % 4, row % 2
    dx = side * first + (1 - side) * second
    dz = first + second - dx
    home = lax.rem(x + SIDE - dx, SIDE) * SIDE + lax.rem(z + SIDE - dz, SIDE)
    rank = home * 16 + side * 8 + lax.rem(y + SIDE - back, SIDE) * 2 + last
    ordered = dot(mine, (rank == iota((rollouts, rollouts), 1)).astype(F32), NN)
    for i in range(16):
        part = ordered[:, i // 8 * 128 : (i // 8 + 1) * 128]
        shift = (128 - i % 8 * 16) % 128
        out[i] = pltpu.roll(part, shift, 1) if shift else part


def finish(sums, known, rr, score, query):
    return pl.pallas_call(
        finish_kernel,
        out_shape=jax.ShapeDtypeStruct((16, 8, 128), F32),
        in_specs=[VMEM] * 8,
        out_specs=VMEM,
        name="finish",
    )(*sums, known, rr, score, query)


def place_kernel(parts, out, rows):
    for i in range(16):
        rows[4 * i : 4 * i + 4, :] = parts[i, 0:4, :]
    pick = lax.broadcasted_iota(jnp.int32, (16, 128), 0) == lax.broadcasted_iota(jnp.int32, (16, 128), 1)
    out[...] = lax.dot_general(pick.astype(F32), rows[...], NT, precision=HIGHEST, preferred_element_type=F32)


def place_scores(parts):
    return pl.pallas_call(
        place_kernel,
        out_shape=jax.ShapeDtypeStruct((16, 64), F32),
        in_specs=[VMEM],
        out_specs=VMEM,
        scratch_shapes=[pltpu.VMEM((64, 128), F32)],
        name="place_scores",
    )(parts)


BOTH = ("dp", "tensor")


def second_stage(line):
    return [line] + [lax.ppermute(line, BOTH, crossed(d, 1)) for d in (1, 2, 3)]


def to_other_core(value):
    return lax.ppermute(value, "tensor", other_core())


def over_y(value):
    return [value] + [lax.ppermute(value, "tensor", along_y(d)) for d in (1, 2, 3)]


def gather_image(part):
    return over_y(jnp.concatenate([part, to_other_core(part)], axis=1))


def per_device(
    activations, out_grads, lengths, bank_in, index_in, bank_out, index_out, prior_cov, val_grads
):
    _, _, _, y, core = place()
    slot = jnp.arange(8, dtype=jnp.int32)
    line = lax.rem(y + slot // 2, SIDE) * 2 + slot % 2

    slab = lax.dynamic_slice_in_dim(prior_cov, (y * CORES + core) * SEG, SEG, 0)
    prior = lax.all_gather(slab, "dp", axis=0, tiled=True)

    banks = (bank_in.transpose(0, 2, 1), bank_out.transpose(0, 2, 1))
    theirs = project((1 - core) * 8 + line, index_in, index_out, activations, out_grads, *banks)
    from_core = to_other_core(theirs)
    mine = project(core * 8 + line, index_in, index_out, activations, out_grads, *banks)
    to_y = [mine[2 * d : 2 * d + 2] + from_core[2 * d : 2 * d + 2] for d in (1, 2, 3)]
    to_y, start_here = lax.optimization_barrier((to_y, val_grads.T.reshape(16, 4, BLK)))
    from_y = [lax.ppermute(v, "tensor", along_y(d)) for d, v in zip((1, 2, 3), to_y)]
    start_here = lax.all_to_all(start_here, "dp", 0, 0, tiled=True)
    lengths, start_here = lax.optimization_barrier((lengths, start_here))

    own = factor(lengths, [mine[0:2], from_core[0:2], *from_y]).reshape(2, 4096)
    part = jnp.concatenate(over_y(own), axis=0)
    start_there = to_other_core(start_here)
    start_pair = jnp.where(
        core == 0,
        jnp.concatenate([start_here, start_there], axis=1),
        jnp.concatenate([start_there, start_here], axis=1),
    )
    start_pieces = over_y(start_pair)
    moved = [lax.ppermute(part, BOTH, crossed(d, 0)) for d in (1, 2, 3)]
    near = second_stage(jnp.concatenate([part] + moved, axis=0))
    far = [to_other_core(piece) for piece in near]

    start, stack, pri_hi, pri_lo, out = prior_image(start_pieces, prior)
    f_hi, f_lo, query, low, square = take_factors(near + far, stack)
    sds = jax.ShapeDtypeStruct
    n = start.shape[1]
    vector, flat = sds((COLS, n), F32), sds((COLS, 128), F32)
    scores_shape, part_shape = sds((COLS, 256), F32), sds((COLS, OWN), F32)
    state_shapes = (vector, vector, sds((2 * COLS, n), BF16), flat, scores_shape)
    res, direc, stack, rr, score, damp, out = cg_call(
        first_kernel,
        (*gather_image(out), start, low, query, square, pri_hi, pri_lo),
        (*state_shapes, sds((8, 128), F32), part_shape), 0,
    )
    for iteration in range(1, ITERS - 1):
        pieces = gather_image(out)
        query, low = low_rank_step(stack, f_hi, f_lo)
        operands = (*pieces, res, direc, rr, score, damp, low, query, pri_hi, pri_lo)
        if iteration + 2 < ITERS:
            res, direc, stack, rr, score, out = cg_call(step_kernel, operands, (*state_shapes, part_shape), 0)
        else:
            stack, rr, score, known, out = cg_call(
                last_kernel, operands, (state_shapes[2], flat, scores_shape, flat, flat), 2
            )
    sums = over_y(out + to_other_core(out))
    query, _ = low_rank_step(stack, f_hi, f_lo)
    return place_scores(lax.all_to_all(finish(sums, known, rr, score, query), "dp", 0, 0, tiled=True))


def solution(mesh):
    return jax.shard_map(
        per_device,
        mesh=mesh,
        in_specs=(
            P("dp", None, "tensor"),
            P("dp", None, "tensor"),
            P("dp"),
            P(),
            P("tensor"),
            P(),
            P("tensor"),
            P("dp", None),
            P("dp", "tensor"),
        ),
        out_specs=P("dp", "tensor"),
        check_vma=False,
    )
```

```python
import functools

import jax
import jax.numpy as jnp
from jax import lax
from jax.experimental import pallas as pl
from jax.experimental.pallas import tpu as pltpu
from jax.sharding import PartitionSpec as P

ITERS = 6
F32 = jnp.float32
BF16 = jnp.bfloat16
HIGHEST = lax.Precision.HIGHEST

NT = (((1,), (1,)), ((), ()))
NN = (((1,), (0,)), ((), ()))
TN = (((0,), (0,)), ((), ()))

SIDE = 4
CORES = 2
BLK = 256
SEG = 32
OWN = 512
COLS = 32
VMEM = pl.BlockSpec(memory_space=pltpu.VMEM)
SMEM = pl.BlockSpec(memory_space=pltpu.SMEM)
HBM = pl.BlockSpec(memory_space=pltpu.HBM)


def params(mib):
    return pltpu.CompilerParams(vmem_limit_bytes=mib << 20)


def in_hbm(values):
    return [pltpu.with_memory_space_constraint(v, pltpu.HBM) for v in values]


def place():
    dp = lax.axis_index("dp").astype(jnp.int32)
    tensor = lax.axis_index("tensor").astype(jnp.int32)
    return lax.div(dp, SIDE), lax.rem(dp, SIDE), dp, lax.div(tensor, CORES), lax.rem(tensor, CORES)


def fetch(sources, targets, sems):
    copies = [pltpu.make_async_copy(a, b, sems.at[i]) for i, (a, b) in enumerate(zip(sources, targets))]
    for copy in copies:
        copy.start()
    return copies


def cost(flops, nbytes):
    return pl.CostEstimate(flops=flops, bytes_accessed=nbytes, transcendentals=0)


def split(value):
    high = value.astype(BF16)
    return high, (value - high.astype(F32)).astype(BF16)


def mm(a, b, dims):
    return lax.dot_general(a, b, dims, preferred_element_type=F32)


def mm3(a, b, dims):
    return mm(a[0], b[0], dims) + mm(a[1], b[0], dims) + mm(a[0], b[1], dims)


def along_z(step):
    return [(i, (i // SIDE) * SIDE + (i + step) % SIDE) for i in range(16)]


def along_x(step):
    return [(i, (i + step * SIDE) % 16) for i in range(16)]


def along_y(step):
    return [(i, (i + step * CORES) % 8) for i in range(8)]


def other_core():
    return [(i, i ^ 1) for i in range(8)]


def crossed(step, flip):
    pairs = []
    for dp in range(16):
        for tensor in range(8):
            table = along_x(step) if (tensor % CORES) ^ flip else along_z(step)
            pairs.append((dp * 8 + tensor, table[dp][1] * 8 + tensor))
    return pairs


def project_kernel(
    idx_in, idx_out, act, grad, bank_in, bank_out, out, acts, grads, proj_in, proj_out, sems, *, flip
):
    _, _, _, y, core = place()
    side = 1 - core if flip else core
    copies = []
    for i, (index, bank, proj) in enumerate(((idx_in, bank_in, proj_in), (idx_out, bank_out, proj_out))):
        blocks = proj.shape[1] // 128
        copies.append(
            fetch(
                [bank.at[index[b]] for b in range(blocks)],
                [proj.at[:, pl.ds(b * 128, 128)] for b in range(blocks)],
                sems.at[pl.ds(16 + 14 * i, blocks)],
            )
        )
    rolls = [side * 8 + lax.rem(y + j // 2, SIDE) * 2 + j % 2 for j in range(8)]
    blocks = []
    for j in range(8):
        blocks.append(fetch((act.at[rolls[j]], grad.at[rolls[j]]), (acts.at[j], grads.at[j]), sems.at[pl.ds(2 * j, 2)]))
    for group in copies:
        for copy in group:
            copy.wait()
    for j in range(8):
        for copy in blocks[j]:
            copy.wait()
        out[j, :, 0:64] = mm(acts[j], proj_in[...], NT)
        out[j, :, 64:128] = mm(grads[j], proj_out[...], NT)


def project(idx_in, idx_out, act, grad, bank_in_t, bank_out_t, flip):
    slots, width, model = act.shape[1], act.shape[2], grad.shape[2]
    return pl.pallas_call(
        functools.partial(project_kernel, flip=flip),
        out_shape=jax.ShapeDtypeStruct((8, slots, 128), F32),
        in_specs=[SMEM] * 2 + [HBM] * 4,
        out_specs=VMEM,
        scratch_shapes=[
            pltpu.VMEM((8, slots, width), BF16), pltpu.VMEM((8, slots, model), BF16),
            pltpu.VMEM((64, width), BF16), pltpu.VMEM((64, model), BF16),
            pltpu.SemaphoreType.DMA((34,)),
        ],
        compiler_params=params(20),
        cost_estimate=cost(16 * slots * (width + model) * 256, 16 * slots * (width + model)),
        name="project",
    )(idx_in, idx_out, *in_hbm([act, grad, bank_in_t, bank_out_t]))


def slab_kernel(prior, out, sem):
    _, _, _, y, core = place()
    rows = pl.ds(pl.multiple_of((y * CORES + core) * SEG, SEG), SEG)
    copy = pltpu.make_async_copy(prior.at[rows], out, sem)
    copy.start()
    copy.wait()


def own_slab(prior):
    return pl.pallas_call(
        slab_kernel,
        out_shape=pltpu.HBM((SEG, prior.shape[1]), F32),
        in_specs=[HBM],
        out_specs=HBM,
        scratch_shapes=[pltpu.SemaphoreType.DMA],
        name="own_slab",
    )(*in_hbm([prior]))


def factor_kernel(lens, a0, a1, b1, b2, b3, out, v0, v1, w1, w2, w3, sems):
    copies = fetch((a0, a1, b1, b2, b3), (v0, v1, w1, w2, w3), sems)
    _, _, _, y, core = place()
    for copy in copies:
        copy.wait()
    slots = v0.shape[1]
    for r in range(2):
        total = (v0[r] + v1[r]) + (w1[r] + w2[r]) + w3[r]
        used = lax.broadcasted_iota(jnp.int32, (slots, 64), 0) < lens[core * 8 + y * 2 + r]
        grad = jnp.where(used, total[:, 64:128], 0.0)
        out[r] = mm3(split(grad), split(total[:, 0:64]), TN)


def factor(lens, pieces):
    shape = pieces[0].shape
    return pl.pallas_call(
        factor_kernel,
        out_shape=jax.ShapeDtypeStruct((2, 64, 64), F32),
        in_specs=[SMEM] + [HBM] * 5,
        out_specs=VMEM,
        scratch_shapes=[pltpu.VMEM(shape, F32)] * 5 + [pltpu.SemaphoreType.DMA((5,))],
        name="factor",
    )(lens, *in_hbm(pieces))


def rowsum(value):
    return jnp.sum(value, axis=1, keepdims=True)


def put(stack, cols, value):
    half = stack.shape[0] // 2
    stack[0:half, cols], stack[half:, cols] = split(value)


def stacked(stack, hi, lo):
    half = stack.shape[0] // 2
    both = mm(stack[...], hi[...], NT)
    return both[0:half] + both[half:] + mm(stack[0:half, :], lo[...], NT)


BLOCKS = [slice(k * BLK, (k + 1) * BLK) for k in range(16)]


def start_kernel(b0, b1, b2, b3, start, stack, pieces, sems):
    begin = fetch((b0, b1, b2, b3), [pieces.at[i] for i in range(4)], sems)
    _, _, _, y, _ = place()
    for d in range(SIDE):
        begin[d].wait()
        at = pl.ds(pl.multiple_of(lax.rem(y + SIDE - d, SIDE) * 8, 8), 8)
        for i in range(16):
            start[at, BLOCKS[i]] = pieces[d, i]
    for cols in BLOCKS:
        put(stack, cols, start[:, cols])


def assemble_start(pieces, n):
    sds = jax.ShapeDtypeStruct
    return pl.pallas_call(
        start_kernel,
        out_shape=(sds((COLS, n), F32), sds((2 * COLS, n), BF16)),
        in_specs=[HBM] * 4,
        out_specs=(VMEM, VMEM),
        scratch_shapes=[pltpu.VMEM((4, 16, 8, BLK), F32), pltpu.SemaphoreType.DMA((4,))],
        compiler_params=params(12),
        name="assemble_start",
    )(*in_hbm(pieces))


def prior_kernel(stack, prior_hbm, pri_hi, pri_lo, out, prior, sems):
    rows = [slice(i * SEG, (i + 1) * SEG) for i in range(16)]
    parts = fetch([prior_hbm.at[pl.ds(i * SEG, SEG)] for i in range(16)], [prior.at[pl.ds(i * SEG, SEG)] for i in range(16)], sems)
    _, _, _, y, core = place()
    t = y * CORES + core
    diag = jnp.zeros((SEG, 128), F32)
    on_diag = lax.broadcasted_iota(jnp.int32, (SEG, 128), 1) == lax.rem(t, 4) * SEG + lax.broadcasted_iota(jnp.int32, (SEG, 128), 0)
    half = stack.shape[0] // 2
    for g in range(4):
        for i in range(4 * g, 4 * g + 4):
            parts[i].wait()
            for cols in BLOCKS:
                pri_hi[rows[i], cols], pri_lo[rows[i], cols] = split(prior[rows[i], cols])
            at = pl.ds(pl.multiple_of(i * BLK + lax.div(t, 4) * 128, 128), 128)
            diag = diag + jnp.where(on_diag, prior[rows[i], at], 0.0)
        group = slice(g * 128, (g + 1) * 128)
        both = mm(stack[...], pri_hi[group, :], NT)
        out[0:COLS, group] = both[0:half] + both[half:] + mm(stack[0:half, :], pri_lo[group, :], NT)
    out[COLS : COLS + 8, :] = jnp.full((8, OWN), jnp.sum(diag), F32)


def prior_image(stack, prior):
    n = prior.shape[1]
    return pl.pallas_call(
        prior_kernel,
        out_shape=(
            pltpu.VMEM((OWN, n), BF16), pltpu.VMEM((OWN, n), BF16), jax.ShapeDtypeStruct((COLS + 8, OWN), F32),
        ),
        in_specs=[VMEM, HBM],
        out_specs=(VMEM,) * 3,
        scratch_shapes=[pltpu.VMEM((OWN, n), F32), pltpu.SemaphoreType.DMA((16,))],
        compiler_params=params(28),
        cost_estimate=cost(6 * 256 * OWN * n, 8 * OWN * n),
        name="prior_image",
    )(stack, *in_hbm([prior]))


def low_rank(stack, f_hi, f_lo, query, low):
    q = stacked(stack, f_hi, f_lo)
    query[...] = q
    parts = split(q * (1.0 / f_hi.shape[0]))
    for cols in BLOCKS:
        low[:, cols] = mm3(parts, (f_hi[:, cols], f_lo[:, cols]), NN)


def factors_kernel(n0, n1, n2, n3, m0, m1, m2, m3, stack, f_hi, f_lo, query, low, square_out, pieces, sems):
    copies = fetch((n0, n1, n2, n3, m0, m1, m2, m3), [pieces.at[i] for i in range(8)], sems)
    square = jnp.zeros((32, BLK), F32)
    for i in range(8):
        copies[i].wait()
        rows = slice(i * 32, (i + 1) * 32)
        for cols in BLOCKS:
            value = pieces[i, :, cols]
            square = square + value * value
            f_hi[rows, cols], f_lo[rows, cols] = split(value)
    square_out[...] = jnp.full(square_out.shape, jnp.sum(square), F32)
    low_rank(stack, f_hi, f_lo, query, low)


def take_factors(pieces, stack):
    n = stack.shape[1]
    sds = jax.ShapeDtypeStruct
    return pl.pallas_call(
        factors_kernel,
        out_shape=(
            pltpu.VMEM((256, n), BF16), pltpu.VMEM((256, n), BF16),
            sds((COLS, 256), F32), sds((COLS, n), F32), sds((8, 128), F32),
        ),
        in_specs=[HBM] * 8 + [VMEM],
        out_specs=(VMEM,) * 5,
        scratch_shapes=[pltpu.VMEM((8, 32, n), F32), pltpu.SemaphoreType.DMA((8,))],
        compiler_params=params(20),
        cost_estimate=cost(12 * 256 * 256 * n, 8 * 256 * n),
        name="take_factors",
    )(*in_hbm(pieces), stack)


def low_rank_step(stack, f_hi, f_lo):
    n = stack.shape[1]
    sds = jax.ShapeDtypeStruct
    return pl.pallas_call(
        low_rank,
        out_shape=(sds((COLS, 256), F32), sds((COLS, n), F32)),
        in_specs=[VMEM] * 3,
        out_specs=(VMEM,) * 2,
        compiler_params=params(16),
        cost_estimate=cost(12 * 256 * 256 * n, 4 * 256 * n),
        name="low_rank",
    )(stack, f_hi, f_lo)


def arrange(mine, theirs, perm, image):
    _, _, _, y, core = place()
    for d in range(SIDE):
        chip = lax.rem(y + SIDE - d, SIDE) * CORES
        for side, line in ((core, mine), (1 - core, theirs)):
            at = pl.ds(pl.multiple_of((chip + side) * OWN, OWN), OWN)
            perm[:, at] = line[0:COLS, d * OWN : (d + 1) * OWN]
    lane = lax.broadcasted_iota(jnp.int32, (COLS, 128), 1)
    low64 = lane < 64
    even = lax.rem(lane // SEG, 2) == 0
    for high in range(2):
        for g in range(4):
            x = [perm[:, pl.ds(((4 * high + k) * 4 + g) * 128, 128)] for k in range(4)]
            rolled = [pltpu.roll(v, 64, 1) for v in x]
            a0 = jnp.where(low64, x[0], rolled[2])
            a2 = jnp.where(low64, rolled[0], x[2])
            a1 = jnp.where(low64, x[1], rolled[3])
            a3 = jnp.where(low64, rolled[1], x[3])
            result = (
                jnp.where(even, a0, pltpu.roll(a1, SEG, 1)), jnp.where(even, pltpu.roll(a0, 128 - SEG, 1), a1),
                jnp.where(even, a2, pltpu.roll(a3, SEG, 1)), jnp.where(even, pltpu.roll(a2, 128 - SEG, 1), a3),
            )
            for m in range(4):
                first = (4 * g + m) * BLK + high * 128
                image[:, first : first + 128] = result[m]


def own_part(direc):
    _, _, _, y, core = place()
    t = y * CORES + core
    group = lax.broadcasted_iota(jnp.int32, (COLS, 128), 1) // SEG
    parts = []
    for g in range(4):
        value = jnp.zeros((COLS, 128), F32)
        for m in range(4):
            at = pl.ds(pl.multiple_of((4 * g + m) * BLK + lax.div(t, 4) * 128, 128), 128)
            moved = pltpu.roll(direc[:, at], lax.rem((m + 4 - lax.rem(t, 4)) * SEG, 128), 1)
            value = jnp.where(group == m, moved, value)
        parts.append(value)
    return jnp.concatenate(parts, axis=1)


def step_body(pieces, damping, norm, res_in, direc_in, low, query, pri_hi, pri_lo, res, direc, stack, perm, image):
    arrange(*pieces, perm, image)
    curve = jnp.zeros((COLS, 1), F32)
    for cols in BLOCKS:
        old = direc_in[:, cols]
        value = image[:, cols] + low[:, cols] + damping * old
        image[:, cols] = value
        curve = curve + rowsum(old * value)
    if norm is None:
        norm = jnp.zeros((COLS, 1), F32)
        for cols in BLOCKS:
            norm = norm + rowsum(res_in[:, cols] * res_in[:, cols])
    alpha = norm / curve
    fresh = jnp.zeros((COLS, 1), F32)
    for cols in BLOCKS:
        value = res_in[:, cols] - alpha * image[:, cols]
        res[:, cols] = value
        fresh = fresh + rowsum(value * value)
    beta = fresh / norm
    for cols in BLOCKS:
        value = res[:, cols] + beta * direc_in[:, cols]
        direc[:, cols] = value
        put(stack, cols, value)
    return alpha, fresh, stacked(stack, pri_hi, pri_lo)


def first_kernel(
    mine, theirs, start, low, query, square, pri_hi, pri_lo,
    res, direc, stack_out, rr, score, damp, out, stack, perm, image,
):
    pieces = (mine, theirs)
    trace = square[0:1, 0:1] * (1.0 / query.shape[1])
    for piece in pieces:
        for d in range(SIDE):
            trace = trace + piece[COLS : COLS + 1, d * OWN : d * OWN + 1]
    damping = 0.1 * trace / start.shape[1]
    damp[...] = jnp.broadcast_to(damping, damp.shape)
    alpha, fresh, out[...] = step_body(
        pieces, damping, None, start, start, low, query, pri_hi, pri_lo, res, direc, stack, perm, image
    )
    stack_out[...] = stack[...]
    rr[...] = jnp.broadcast_to(fresh, rr.shape)
    score[...] = alpha * query[...]


def step_kernel(
    mine, theirs, res_in, direc_in, rr_in, score_in, damp, low, query, pri_hi, pri_lo,
    res, direc, stack_out, rr, score, out, stack, perm, image,
):
    alpha, fresh, out[...] = step_body(
        (mine, theirs), damp[0:1, 0:1], rr_in[:, 0:1], res_in, direc_in, low, query, pri_hi, pri_lo,
        res, direc, stack, perm, image,
    )
    stack_out[...] = stack[...]
    rr[...] = jnp.broadcast_to(fresh, rr.shape)
    score[...] = score_in[...] + alpha * query[...]


def last_kernel(
    mine, theirs, res_in, direc_in, rr_in, score_in, damp, low, query, pri_hi, pri_lo,
    stack_out, rr, score, known, out, res, direc, stack, perm, image,
):
    alpha, fresh, own_image = step_body(
        (mine, theirs), damp[0:1, 0:1], rr_in[:, 0:1], res_in, direc_in, low, query, pri_hi, pri_lo,
        res, direc, stack, perm, image,
    )
    out[...] = jnp.broadcast_to(rowsum(own_part(direc) * own_image), out.shape)
    stack_out[...] = stack[...]
    size = jnp.zeros((COLS, 1), F32)
    for cols in BLOCKS:
        size = size + rowsum(direc[:, cols] * direc[:, cols])
    known[...] = jnp.broadcast_to(damp[0:1, 0:1] * size, known.shape)
    rr[...] = jnp.broadcast_to(fresh, rr.shape)
    score[...] = score_in[...] + alpha * query[...]


def cg_call(kernel, operands, outs, extra):
    n = operands[-1].shape[1]
    scratch = [pltpu.VMEM((COLS, n), F32)] * extra + [
        pltpu.VMEM((2 * COLS, n), BF16), pltpu.VMEM((COLS, n), F32), pltpu.VMEM((COLS, n), F32)
    ]
    return pl.pallas_call(
        kernel,
        out_shape=outs,
        in_specs=[VMEM] * len(operands),
        out_specs=(VMEM,) * len(outs),
        scratch_shapes=scratch,
        compiler_params=params(24),
        name=kernel.__name__[:-7],
    )(*operands)


def iota(shape, axis):
    return lax.broadcasted_iota(jnp.int32, shape, axis)


exact = functools.partial(lax.dot_general, precision=HIGHEST, preferred_element_type=F32)


def own_columns(y, core):
    return (iota((8, COLS), 1) == iota((8, COLS), 0) + 4 * (y * CORES + core)).astype(F32)


def query_kernel(stack, f_hi, f_lo, score, size, own):
    x, z, _, y, core = place()
    q = stacked(stack, f_hi, f_lo)
    rollouts = q.shape[1]
    size[...] = jnp.broadcast_to(rowsum(q * q) * (1.0 / rollouts), size.shape)
    pick = own_columns(y, core)
    both = jnp.concatenate([exact(pick, q, NN), exact(pick, score[...], NN)], axis=0)
    row = iota((rollouts, rollouts), 0)
    side = lax.rem(core + row // 128, CORES)
    second, first, back, last = row // 32 % 4, row // 8 % 4, row // 2 % 4, row % 2
    dx = side * first + (1 - side) * second
    dz = first + second - dx
    home = lax.rem(x + SIDE - dx, SIDE) * SIDE + lax.rem(z + SIDE - dz, SIDE)
    rank = home * 16 + side * 8 + lax.rem(y + SIDE - back, SIDE) * 2 + last
    own[...] = exact(both, (rank == iota((rollouts, rollouts), 1)).astype(F32), NN)


def last_query(stack, f_hi, f_lo, score):
    sds = jax.ShapeDtypeStruct
    return pl.pallas_call(
        query_kernel,
        out_shape=(sds((COLS, 128), F32), sds((16, 256), F32)),
        in_specs=[VMEM] * 4,
        out_specs=(VMEM,) * 2,
        compiler_params=params(16),
        cost_estimate=cost(6 * 256 * 256 * f_hi.shape[1], 4 * 256 * f_hi.shape[1]),
        name="last_query",
    )(stack, f_hi, f_lo, score)


def finish_kernel(sums0, sums1, sums2, sums3, known, size, rr, own, out):
    _, _, _, y, core = place()
    curve = (sums0[...] + sums1[...]) + (sums2[...] + sums3[...]) + known[...] + size[...]
    alpha = exact(own_columns(y, core), rr[...] / curve, NN)[:, 0:1]
    ordered = own[8:16, :] + alpha * own[0:8, :]
    for i in range(16):
        part = ordered[:, i // 8 * 128 : (i // 8 + 1) * 128]
        shift = (128 - i % 8 * 16) % 128
        out[i] = pltpu.roll(part, shift, 1) if shift else part


def finish(sums, known, size, rr, own):
    return pl.pallas_call(
        finish_kernel,
        out_shape=jax.ShapeDtypeStruct((16, 8, 128), F32),
        in_specs=[VMEM] * 8,
        out_specs=VMEM,
        name="finish",
    )(*sums, known, size, rr, own)


def place_kernel(parts, out, rows):
    for i in range(16):
        rows[4 * i : 4 * i + 4, :] = parts[i, 0:4, :]
    pick = lax.broadcasted_iota(jnp.int32, (16, 128), 0) == lax.broadcasted_iota(jnp.int32, (16, 128), 1)
    out[...] = lax.dot_general(pick.astype(F32), rows[...], NT, precision=HIGHEST, preferred_element_type=F32)


def place_scores(parts):
    return pl.pallas_call(
        place_kernel,
        out_shape=jax.ShapeDtypeStruct((16, 64), F32),
        in_specs=[VMEM],
        out_specs=VMEM,
        scratch_shapes=[pltpu.VMEM((64, 128), F32)],
        name="place_scores",
    )(parts)


BOTH = ("dp", "tensor")


def second_stage(line):
    return [line] + [lax.ppermute(line, BOTH, crossed(d, 1)) for d in (1, 2, 3)]


def to_other_core(value):
    return lax.ppermute(value, "tensor", other_core())


def over_y(value):
    return [value] + [lax.ppermute(value, "tensor", along_y(d)) for d in (1, 2, 3)]


def join_image(pieces):
    line = jnp.concatenate(pieces, axis=1)
    return line, to_other_core(line)


def per_device(
    activations, out_grads, lengths, bank_in, index_in, bank_out, index_out, prior_cov, val_grads
):
    _, _, _, _, core = place()
    prior = lax.all_gather(own_slab(prior_cov), "dp", axis=0, tiled=True)

    tokens = (index_in, index_out, activations, out_grads, bank_in.transpose(0, 2, 1), bank_out.transpose(0, 2, 1))
    theirs = project(*tokens, True)
    from_core = to_other_core(theirs)
    mine = project(*tokens, False)
    to_y = [mine[2 * d : 2 * d + 2] + from_core[2 * d : 2 * d + 2] for d in (1, 2, 3)]
    to_y, start_here = lax.optimization_barrier((to_y, val_grads.T.reshape(16, 4, BLK)))
    from_y = [lax.ppermute(v, "tensor", along_y(d)) for d, v in zip((1, 2, 3), to_y)]
    start_here = lax.all_to_all(start_here, "dp", 0, 0, tiled=True)
    lengths, start_here = lax.optimization_barrier((lengths, start_here))

    own = factor(lengths, [mine[0:2], from_core[0:2], *from_y]).reshape(2, 4096)
    part = jnp.concatenate(over_y(own), axis=0)
    start_there = to_other_core(start_here)
    start_pair = jnp.where(
        core == 0,
        jnp.concatenate([start_here, start_there], axis=1),
        jnp.concatenate([start_there, start_here], axis=1),
    )
    part, start_pair = lax.optimization_barrier((part, start_pair))
    start_pieces = over_y(start_pair)
    moved = [lax.ppermute(part, BOTH, crossed(d, 0)) for d in (1, 2, 3)]
    moved, start_pieces = lax.optimization_barrier((moved, start_pieces))
    near = second_stage(jnp.concatenate([part] + moved, axis=0))
    far = [to_other_core(piece) for piece in near]

    start, stack = assemble_start(start_pieces, prior_cov.shape[1])
    far, prior = lax.optimization_barrier((far, prior))
    pri_hi, pri_lo, out = prior_image(stack, prior)
    pieces = over_y(out)
    f_hi, f_lo, query, low, square = take_factors(near + far, stack)
    pieces, square = lax.optimization_barrier((pieces, square))
    sds = jax.ShapeDtypeStruct
    n = start.shape[1]
    vector, flat = sds((COLS, n), F32), sds((COLS, 128), F32)
    scores_shape, part_shape = sds((COLS, 256), F32), sds((COLS, OWN), F32)
    state_shapes = (vector, vector, sds((2 * COLS, n), BF16), flat, scores_shape)
    res, direc, stack, rr, score, damp, out = cg_call(
        first_kernel,
        (*join_image(pieces), start, low, query, square, pri_hi, pri_lo),
        (*state_shapes, sds((8, 128), F32), part_shape), 0,
    )
    for iteration in range(1, ITERS - 1):
        pieces = over_y(out)
        query, low = low_rank_step(stack, f_hi, f_lo)
        pieces, query, low = lax.optimization_barrier((pieces, query, low))
        operands = (*join_image(pieces), res, direc, rr, score, damp, low, query, pri_hi, pri_lo)
        if iteration + 2 < ITERS:
            res, direc, stack, rr, score, out = cg_call(step_kernel, operands, (*state_shapes, part_shape), 0)
        else:
            stack, rr, score, known, out = cg_call(
                last_kernel, operands, (state_shapes[2], flat, scores_shape, flat, flat), 2
            )
    sums = over_y(out + to_other_core(out))
    size, own = last_query(stack, f_hi, f_lo, score)
    return place_scores(lax.all_to_all(finish(sums, known, size, rr, own), "dp", 0, 0, tiled=True))


def solution(mesh):
    return jax.shard_map(
        per_device,
        mesh=mesh,
        in_specs=(
            P("dp", None, "tensor"),
            P("dp", None, "tensor"),
            P("dp"),
            P(),
            P("tensor"),
            P(),
            P("tensor"),
            P("dp", None),
            P("dp", "tensor"),
        ),
        out_specs=P("dp", "tensor"),
        check_vma=False,
    )
```

```python
import functools

import jax
import jax.numpy as jnp
from jax import lax
from jax.experimental import pallas as pl
from jax.experimental.pallas import tpu as pltpu
from jax.sharding import PartitionSpec as P

ITERS = 6
F32 = jnp.float32
BF16 = jnp.bfloat16
HIGHEST = lax.Precision.HIGHEST

NT = (((1,), (1,)), ((), ()))
NN = (((1,), (0,)), ((), ()))
TN = (((0,), (0,)), ((), ()))

SIDE = 4
CORES = 2
BLK = 256
SEG = 32
OWN = 512
COLS = 32
VMEM = pl.BlockSpec(memory_space=pltpu.VMEM)
SMEM = pl.BlockSpec(memory_space=pltpu.SMEM)
HBM = pl.BlockSpec(memory_space=pltpu.HBM)


def params(mib):
    return pltpu.CompilerParams(vmem_limit_bytes=mib << 20)


def in_vmem(values):
    return [pltpu.with_memory_space_constraint(v, pltpu.VMEM) for v in values]


def in_hbm(values):
    return [pltpu.with_memory_space_constraint(v, pltpu.HBM) for v in values]


def place():
    dp = lax.axis_index("dp").astype(jnp.int32)
    tensor = lax.axis_index("tensor").astype(jnp.int32)
    return lax.div(dp, SIDE), lax.rem(dp, SIDE), dp, lax.div(tensor, CORES), lax.rem(tensor, CORES)


def fetch(sources, targets, sems):
    copies = [pltpu.make_async_copy(a, b, sems.at[i]) for i, (a, b) in enumerate(zip(sources, targets))]
    for copy in copies:
        copy.start()
    return copies


def cost(flops, nbytes):
    return pl.CostEstimate(flops=flops, bytes_accessed=nbytes, transcendentals=0)


def split(value):
    high = value.astype(BF16)
    return high, (value - high.astype(F32)).astype(BF16)


def mm(a, b, dims):
    return lax.dot_general(a, b, dims, preferred_element_type=F32)


def mm3(a, b, dims):
    return mm(a[0], b[0], dims) + mm(a[1], b[0], dims) + mm(a[0], b[1], dims)


def along_z(step):
    return [(i, (i // SIDE) * SIDE + (i + step) % SIDE) for i in range(16)]


def along_x(step):
    return [(i, (i + step * SIDE) % 16) for i in range(16)]


def along_y(step):
    return [(i, (i + step * CORES) % 8) for i in range(8)]


def other_core():
    return [(i, i ^ 1) for i in range(8)]


ORDER = ("zxy", "yzx")


def shifted(step, stage):
    pairs = []
    for dp in range(16):
        for tensor in range(8):
            axis = ORDER[tensor % CORES][stage]
            to_dp = {"x": along_x, "z": along_z}[axis](step)[dp][1] if axis != "y" else dp
            to_tensor = along_y(step)[tensor][1] if axis == "y" else tensor
            pairs.append((dp * 8 + tensor, to_dp * 8 + to_tensor))
    return pairs


def project_kernel(
    idx_in, idx_out, act, grad, bank_in, bank_out, out, acts, grads, proj_in, proj_out, sems, *, flip
):
    _, _, _, y, core = place()
    side = 1 - core if flip else core
    copies = []
    for i, (index, bank, proj) in enumerate(((idx_in, bank_in, proj_in), (idx_out, bank_out, proj_out))):
        blocks = proj.shape[1] // 128
        copies.append(
            fetch(
                [bank.at[index[b]] for b in range(blocks)],
                [proj.at[:, pl.ds(b * 128, 128)] for b in range(blocks)],
                sems.at[pl.ds(16 + 14 * i, blocks)],
            )
        )
    rolls = [side * 8 + lax.rem(y + j // 2, SIDE) * 2 + j % 2 for j in range(8)]
    blocks = []
    for j in range(8):
        blocks.append(fetch((act.at[rolls[j]], grad.at[rolls[j]]), (acts.at[j], grads.at[j]), sems.at[pl.ds(2 * j, 2)]))
    for group in copies:
        for copy in group:
            copy.wait()
    for j in range(8):
        for copy in blocks[j]:
            copy.wait()
        out[j, :, 0:64] = mm(acts[j], proj_in[...], NT)
        out[j, :, 64:128] = mm(grads[j], proj_out[...], NT)


def project(idx_in, idx_out, act, grad, bank_in_t, bank_out_t, flip):
    slots, width, model = act.shape[1], act.shape[2], grad.shape[2]
    return pl.pallas_call(
        functools.partial(project_kernel, flip=flip),
        out_shape=jax.ShapeDtypeStruct((8, slots, 128), F32),
        in_specs=[SMEM] * 2 + [HBM] * 4,
        out_specs=VMEM,
        scratch_shapes=[
            pltpu.VMEM((8, slots, width), BF16), pltpu.VMEM((8, slots, model), BF16),
            pltpu.VMEM((64, width), BF16), pltpu.VMEM((64, model), BF16),
            pltpu.SemaphoreType.DMA((34,)),
        ],
        compiler_params=params(20),
        cost_estimate=cost(16 * slots * (width + model) * 256, 16 * slots * (width + model)),
        name="project",
    )(idx_in, idx_out, *in_hbm([act, grad, bank_in_t, bank_out_t]))


def slab_kernel(prior, out, rows, sems):
    _, _, _, y, core = place()
    first = (y * CORES + core) * SEG
    parts = [pl.ds(i * 8, 8) for i in range(SEG // 8)]
    reads = fetch(
        [prior.at[pl.ds(pl.multiple_of(first + i * 8, 8), 8)] for i in range(SEG // 8)],
        [rows.at[p] for p in parts], sems,
    )
    writes = []
    for i, read in enumerate(reads):
        read.wait()
        writes += fetch([rows.at[parts[i]]], [out.at[parts[i]]], sems.at[pl.ds(SEG // 8 + i, 1)])
    for write in writes:
        write.wait()


def own_slab(prior):
    shape = (SEG, prior.shape[1])
    return pl.pallas_call(
        slab_kernel,
        out_shape=pltpu.HBM(shape, F32),
        in_specs=[HBM],
        out_specs=HBM,
        scratch_shapes=[pltpu.VMEM(shape, F32), pltpu.SemaphoreType.DMA((SEG // 4,))],
        name="own_slab",
    )(*in_hbm([prior]))


def factor_kernel(lens, v0, v1, w1, w2, w3, out):
    _, _, _, y, core = place()
    slots = v0.shape[1]
    for r in range(2):
        total = (v0[r] + v1[r]) + (w1[r] + w2[r]) + w3[r]
        used = lax.broadcasted_iota(jnp.int32, (slots, 64), 0) < lens[core * 8 + y * 2 + r]
        grad = jnp.where(used, total[:, 64:128], 0.0)
        out[r] = mm3(split(grad), split(total[:, 0:64]), TN)


def factor(lens, pieces):
    return pl.pallas_call(
        factor_kernel,
        out_shape=jax.ShapeDtypeStruct((2, 64, 64), F32),
        in_specs=[SMEM] + [VMEM] * 5,
        out_specs=VMEM,
        name="factor",
    )(lens, *in_vmem(pieces))


def rowsum(value):
    return jnp.sum(value, axis=1, keepdims=True)


def put(stack, cols, value):
    half = stack.shape[0] // 2
    stack[0:half, cols], stack[half:, cols] = split(value)


def stacked(stack, hi, lo):
    half = stack.shape[0] // 2
    both = mm(stack[...], hi[...], NT)
    return both[0:half] + both[half:] + mm(stack[0:half, :], lo[...], NT)


BLOCKS = [slice(k * BLK, (k + 1) * BLK) for k in range(16)]


def start_kernel(b0, b1, b2, b3, start, stack, pieces, sems):
    begin = fetch((b0, b1, b2, b3), [pieces.at[i] for i in range(4)], sems)
    _, _, _, y, _ = place()
    for d in range(SIDE):
        begin[d].wait()
        at = pl.ds(pl.multiple_of(lax.rem(y + SIDE - d, SIDE) * 8, 8), 8)
        for i in range(16):
            start[at, BLOCKS[i]] = pieces[d, i]
    for cols in BLOCKS:
        put(stack, cols, start[:, cols])


def assemble_start(pieces, n):
    sds = jax.ShapeDtypeStruct
    return pl.pallas_call(
        start_kernel,
        out_shape=(sds((COLS, n), F32), sds((2 * COLS, n), BF16)),
        in_specs=[HBM] * 4,
        out_specs=(VMEM, VMEM),
        scratch_shapes=[pltpu.VMEM((4, 16, 8, BLK), F32), pltpu.SemaphoreType.DMA((4,))],
        compiler_params=params(12),
        name="assemble_start",
    )(*in_hbm(pieces))


def prior_kernel(stack, prior_hbm, pri_hi, pri_lo, out, prior, sems):
    rows = [slice(i * SEG, (i + 1) * SEG) for i in range(16)]
    parts = fetch([prior_hbm.at[pl.ds(i * SEG, SEG)] for i in range(16)], [prior.at[pl.ds(i * SEG, SEG)] for i in range(16)], sems)
    _, _, _, y, core = place()
    t = y * CORES + core
    diag = jnp.zeros((SEG, 128), F32)
    on_diag = lax.broadcasted_iota(jnp.int32, (SEG, 128), 1) == lax.rem(t, 4) * SEG + lax.broadcasted_iota(jnp.int32, (SEG, 128), 0)
    half = stack.shape[0] // 2
    for g in range(4):
        for i in range(4 * g, 4 * g + 4):
            parts[i].wait()
            for cols in BLOCKS:
                pri_hi[rows[i], cols], pri_lo[rows[i], cols] = split(prior[rows[i], cols])
            at = pl.ds(pl.multiple_of(i * BLK + lax.div(t, 4) * 128, 128), 128)
            diag = diag + jnp.where(on_diag, prior[rows[i], at], 0.0)
        group = slice(g * 128, (g + 1) * 128)
        both = mm(stack[...], pri_hi[group, :], NT)
        out[0:COLS, group] = both[0:half] + both[half:] + mm(stack[0:half, :], pri_lo[group, :], NT)
    out[COLS : COLS + 8, :] = jnp.full((8, OWN), jnp.sum(diag), F32)


def prior_image(stack, prior):
    n = prior.shape[1]
    return pl.pallas_call(
        prior_kernel,
        out_shape=(
            pltpu.VMEM((OWN, n), BF16), pltpu.VMEM((OWN, n), BF16), jax.ShapeDtypeStruct((COLS + 8, OWN), F32),
        ),
        in_specs=[VMEM, HBM],
        out_specs=(VMEM,) * 3,
        scratch_shapes=[pltpu.VMEM((OWN, n), F32), pltpu.SemaphoreType.DMA((16,))],
        compiler_params=params(28),
        cost_estimate=cost(6 * 256 * OWN * n, 8 * OWN * n),
        name="prior_image",
    )(stack, *in_hbm([prior]))


def low_rank(stack, f_hi, f_lo, query, low):
    q = stacked(stack, f_hi, f_lo)
    query[...] = q
    parts = split(q * (1.0 / f_hi.shape[0]))
    for cols in BLOCKS:
        low[:, cols] = mm3(parts, (f_hi[:, cols], f_lo[:, cols]), NN)


def factors_kernel(n0, n1, n2, n3, m0, m1, m2, m3, stack, f_hi, f_lo, query, low, square_out, pieces, sems):
    copies = fetch((n0, n1, n2, n3, m0, m1, m2, m3), [pieces.at[i] for i in range(8)], sems)
    square = jnp.zeros((32, BLK), F32)
    for i in range(8):
        copies[i].wait()
        rows = slice(i * 32, (i + 1) * 32)
        for cols in BLOCKS:
            value = pieces[i, :, cols]
            square = square + value * value
            f_hi[rows, cols], f_lo[rows, cols] = split(value)
    square_out[...] = jnp.full(square_out.shape, jnp.sum(square), F32)
    low_rank(stack, f_hi, f_lo, query, low)


def take_factors(pieces, stack):
    n = stack.shape[1]
    sds = jax.ShapeDtypeStruct
    return pl.pallas_call(
        factors_kernel,
        out_shape=(
            pltpu.VMEM((256, n), BF16), pltpu.VMEM((256, n), BF16),
            sds((COLS, 256), F32), sds((COLS, n), F32), sds((8, 128), F32),
        ),
        in_specs=[HBM] * 8 + [VMEM],
        out_specs=(VMEM,) * 5,
        scratch_shapes=[pltpu.VMEM((8, 32, n), F32), pltpu.SemaphoreType.DMA((8,))],
        compiler_params=params(20),
        cost_estimate=cost(12 * 256 * 256 * n, 8 * 256 * n),
        name="take_factors",
    )(*in_hbm(pieces), stack)


def low_rank_step(stack, f_hi, f_lo):
    n = stack.shape[1]
    sds = jax.ShapeDtypeStruct
    return pl.pallas_call(
        low_rank,
        out_shape=(sds((COLS, 256), F32), sds((COLS, n), F32)),
        in_specs=[VMEM] * 3,
        out_specs=(VMEM,) * 2,
        compiler_params=params(16),
        cost_estimate=cost(12 * 256 * 256 * n, 4 * 256 * n),
        name="low_rank",
    )(stack, f_hi, f_lo)


def arrange(mine, theirs, perm, image):
    _, _, _, y, core = place()
    for d in range(SIDE):
        chip = lax.rem(y + SIDE - d, SIDE) * CORES
        for side, line in ((core, mine), (1 - core, theirs)):
            at = pl.ds(pl.multiple_of((chip + side) * OWN, OWN), OWN)
            perm[:, at] = line[0:COLS, d * OWN : (d + 1) * OWN]
    lane = lax.broadcasted_iota(jnp.int32, (COLS, 128), 1)
    low64 = lane < 64
    even = lax.rem(lane // SEG, 2) == 0
    for high in range(2):
        for g in range(4):
            x = [perm[:, pl.ds(((4 * high + k) * 4 + g) * 128, 128)] for k in range(4)]
            rolled = [pltpu.roll(v, 64, 1) for v in x]
            a0 = jnp.where(low64, x[0], rolled[2])
            a2 = jnp.where(low64, rolled[0], x[2])
            a1 = jnp.where(low64, x[1], rolled[3])
            a3 = jnp.where(low64, rolled[1], x[3])
            result = (
                jnp.where(even, a0, pltpu.roll(a1, SEG, 1)), jnp.where(even, pltpu.roll(a0, 128 - SEG, 1), a1),
                jnp.where(even, a2, pltpu.roll(a3, SEG, 1)), jnp.where(even, pltpu.roll(a2, 128 - SEG, 1), a3),
            )
            for m in range(4):
                first = (4 * g + m) * BLK + high * 128
                image[:, first : first + 128] = result[m]


def own_part(direc):
    _, _, _, y, core = place()
    t = y * CORES + core
    group = lax.broadcasted_iota(jnp.int32, (COLS, 128), 1) // SEG
    parts = []
    for g in range(4):
        value = jnp.zeros((COLS, 128), F32)
        for m in range(4):
            at = pl.ds(pl.multiple_of((4 * g + m) * BLK + lax.div(t, 4) * 128, 128), 128)
            moved = pltpu.roll(direc[:, at], lax.rem((m + 4 - lax.rem(t, 4)) * SEG, 128), 1)
            value = jnp.where(group == m, moved, value)
        parts.append(value)
    return jnp.concatenate(parts, axis=1)


def step_body(pieces, damping, norm, res_in, direc_in, low, query, pri_hi, pri_lo, res, direc, stack, perm, image):
    arrange(*pieces, perm, image)
    curve = jnp.zeros((COLS, 1), F32)
    for cols in BLOCKS:
        old = direc_in[:, cols]
        value = image[:, cols] + low[:, cols] + damping * old
        image[:, cols] = value
        curve = curve + rowsum(old * value)
    if norm is None:
        norm = jnp.zeros((COLS, 1), F32)
        for cols in BLOCKS:
            norm = norm + rowsum(res_in[:, cols] * res_in[:, cols])
    alpha = norm / curve
    fresh = jnp.zeros((COLS, 1), F32)
    for cols in BLOCKS:
        value = res_in[:, cols] - alpha * image[:, cols]
        res[:, cols] = value
        fresh = fresh + rowsum(value * value)
    beta = fresh / norm
    for cols in BLOCKS:
        value = res[:, cols] + beta * direc_in[:, cols]
        direc[:, cols] = value
        put(stack, cols, value)
    return alpha, fresh, stacked(stack, pri_hi, pri_lo)


def first_kernel(
    mine, theirs, start, low, query, square, pri_hi, pri_lo,
    res, direc, stack_out, rr, score, damp, out, stack, perm, image,
):
    pieces = (mine, theirs)
    trace = square[0:1, 0:1] * (1.0 / query.shape[1])
    for piece in pieces:
        for d in range(SIDE):
            trace = trace + piece[COLS : COLS + 1, d * OWN : d * OWN + 1]
    damping = 0.1 * trace / start.shape[1]
    damp[...] = jnp.broadcast_to(damping, damp.shape)
    alpha, fresh, out[...] = step_body(
        pieces, damping, None, start, start, low, query, pri_hi, pri_lo, res, direc, stack, perm, image
    )
    stack_out[...] = stack[...]
    rr[...] = jnp.broadcast_to(fresh, rr.shape)
    score[...] = alpha * query[...]


def step_kernel(
    mine, theirs, res_in, direc_in, rr_in, score_in, damp, low, query, pri_hi, pri_lo,
    res, direc, stack_out, rr, score, out, stack, perm, image,
):
    alpha, fresh, out[...] = step_body(
        (mine, theirs), damp[0:1, 0:1], rr_in[:, 0:1], res_in, direc_in, low, query, pri_hi, pri_lo,
        res, direc, stack, perm, image,
    )
    stack_out[...] = stack[...]
    rr[...] = jnp.broadcast_to(fresh, rr.shape)
    score[...] = score_in[...] + alpha * query[...]


def last_kernel(
    mine, theirs, res_in, direc_in, rr_in, score_in, damp, low, query, pri_hi, pri_lo,
    stack_out, rr, score, known, out, res, direc, stack, perm, image,
):
    alpha, fresh, own_image = step_body(
        (mine, theirs), damp[0:1, 0:1], rr_in[:, 0:1], res_in, direc_in, low, query, pri_hi, pri_lo,
        res, direc, stack, perm, image,
    )
    out[...] = jnp.broadcast_to(rowsum(own_part(direc) * own_image), out.shape)
    stack_out[...] = stack[...]
    size = jnp.zeros((COLS, 1), F32)
    for cols in BLOCKS:
        size = size + rowsum(direc[:, cols] * direc[:, cols])
    known[...] = jnp.broadcast_to(damp[0:1, 0:1] * size, known.shape)
    rr[...] = jnp.broadcast_to(fresh, rr.shape)
    score[...] = score_in[...] + alpha * query[...]


def cg_call(kernel, operands, outs, extra):
    n = operands[-1].shape[1]
    scratch = [pltpu.VMEM((COLS, n), F32)] * extra + [
        pltpu.VMEM((2 * COLS, n), BF16), pltpu.VMEM((COLS, n), F32), pltpu.VMEM((COLS, n), F32)
    ]
    return pl.pallas_call(
        kernel,
        out_shape=outs,
        in_specs=[VMEM] * len(operands),
        out_specs=(VMEM,) * len(outs),
        scratch_shapes=scratch,
        compiler_params=params(24),
        name=kernel.__name__[:-7],
    )(*operands)


def iota(shape, axis):
    return lax.broadcasted_iota(jnp.int32, shape, axis)


exact = functools.partial(lax.dot_general, precision=HIGHEST, preferred_element_type=F32)


def own_columns(y, core):
    return (iota((8, COLS), 1) == iota((8, COLS), 0) + 4 * (y * CORES + core)).astype(F32)


def query_kernel(stack, f_hi, f_lo, score, size, own):
    x, z, _, y, core = place()
    q = stacked(stack, f_hi, f_lo)
    rollouts = q.shape[1]
    size[...] = jnp.broadcast_to(rowsum(q * q) * (1.0 / rollouts), size.shape)
    pick = own_columns(y, core)
    both = jnp.concatenate([exact(pick, q, NN), exact(pick, score[...], NN)], axis=0)
    row = iota((rollouts, rollouts), 0)
    side = lax.rem(core + row // 128, CORES)
    third, second, first, last = row // 32 % 4, row // 8 % 4, row // 2 % 4, row % 2
    even = 1 - side
    dx = even * second + side * third
    dz = even * first + side * second
    dy = even * third + side * first
    home = lax.rem(x + SIDE - dx, SIDE) * SIDE + lax.rem(z + SIDE - dz, SIDE)
    rank = home * 16 + side * 8 + lax.rem(y + SIDE - dy, SIDE) * 2 + last
    own[...] = exact(both, (rank == iota((rollouts, rollouts), 1)).astype(F32), NN)


def last_query(stack, f_hi, f_lo, score):
    return pl.pallas_call(
        query_kernel,
        out_shape=(pltpu.VMEM((COLS, 128), F32), pltpu.VMEM((16, 256), F32)),
        in_specs=[VMEM] * 4,
        out_specs=(VMEM,) * 2,
        compiler_params=params(16),
        cost_estimate=cost(6 * 256 * 256 * f_hi.shape[1], 4 * 256 * f_hi.shape[1]),
        name="last_query",
    )(stack, f_hi, f_lo, score)


def finish_kernel(ours, theirs, known, size, rr, own, out):
    _, _, _, y, core = place()
    curve = (ours[...] + theirs[...]) + known[...] + size[...]
    alpha = exact(own_columns(y, core), rr[...] / curve, NN)[:, 0:1]
    ordered = own[8:16, :] + alpha * own[0:8, :]
    for i in range(16):
        part = ordered[:, i // 8 * 128 : (i // 8 + 1) * 128]
        shift = (128 - i % 8 * 16) % 128
        out[i] = pltpu.roll(part, shift, 1) if shift else part


def finish(ours, theirs, known, size, rr, own):
    return pl.pallas_call(
        finish_kernel,
        out_shape=jax.ShapeDtypeStruct((16, 8, 128), F32),
        in_specs=[VMEM] * 6,
        out_specs=VMEM,
        name="finish",
    )(*in_vmem([ours, theirs, known, size, rr, own]))


def place_kernel(parts, out, rows):
    for i in range(16):
        rows[4 * i : 4 * i + 4, :] = parts[i, 0:4, :]
    pick = lax.broadcasted_iota(jnp.int32, (16, 128), 0) == lax.broadcasted_iota(jnp.int32, (16, 128), 1)
    out[...] = lax.dot_general(pick.astype(F32), rows[...], NT, precision=HIGHEST, preferred_element_type=F32)


def place_scores(parts):
    return pl.pallas_call(
        place_kernel,
        out_shape=jax.ShapeDtypeStruct((16, 64), F32),
        in_specs=[VMEM],
        out_specs=VMEM,
        scratch_shapes=[pltpu.VMEM((64, 128), F32)],
        name="place_scores",
    )(parts)


BOTH = ("dp", "tensor")


def over_stage(value, stage):
    return [value] + [lax.ppermute(value, BOTH, shifted(d, stage)) for d in (1, 2, 3)]


def to_other_core(value):
    return lax.ppermute(value, "tensor", other_core())


def over_y(value):
    return [value] + [lax.ppermute(value, "tensor", along_y(d)) for d in (1, 2, 3)]


def join_image(pieces):
    line = jnp.concatenate(pieces, axis=1)
    return line, to_other_core(line)


def per_device(
    activations, out_grads, lengths, bank_in, index_in, bank_out, index_out, prior_cov, val_grads
):
    _, _, _, _, core = place()
    prior = lax.all_gather(own_slab(prior_cov), "dp", axis=0, tiled=True)

    tokens = (index_in, index_out, activations, out_grads, bank_in.transpose(0, 2, 1), bank_out.transpose(0, 2, 1))
    theirs = project(*tokens, True)
    from_core = to_other_core(theirs)
    mine = project(*tokens, False)
    to_y = [mine[2 * d : 2 * d + 2] + from_core[2 * d : 2 * d + 2] for d in (1, 2, 3)]
    to_y, start_here = lax.optimization_barrier((to_y, val_grads.T.reshape(16, 4, BLK)))
    from_y = [lax.ppermute(v, "tensor", along_y(d)) for d, v in zip((1, 2, 3), to_y)]
    start_here = lax.all_to_all(start_here, "dp", 0, 0, tiled=True)
    lengths, start_here = lax.optimization_barrier((lengths, start_here))

    own = factor(lengths, [mine[0:2], from_core[0:2], *from_y]).reshape(2, 4096)
    part = jnp.concatenate(over_stage(own, 0), axis=0)
    start_there = to_other_core(start_here)
    start_pair = jnp.where(
        core == 0,
        jnp.concatenate([start_here, start_there], axis=1),
        jnp.concatenate([start_there, start_here], axis=1),
    )
    part, start_pair = lax.optimization_barrier((part, start_pair))
    start_pieces = over_y(start_pair)
    moved = over_stage(part, 1)
    moved, start_pieces = lax.optimization_barrier((moved, start_pieces))
    near = over_stage(jnp.concatenate(moved, axis=0), 2)
    far = [to_other_core(piece) for piece in near]

    start, stack = assemble_start(start_pieces, prior_cov.shape[1])
    far, prior = lax.optimization_barrier((far, prior))
    pri_hi, pri_lo, out = prior_image(stack, prior)
    pieces = over_y(out)
    f_hi, f_lo, query, low, square = take_factors(near + far, stack)
    pieces, square = lax.optimization_barrier((pieces, square))
    sds = jax.ShapeDtypeStruct
    n = start.shape[1]
    vector, flat = sds((COLS, n), F32), sds((COLS, 128), F32)
    scores_shape, part_shape = sds((COLS, 256), F32), sds((COLS, OWN), F32)
    state_shapes = (vector, vector, sds((2 * COLS, n), BF16), flat, scores_shape)
    res, direc, stack, rr, score, damp, out = cg_call(
        first_kernel,
        (*join_image(pieces), start, low, query, square, pri_hi, pri_lo),
        (*state_shapes, sds((8, 128), F32), part_shape), 0,
    )
    for iteration in range(1, ITERS - 1):
        pieces = over_y(out)
        query, low = low_rank_step(stack, f_hi, f_lo)
        pieces, query, low = lax.optimization_barrier((pieces, query, low))
        operands = (*join_image(pieces), res, direc, rr, score, damp, low, query, pri_hi, pri_lo)
        if iteration + 2 < ITERS:
            res, direc, stack, rr, score, out = cg_call(step_kernel, operands, (*state_shapes, part_shape), 0)
        else:
            stack, rr, score, known, out = cg_call(
                last_kernel, operands,
                (
                    pltpu.VMEM((2 * COLS, n), BF16), pltpu.VMEM((COLS, 128), F32), pltpu.VMEM((COLS, 256), F32),
                    pltpu.VMEM((COLS, 128), F32), pltpu.VMEM((COLS, 128), F32),
                ),
                2,
            )
    pieces = over_y(out)
    size, own = last_query(stack, f_hi, f_lo, score)
    pieces, size = lax.optimization_barrier((pieces, size))
    ours = (pieces[0] + pieces[1]) + (pieces[2] + pieces[3])
    parts = finish(ours, to_other_core(ours), known, size, rr, own)
    return place_scores(lax.all_to_all(parts, "dp", 0, 0, tiled=True))


def solution(mesh):
    return jax.shard_map(
        per_device,
        mesh=mesh,
        in_specs=(
            P("dp", None, "tensor"),
            P("dp", None, "tensor"),
            P("dp"),
            P(),
            P("tensor"),
            P(),
            P("tensor"),
            P("dp", None),
            P("dp", "tensor"),
        ),
        out_specs=P("dp", "tensor"),
        check_vma=False,
    )
```

```python
import functools

import jax
import jax.numpy as jnp
from jax import lax
from jax.experimental import pallas as pl
from jax.experimental.pallas import tpu as pltpu
from jax.sharding import PartitionSpec as P

ITERS = 6
F32 = jnp.float32
BF16 = jnp.bfloat16
HIGHEST = lax.Precision.HIGHEST

NT = (((1,), (1,)), ((), ()))
NN = (((1,), (0,)), ((), ()))
TN = (((0,), (0,)), ((), ()))

SIDE = 4
CORES = 2
BLK = 256
SEG = 32
OWN = 512
COLS = 32
VMEM = pl.BlockSpec(memory_space=pltpu.VMEM)
SMEM = pl.BlockSpec(memory_space=pltpu.SMEM)
HBM = pl.BlockSpec(memory_space=pltpu.HBM)


def params(mib):
    return pltpu.CompilerParams(vmem_limit_bytes=mib << 20)


def in_vmem(values):
    return [pltpu.with_memory_space_constraint(v, pltpu.VMEM) for v in values]


def in_hbm(values):
    return [pltpu.with_memory_space_constraint(v, pltpu.HBM) for v in values]


def place():
    dp = lax.axis_index("dp").astype(jnp.int32)
    tensor = lax.axis_index("tensor").astype(jnp.int32)
    return lax.div(dp, SIDE), lax.rem(dp, SIDE), dp, lax.div(tensor, CORES), lax.rem(tensor, CORES)


def fetch(sources, targets, sems):
    copies = [pltpu.make_async_copy(a, b, sems.at[i]) for i, (a, b) in enumerate(zip(sources, targets))]
    for copy in copies:
        copy.start()
    return copies


def cost(flops, nbytes):
    return pl.CostEstimate(flops=flops, bytes_accessed=nbytes, transcendentals=0)


def split(value):
    high = value.astype(BF16)
    return high, (value - high.astype(F32)).astype(BF16)


def mm(a, b, dims):
    return lax.dot_general(a, b, dims, preferred_element_type=F32)


def mm3(a, b, dims):
    return mm(a[0], b[0], dims) + mm(a[1], b[0], dims) + mm(a[0], b[1], dims)


def along_z(step):
    return [(i, (i // SIDE) * SIDE + (i + step) % SIDE) for i in range(16)]


def along_x(step):
    return [(i, (i + step * SIDE) % 16) for i in range(16)]


def along_y(step):
    return [(i, (i + step * CORES) % 8) for i in range(8)]


def other_core():
    return [(i, i ^ 1) for i in range(8)]


ORDER = ("zxy", "yzx")


def shifted(step, stage):
    pairs = []
    for dp in range(16):
        for tensor in range(8):
            axis = ORDER[tensor % CORES][stage]
            to_dp = {"x": along_x, "z": along_z}[axis](step)[dp][1] if axis != "y" else dp
            to_tensor = along_y(step)[tensor][1] if axis == "y" else tensor
            pairs.append((dp * 8 + tensor, to_dp * 8 + to_tensor))
    return pairs


def project_kernel(
    idx_in, idx_out, act, grad, bank_in, bank_out, out, acts, grads, proj_in, proj_out, sems, *, flip
):
    _, _, _, y, core = place()
    side = 1 - core if flip else core
    copies = []
    for i, (index, bank, proj) in enumerate(((idx_in, bank_in, proj_in), (idx_out, bank_out, proj_out))):
        blocks = proj.shape[1] // 128
        copies.append(
            fetch(
                [bank.at[index[b]] for b in range(blocks)],
                [proj.at[:, pl.ds(b * 128, 128)] for b in range(blocks)],
                sems.at[pl.ds(16 + 14 * i, blocks)],
            )
        )
    rolls = [side * 8 + lax.rem(y + j // 2, SIDE) * 2 + j % 2 for j in range(8)]
    blocks = []
    for j in range(8):
        blocks.append(fetch((act.at[rolls[j]], grad.at[rolls[j]]), (acts.at[j], grads.at[j]), sems.at[pl.ds(2 * j, 2)]))
    for group in copies:
        for copy in group:
            copy.wait()
    for j in range(8):
        for copy in blocks[j]:
            copy.wait()
        out[j, :, 0:64] = mm(acts[j], proj_in[...], NT)
        out[j, :, 64:128] = mm(grads[j], proj_out[...], NT)


def project(idx_in, idx_out, act, grad, bank_in_t, bank_out_t, flip):
    slots, width, model = act.shape[1], act.shape[2], grad.shape[2]
    return pl.pallas_call(
        functools.partial(project_kernel, flip=flip),
        out_shape=jax.ShapeDtypeStruct((8, slots, 128), F32),
        in_specs=[SMEM] * 2 + [HBM] * 4,
        out_specs=VMEM,
        scratch_shapes=[
            pltpu.VMEM((8, slots, width), BF16), pltpu.VMEM((8, slots, model), BF16),
            pltpu.VMEM((64, width), BF16), pltpu.VMEM((64, model), BF16),
            pltpu.SemaphoreType.DMA((34,)),
        ],
        compiler_params=params(20),
        cost_estimate=cost(16 * slots * (width + model) * 256, 16 * slots * (width + model)),
        name="project",
    )(idx_in, idx_out, *in_hbm([act, grad, bank_in_t, bank_out_t]))


def slab_kernel(prior, out, rows, sems):
    _, _, _, y, core = place()
    first = (y * CORES + core) * SEG
    parts = [pl.ds(i * 8, 8) for i in range(SEG // 8)]
    reads = fetch(
        [prior.at[pl.ds(pl.multiple_of(first + i * 8, 8), 8)] for i in range(SEG // 8)],
        [rows.at[p] for p in parts], sems,
    )
    writes = []
    for i, read in enumerate(reads):
        read.wait()
        writes += fetch([rows.at[parts[i]]], [out.at[parts[i]]], sems.at[pl.ds(SEG // 8 + i, 1)])
    for write in writes:
        write.wait()


def own_slab(prior):
    shape = (SEG, prior.shape[1])
    return pl.pallas_call(
        slab_kernel,
        out_shape=pltpu.HBM(shape, F32),
        in_specs=[HBM],
        out_specs=HBM,
        scratch_shapes=[pltpu.VMEM(shape, F32), pltpu.SemaphoreType.DMA((SEG // 4,))],
        name="own_slab",
    )(*in_hbm([prior]))


def factor_kernel(lens, v0, v1, w1, w2, w3, out):
    _, _, _, y, core = place()
    slots = v0.shape[1]
    for r in range(2):
        total = (v0[r] + v1[r]) + (w1[r] + w2[r]) + w3[r]
        used = lax.broadcasted_iota(jnp.int32, (slots, 64), 0) < lens[core * 8 + y * 2 + r]
        grad = jnp.where(used, total[:, 64:128], 0.0)
        out[r] = mm3(split(grad), split(total[:, 0:64]), TN)


def factor(lens, pieces):
    return pl.pallas_call(
        factor_kernel,
        out_shape=jax.ShapeDtypeStruct((2, 64, 64), F32),
        in_specs=[SMEM] + [VMEM] * 5,
        out_specs=VMEM,
        name="factor",
    )(lens, *in_vmem(pieces))


def rowsum(value):
    return jnp.sum(value, axis=1, keepdims=True)


def put(stack, cols, value):
    half = stack.shape[0] // 2
    stack[0:half, cols], stack[half:, cols] = split(value)


def loop(count, body, carry=None):
    return lax.fori_loop(0, count, body, carry)


def part_at(i, size):
    return pl.ds(pl.multiple_of(i * size, size), size)


def against_prior(stack, hi, lo, out):
    half = stack.shape[0] // 2

    def rows(i, carry):
        at = part_at(i, 256)
        both = mm(stack[...], hi[at, :], NT)
        out[0:half, at] = both[0:half] + both[half:] + mm(stack[0:half, :], lo[at, :], NT)
        return carry

    loop(hi.shape[0] // 256, rows)


def against_factors(stack, hi, lo):
    half = stack.shape[0] // 2
    size = hi.shape[1] // 2

    def chunk(i, acc):
        at = part_at(i, size)
        both = mm(stack[:, at], hi[:, at], NT)
        return acc + both[0:half] + both[half:] + mm(stack[0:half, at], lo[:, at], NT)

    return loop(2, chunk, jnp.zeros((half, hi.shape[0]), F32))


BLOCKS = [slice(k * BLK, (k + 1) * BLK) for k in range(16)]


def start_kernel(b0, b1, b2, b3, start, stack, pieces, sems):
    begin = fetch((b0, b1, b2, b3), [pieces.at[i] for i in range(4)], sems)
    _, _, _, y, _ = place()
    for d in range(SIDE):
        begin[d].wait()
        at = pl.ds(pl.multiple_of(lax.rem(y + SIDE - d, SIDE) * 8, 8), 8)
        for i in range(16):
            start[at, BLOCKS[i]] = pieces[d, i]
    for cols in BLOCKS:
        put(stack, cols, start[:, cols])


def assemble_start(pieces, n):
    sds = jax.ShapeDtypeStruct
    return pl.pallas_call(
        start_kernel,
        out_shape=(sds((COLS, n), F32), sds((2 * COLS, n), BF16)),
        in_specs=[HBM] * 4,
        out_specs=(VMEM, VMEM),
        scratch_shapes=[pltpu.VMEM((4, 16, 8, BLK), F32), pltpu.SemaphoreType.DMA((4,))],
        compiler_params=params(12),
        name="assemble_start",
    )(*in_hbm(pieces))


def prior_kernel(stack, prior_hbm, pri_hi, pri_lo, out, prior, sems):
    pieces = [pl.ds(i * SEG, SEG) for i in range(16)]
    fetch([prior_hbm.at[p] for p in pieces], [prior.at[p] for p in pieces], sems)
    _, _, _, y, core = place()
    t = y * CORES + core
    on_diag = lax.broadcasted_iota(jnp.int32, (SEG, 128), 1) == lax.rem(t, 4) * SEG + lax.broadcasted_iota(jnp.int32, (SEG, 128), 0)

    def piece(i, diag):
        rows = part_at(i, SEG)
        pltpu.make_async_copy(prior_hbm.at[rows], prior.at[rows], sems.at[i]).wait()
        for cols in BLOCKS:
            pri_hi[rows, cols], pri_lo[rows, cols] = split(prior[rows, cols])
        at = pl.ds(pl.multiple_of(i * BLK + lax.div(t, 4) * 128, 128), 128)
        return diag + jnp.where(on_diag, prior[rows, at], 0.0)

    diag = loop(16, piece, jnp.zeros((SEG, 128), F32))
    against_prior(stack, pri_hi, pri_lo, out)
    out[COLS : COLS + 8, :] = jnp.full((8, OWN), jnp.sum(diag), F32)


def prior_image(stack, prior):
    n = prior.shape[1]
    return pl.pallas_call(
        prior_kernel,
        out_shape=(
            pltpu.VMEM((OWN, n), BF16), pltpu.VMEM((OWN, n), BF16), jax.ShapeDtypeStruct((COLS + 8, OWN), F32),
        ),
        in_specs=[VMEM, HBM],
        out_specs=(VMEM,) * 3,
        scratch_shapes=[pltpu.VMEM((OWN, n), F32), pltpu.SemaphoreType.DMA((16,))],
        compiler_params=params(28),
        cost_estimate=cost(6 * 256 * OWN * n, 8 * OWN * n),
        name="prior_image",
    )(stack, *in_hbm([prior]))


def low_rank(stack, f_hi, f_lo, query, low):
    q = against_factors(stack, f_hi, f_lo)
    query[...] = q
    parts = split(q * (1.0 / f_hi.shape[0]))

    def columns(i, carry):
        for k in range(4):
            at = part_at(4 * i + k, BLK)
            low[:, at] = mm3(parts, (f_hi[:, at], f_lo[:, at]), NN)
        return carry

    loop(4, columns)


def factors_kernel(n0, n1, n2, n3, m0, m1, m2, m3, stack, f_hi, f_lo, query, low, square_out, pieces, sems):
    copies = fetch((n0, n1, n2, n3, m0, m1, m2, m3), [pieces.at[i] for i in range(8)], sems)
    square = jnp.zeros((32, BLK), F32)
    for i in range(8):
        copies[i].wait()
        rows = slice(i * 32, (i + 1) * 32)
        for cols in BLOCKS:
            value = pieces[i, :, cols]
            square = square + value * value
            f_hi[rows, cols], f_lo[rows, cols] = split(value)
    square_out[...] = jnp.full(square_out.shape, jnp.sum(square), F32)
    low_rank(stack, f_hi, f_lo, query, low)


def take_factors(pieces, stack):
    n = stack.shape[1]
    sds = jax.ShapeDtypeStruct
    return pl.pallas_call(
        factors_kernel,
        out_shape=(
            pltpu.VMEM((256, n), BF16), pltpu.VMEM((256, n), BF16),
            sds((COLS, 256), F32), sds((COLS, n), F32), sds((8, 128), F32),
        ),
        in_specs=[HBM] * 8 + [VMEM],
        out_specs=(VMEM,) * 5,
        scratch_shapes=[pltpu.VMEM((8, 32, n), F32), pltpu.SemaphoreType.DMA((8,))],
        compiler_params=params(20),
        cost_estimate=cost(12 * 256 * 256 * n, 8 * 256 * n),
        name="take_factors",
    )(*in_hbm(pieces), stack)


def low_rank_step(stack, f_hi, f_lo):
    n = stack.shape[1]
    sds = jax.ShapeDtypeStruct
    return pl.pallas_call(
        low_rank,
        out_shape=(sds((COLS, 256), F32), sds((COLS, n), F32)),
        in_specs=[VMEM] * 3,
        out_specs=(VMEM,) * 2,
        compiler_params=params(16),
        cost_estimate=cost(12 * 256 * 256 * n, 4 * 256 * n),
        name="low_rank",
    )(stack, f_hi, f_lo)


def arrange(mine, theirs, perm, image):
    _, _, _, y, core = place()
    for d in range(SIDE):
        chip = lax.rem(y + SIDE - d, SIDE) * CORES
        for side, line in ((core, mine), (1 - core, theirs)):
            at = pl.ds(pl.multiple_of((chip + side) * OWN, OWN), OWN)
            perm[:, at] = line[0:COLS, d * OWN : (d + 1) * OWN]
    lane = lax.broadcasted_iota(jnp.int32, (COLS, 128), 1)
    low64 = lane < 64
    even = lax.rem(lane // SEG, 2) == 0
    for high in range(2):
        for g in range(4):
            x = [perm[:, pl.ds(((4 * high + k) * 4 + g) * 128, 128)] for k in range(4)]
            rolled = [pltpu.roll(v, 64, 1) for v in x]
            a0 = jnp.where(low64, x[0], rolled[2])
            a2 = jnp.where(low64, rolled[0], x[2])
            a1 = jnp.where(low64, x[1], rolled[3])
            a3 = jnp.where(low64, rolled[1], x[3])
            result = (
                jnp.where(even, a0, pltpu.roll(a1, SEG, 1)), jnp.where(even, pltpu.roll(a0, 128 - SEG, 1), a1),
                jnp.where(even, a2, pltpu.roll(a3, SEG, 1)), jnp.where(even, pltpu.roll(a2, 128 - SEG, 1), a3),
            )
            for m in range(4):
                first = (4 * g + m) * BLK + high * 128
                image[:, first : first + 128] = result[m]


def own_part(direc):
    _, _, _, y, core = place()
    t = y * CORES + core
    group = lax.broadcasted_iota(jnp.int32, (COLS, 128), 1) // SEG
    parts = []
    for g in range(4):
        value = jnp.zeros((COLS, 128), F32)
        for m in range(4):
            at = pl.ds(pl.multiple_of((4 * g + m) * BLK + lax.div(t, 4) * 128, 128), 128)
            moved = pltpu.roll(direc[:, at], lax.rem((m + 4 - lax.rem(t, 4)) * SEG, 128), 1)
            value = jnp.where(group == m, moved, value)
        parts.append(value)
    return jnp.concatenate(parts, axis=1)


def step_body(pieces, damping, norm, res_in, direc_in, low, query, pri_hi, pri_lo, out, res, direc, stack, perm, image):
    arrange(*pieces, perm, image)
    curve = jnp.zeros((COLS, 1), F32)
    for cols in BLOCKS:
        old = direc_in[:, cols]
        value = image[:, cols] + low[:, cols] + damping * old
        image[:, cols] = value
        curve = curve + rowsum(old * value)
    if norm is None:
        norm = jnp.zeros((COLS, 1), F32)
        for cols in BLOCKS:
            norm = norm + rowsum(res_in[:, cols] * res_in[:, cols])
    alpha = norm / curve
    fresh = jnp.zeros((COLS, 1), F32)
    for cols in BLOCKS:
        value = res_in[:, cols] - alpha * image[:, cols]
        res[:, cols] = value
        fresh = fresh + rowsum(value * value)
    beta = fresh / norm
    for cols in BLOCKS:
        value = res[:, cols] + beta * direc_in[:, cols]
        direc[:, cols] = value
        put(stack, cols, value)
    against_prior(stack, pri_hi, pri_lo, out)
    return alpha, fresh


def first_kernel(
    mine, theirs, start, low, query, square, pri_hi, pri_lo,
    res, direc, stack_out, rr, score, damp, out, stack, perm, image,
):
    pieces = (mine, theirs)
    trace = square[0:1, 0:1] * (1.0 / query.shape[1])
    for piece in pieces:
        for d in range(SIDE):
            trace = trace + piece[COLS : COLS + 1, d * OWN : d * OWN + 1]
    damping = 0.1 * trace / start.shape[1]
    damp[...] = jnp.broadcast_to(damping, damp.shape)
    alpha, fresh = step_body(
        pieces, damping, None, start, start, low, query, pri_hi, pri_lo, out, res, direc, stack, perm, image
    )
    stack_out[...] = stack[...]
    rr[...] = jnp.broadcast_to(fresh, rr.shape)
    score[...] = alpha * query[...]


def step_kernel(
    mine, theirs, res_in, direc_in, rr_in, score_in, damp, low, query, pri_hi, pri_lo,
    res, direc, stack_out, rr, score, out, stack, perm, image,
):
    alpha, fresh = step_body(
        (mine, theirs), damp[0:1, 0:1], rr_in[:, 0:1], res_in, direc_in, low, query, pri_hi, pri_lo,
        out, res, direc, stack, perm, image,
    )
    stack_out[...] = stack[...]
    rr[...] = jnp.broadcast_to(fresh, rr.shape)
    score[...] = score_in[...] + alpha * query[...]


def last_kernel(
    mine, theirs, res_in, direc_in, rr_in, score_in, damp, low, query, pri_hi, pri_lo,
    stack_out, rr, score, known, out, own_image, res, direc, stack, perm, image,
):
    alpha, fresh = step_body(
        (mine, theirs), damp[0:1, 0:1], rr_in[:, 0:1], res_in, direc_in, low, query, pri_hi, pri_lo,
        own_image, res, direc, stack, perm, image,
    )
    out[...] = jnp.broadcast_to(rowsum(own_part(direc) * own_image[...]), out.shape)
    stack_out[...] = stack[...]
    size = jnp.zeros((COLS, 1), F32)
    for cols in BLOCKS:
        size = size + rowsum(direc[:, cols] * direc[:, cols])
    known[...] = jnp.broadcast_to(damp[0:1, 0:1] * size, known.shape)
    rr[...] = jnp.broadcast_to(fresh, rr.shape)
    score[...] = score_in[...] + alpha * query[...]


def cg_call(kernel, operands, outs, extra):
    n = operands[-1].shape[1]
    scratch = ([pltpu.VMEM((COLS, OWN), F32)] if extra else []) + [pltpu.VMEM((COLS, n), F32)] * extra + [
        pltpu.VMEM((2 * COLS, n), BF16), pltpu.VMEM((COLS, n), F32), pltpu.VMEM((COLS, n), F32)
    ]
    return pl.pallas_call(
        kernel,
        out_shape=outs,
        in_specs=[VMEM] * len(operands),
        out_specs=(VMEM,) * len(outs),
        scratch_shapes=scratch,
        compiler_params=params(24),
        name=kernel.__name__[:-7],
    )(*operands)


def iota(shape, axis):
    return lax.broadcasted_iota(jnp.int32, shape, axis)


exact = functools.partial(lax.dot_general, precision=HIGHEST, preferred_element_type=F32)


def own_columns(y, core):
    return (iota((8, COLS), 1) == iota((8, COLS), 0) + 4 * (y * CORES + core)).astype(F32)


def query_kernel(stack, f_hi, f_lo, score, size, own):
    x, z, _, y, core = place()
    q = against_factors(stack, f_hi, f_lo)
    rollouts = q.shape[1]
    size[...] = jnp.broadcast_to(rowsum(q * q) * (1.0 / rollouts), size.shape)
    pick = own_columns(y, core)
    both = jnp.concatenate([exact(pick, q, NN), exact(pick, score[...], NN)], axis=0)
    row = iota((rollouts, rollouts), 0)
    side = lax.rem(core + row // 128, CORES)
    third, second, first, last = row // 32 % 4, row // 8 % 4, row // 2 % 4, row % 2
    even = 1 - side
    dx = even * second + side * third
    dz = even * first + side * second
    dy = even * third + side * first
    home = lax.rem(x + SIDE - dx, SIDE) * SIDE + lax.rem(z + SIDE - dz, SIDE)
    rank = home * 16 + side * 8 + lax.rem(y + SIDE - dy, SIDE) * 2 + last
    own[...] = exact(both, (rank == iota((rollouts, rollouts), 1)).astype(F32), NN)


def last_query(stack, f_hi, f_lo, score):
    return pl.pallas_call(
        query_kernel,
        out_shape=(pltpu.VMEM((COLS, 128), F32), pltpu.VMEM((16, 256), F32)),
        in_specs=[VMEM] * 4,
        out_specs=(VMEM,) * 2,
        compiler_params=params(16),
        cost_estimate=cost(6 * 256 * 256 * f_hi.shape[1], 4 * 256 * f_hi.shape[1]),
        name="last_query",
    )(stack, f_hi, f_lo, score)


def finish_kernel(ours, theirs, known, size, rr, own, out):
    _, _, _, y, core = place()
    curve = (ours[...] + theirs[...]) + known[...] + size[...]
    alpha = exact(own_columns(y, core), rr[...] / curve, NN)[:, 0:1]
    ordered = own[8:16, :] + alpha * own[0:8, :]
    for i in range(16):
        part = ordered[:, i // 8 * 128 : (i // 8 + 1) * 128]
        shift = (128 - i % 8 * 16) % 128
        out[i] = pltpu.roll(part, shift, 1) if shift else part


def finish(ours, theirs, known, size, rr, own):
    return pl.pallas_call(
        finish_kernel,
        out_shape=jax.ShapeDtypeStruct((16, 8, 128), F32),
        in_specs=[VMEM] * 6,
        out_specs=VMEM,
        name="finish",
    )(*in_vmem([ours, theirs, known, size, rr, own]))


def place_kernel(parts, out, rows):
    for i in range(16):
        rows[4 * i : 4 * i + 4, :] = parts[i, 0:4, :]
    pick = lax.broadcasted_iota(jnp.int32, (16, 128), 0) == lax.broadcasted_iota(jnp.int32, (16, 128), 1)
    out[...] = lax.dot_general(pick.astype(F32), rows[...], NT, precision=HIGHEST, preferred_element_type=F32)


def place_scores(parts):
    return pl.pallas_call(
        place_kernel,
        out_shape=jax.ShapeDtypeStruct((16, 64), F32),
        in_specs=[VMEM],
        out_specs=VMEM,
        scratch_shapes=[pltpu.VMEM((64, 128), F32)],
        name="place_scores",
    )(parts)


BOTH = ("dp", "tensor")


def over_stage(value, stage):
    return [value] + [lax.ppermute(value, BOTH, shifted(d, stage)) for d in (1, 2, 3)]


def to_other_core(value):
    return lax.ppermute(value, "tensor", other_core())


def over_y(value):
    return [value] + [lax.ppermute(value, "tensor", along_y(d)) for d in (1, 2, 3)]


def join_image(pieces):
    line = jnp.concatenate(pieces, axis=1)
    return line, to_other_core(line)


def per_device(
    activations, out_grads, lengths, bank_in, index_in, bank_out, index_out, prior_cov, val_grads
):
    _, _, _, _, core = place()
    prior = lax.all_gather(own_slab(prior_cov), "dp", axis=0, tiled=True)

    tokens = (index_in, index_out, activations, out_grads, bank_in.transpose(0, 2, 1), bank_out.transpose(0, 2, 1))
    theirs = project(*tokens, True)
    from_core = to_other_core(theirs)
    mine = project(*tokens, False)
    to_y = [mine[2 * d : 2 * d + 2] + from_core[2 * d : 2 * d + 2] for d in (1, 2, 3)]
    to_y, start_here = lax.optimization_barrier((to_y, val_grads.T.reshape(16, 4, BLK)))
    from_y = [lax.ppermute(v, "tensor", along_y(d)) for d, v in zip((1, 2, 3), to_y)]
    start_here = lax.all_to_all(start_here, "dp", 0, 0, tiled=True)
    lengths, start_here = lax.optimization_barrier((lengths, start_here))

    own = factor(lengths, [mine[0:2], from_core[0:2], *from_y]).reshape(2, 4096)
    part = jnp.concatenate(over_stage(own, 0), axis=0)
    start_there = to_other_core(start_here)
    start_pair = jnp.where(
        core == 0,
        jnp.concatenate([start_here, start_there], axis=1),
        jnp.concatenate([start_there, start_here], axis=1),
    )
    part, start_pair = lax.optimization_barrier((part, start_pair))
    start_pieces = over_y(start_pair)
    moved = over_stage(part, 1)
    moved, start_pieces = lax.optimization_barrier((moved, start_pieces))
    near = over_stage(jnp.concatenate(moved, axis=0), 2)
    start, stack = assemble_start(start_pieces, prior_cov.shape[1])
    near[1], stack = lax.optimization_barrier((near[1], stack))
    far = [to_other_core(piece) for piece in near]
    far, prior = lax.optimization_barrier((far, prior))
    pri_hi, pri_lo, out = prior_image(stack, prior)
    pieces = over_y(out)
    f_hi, f_lo, query, low, square = take_factors(near + far, stack)
    pieces, square = lax.optimization_barrier((pieces, square))
    sds = jax.ShapeDtypeStruct
    n = start.shape[1]
    vector, flat = sds((COLS, n), F32), sds((COLS, 128), F32)
    scores_shape, part_shape = sds((COLS, 256), F32), sds((COLS, OWN), F32)
    state_shapes = (vector, vector, sds((2 * COLS, n), BF16), flat, scores_shape)
    res, direc, stack, rr, score, damp, out = cg_call(
        first_kernel,
        (*join_image(pieces), start, low, query, square, pri_hi, pri_lo),
        (*state_shapes, sds((8, 128), F32), part_shape), 0,
    )
    for iteration in range(1, ITERS - 1):
        pieces = over_y(out)
        query, low = low_rank_step(stack, f_hi, f_lo)
        pieces, query, low = lax.optimization_barrier((pieces, query, low))
        operands = (*join_image(pieces), res, direc, rr, score, damp, low, query, pri_hi, pri_lo)
        if iteration + 2 < ITERS:
            res, direc, stack, rr, score, out = cg_call(step_kernel, operands, (*state_shapes, part_shape), 0)
        else:
            stack, rr, score, known, out = cg_call(
                last_kernel, operands,
                (
                    pltpu.VMEM((2 * COLS, n), BF16), pltpu.VMEM((COLS, 128), F32), pltpu.VMEM((COLS, 256), F32),
                    pltpu.VMEM((COLS, 128), F32), pltpu.VMEM((COLS, 128), F32),
                ),
                2,
            )
    pieces = over_y(out)
    size, own = last_query(stack, f_hi, f_lo, score)
    pieces, size = lax.optimization_barrier((pieces, size))
    ours = (pieces[0] + pieces[1]) + (pieces[2] + pieces[3])
    parts = finish(ours, to_other_core(ours), known, size, rr, own)
    return place_scores(lax.all_to_all(parts, "dp", 0, 0, tiled=True))


def solution(mesh):
    return jax.shard_map(
        per_device,
        mesh=mesh,
        in_specs=(
            P("dp", None, "tensor"),
            P("dp", None, "tensor"),
            P("dp"),
            P(),
            P("tensor"),
            P(),
            P("tensor"),
            P("dp", None),
            P("dp", "tensor"),
        ),
        out_specs=P("dp", "tensor"),
        check_vma=False,
    )
```

```python
import functools

import jax
import jax.numpy as jnp
from jax import lax
from jax.experimental import pallas as pl
from jax.experimental.pallas import tpu as pltpu
from jax.sharding import PartitionSpec as P

ITERS = 6
F32 = jnp.float32
BF16 = jnp.bfloat16
HIGHEST = lax.Precision.HIGHEST

NT = (((1,), (1,)), ((), ()))
NN = (((1,), (0,)), ((), ()))
TN = (((0,), (0,)), ((), ()))

SIDE = 4
CORES = 2
BLK = 256
SEG = 32
OWN = 512
COLS = 32
VMEM = pl.BlockSpec(memory_space=pltpu.VMEM)
SMEM = pl.BlockSpec(memory_space=pltpu.SMEM)
HBM = pl.BlockSpec(memory_space=pltpu.HBM)


def params(mib):
    return pltpu.CompilerParams(vmem_limit_bytes=mib << 20)


def in_vmem(values):
    return [pltpu.with_memory_space_constraint(v, pltpu.VMEM) for v in values]


def in_hbm(values):
    return [pltpu.with_memory_space_constraint(v, pltpu.HBM) for v in values]


def place():
    dp = lax.axis_index("dp").astype(jnp.int32)
    tensor = lax.axis_index("tensor").astype(jnp.int32)
    return lax.div(dp, SIDE), lax.rem(dp, SIDE), dp, lax.div(tensor, CORES), lax.rem(tensor, CORES)


def fetch(sources, targets, sems):
    copies = [pltpu.make_async_copy(a, b, sems.at[i]) for i, (a, b) in enumerate(zip(sources, targets))]
    for copy in copies:
        copy.start()
    return copies


def cost(flops, nbytes):
    return pl.CostEstimate(flops=flops, bytes_accessed=nbytes, transcendentals=0)


def split(value):
    high = value.astype(BF16)
    return high, (value - high.astype(F32)).astype(BF16)


def mm(a, b, dims):
    return lax.dot_general(a, b, dims, preferred_element_type=F32)


def mm3(a, b, dims):
    return mm(a[0], b[0], dims) + mm(a[1], b[0], dims) + mm(a[0], b[1], dims)


def along_z(step):
    return [(i, (i // SIDE) * SIDE + (i + step) % SIDE) for i in range(16)]


def along_x(step):
    return [(i, (i + step * SIDE) % 16) for i in range(16)]


def along_y(step):
    return [(i, (i + step * CORES) % 8) for i in range(8)]


def other_core():
    return [(i, i ^ 1) for i in range(8)]


ORDER = ("zxy", "yzx")


def shifted(step, stage):
    pairs = []
    for dp in range(16):
        for tensor in range(8):
            axis = ORDER[tensor % CORES][stage]
            to_dp = {"x": along_x, "z": along_z}[axis](step)[dp][1] if axis != "y" else dp
            to_tensor = along_y(step)[tensor][1] if axis == "y" else tensor
            pairs.append((dp * 8 + tensor, to_dp * 8 + to_tensor))
    return pairs


def project_kernel(
    idx_in, idx_out, act, grad, bank_in, bank_out, out, acts, grads, proj_in, proj_out, sems, *, flip
):
    _, _, _, y, core = place()
    side = 1 - core if flip else core
    copies = []
    for i, (index, bank, proj) in enumerate(((idx_in, bank_in, proj_in), (idx_out, bank_out, proj_out))):
        blocks = proj.shape[1] // 128
        copies.append(
            fetch(
                [bank.at[index[b]] for b in range(blocks)],
                [proj.at[:, pl.ds(b * 128, 128)] for b in range(blocks)],
                sems.at[pl.ds(16 + 14 * i, blocks)],
            )
        )
    rolls = [side * 8 + lax.rem(y + j // 2, SIDE) * 2 + j % 2 for j in range(8)]
    blocks = []
    for j in range(8):
        blocks.append(fetch((act.at[rolls[j]], grad.at[rolls[j]]), (acts.at[j], grads.at[j]), sems.at[pl.ds(2 * j, 2)]))
    for group in copies:
        for copy in group:
            copy.wait()
    for j in range(8):
        for copy in blocks[j]:
            copy.wait()
        out[j, :, 0:64] = mm(acts[j], proj_in[...], NT)
        out[j, :, 64:128] = mm(grads[j], proj_out[...], NT)


def project(idx_in, idx_out, act, grad, bank_in_t, bank_out_t, flip):
    slots, width, model = act.shape[1], act.shape[2], grad.shape[2]
    return pl.pallas_call(
        functools.partial(project_kernel, flip=flip),
        out_shape=jax.ShapeDtypeStruct((8, slots, 128), F32),
        in_specs=[SMEM] * 2 + [HBM] * 4,
        out_specs=VMEM,
        scratch_shapes=[
            pltpu.VMEM((8, slots, width), BF16), pltpu.VMEM((8, slots, model), BF16),
            pltpu.VMEM((64, width), BF16), pltpu.VMEM((64, model), BF16),
            pltpu.SemaphoreType.DMA((34,)),
        ],
        compiler_params=params(20),
        cost_estimate=cost(16 * slots * (width + model) * 256, 16 * slots * (width + model)),
        name="project",
    )(idx_in, idx_out, *in_hbm([act, grad, bank_in_t, bank_out_t]))


def slab_kernel(prior, out, rows, sems):
    _, _, _, y, core = place()
    first = (y * CORES + core) * SEG
    parts = [pl.ds(i * 8, 8) for i in range(SEG // 8)]
    reads = fetch(
        [prior.at[pl.ds(pl.multiple_of(first + i * 8, 8), 8)] for i in range(SEG // 8)],
        [rows.at[p] for p in parts], sems,
    )
    writes = []
    for i, read in enumerate(reads):
        read.wait()
        writes += fetch([rows.at[parts[i]]], [out.at[parts[i]]], sems.at[pl.ds(SEG // 8 + i, 1)])
    for write in writes:
        write.wait()


def own_slab(prior):
    shape = (SEG, prior.shape[1])
    return pl.pallas_call(
        slab_kernel,
        out_shape=pltpu.HBM(shape, F32),
        in_specs=[HBM],
        out_specs=HBM,
        scratch_shapes=[pltpu.VMEM(shape, F32), pltpu.SemaphoreType.DMA((SEG // 4,))],
        name="own_slab",
    )(*in_hbm([prior]))


def factor_kernel(lens, v0, v1, w1, w2, w3, out):
    _, _, _, y, core = place()
    slots = v0.shape[1]
    for r in range(2):
        total = (v0[r] + v1[r]) + (w1[r] + w2[r]) + w3[r]
        used = lax.broadcasted_iota(jnp.int32, (slots, 64), 0) < lens[core * 8 + y * 2 + r]
        grad = jnp.where(used, total[:, 64:128], 0.0)
        product = mm3(split(grad), split(total[:, 0:64]), TN)
        for k in range(64):
            out[r : r + 1, k * 64 : (k + 1) * 64] = product[k : k + 1, :]


def factor(lens, pieces):
    return pl.pallas_call(
        factor_kernel,
        out_shape=jax.ShapeDtypeStruct((2, 4096), F32),
        in_specs=[SMEM] + [VMEM] * 5,
        out_specs=VMEM,
        name="factor",
    )(lens, *in_vmem(pieces))


def rowsum(value):
    return jnp.sum(value, axis=1, keepdims=True)


def put(stack, cols, value):
    half = stack.shape[0] // 2
    stack[0:half, cols], stack[half:, cols] = split(value)


def loop(count, body, carry=None):
    return lax.fori_loop(0, count, body, carry)


def part_at(i, size):
    return pl.ds(pl.multiple_of(i * size, size), size)


def against_prior(stack, hi, lo, out):
    half = stack.shape[0] // 2

    def rows(i, carry):
        at = part_at(i, 256)
        both = mm(stack[...], hi[at, :], NT)
        out[0:half, at] = both[0:half] + both[half:] + mm(stack[0:half, :], lo[at, :], NT)
        return carry

    loop(hi.shape[0] // 256, rows)


def against_factors(stack, hi, lo):
    half = stack.shape[0] // 2
    size = hi.shape[1] // 2

    def chunk(i, acc):
        at = part_at(i, size)
        both = mm(stack[:, at], hi[:, at], NT)
        return acc + both[0:half] + both[half:] + mm(stack[0:half, at], lo[:, at], NT)

    return loop(2, chunk, jnp.zeros((half, hi.shape[0]), F32))


BLOCKS = [slice(k * BLK, (k + 1) * BLK) for k in range(16)]


def start_kernel(b0, b1, b2, b3, start, stack, pieces, sems):
    begin = fetch((b0, b1, b2, b3), [pieces.at[i] for i in range(4)], sems)
    _, _, _, y, _ = place()
    for d in range(SIDE):
        begin[d].wait()
        at = pl.ds(pl.multiple_of(lax.rem(y + SIDE - d, SIDE) * 8, 8), 8)
        for i in range(16):
            start[at, BLOCKS[i]] = pieces[d, i]
    for cols in BLOCKS:
        put(stack, cols, start[:, cols])


def assemble_start(pieces, n):
    sds = jax.ShapeDtypeStruct
    return pl.pallas_call(
        start_kernel,
        out_shape=(sds((COLS, n), F32), sds((2 * COLS, n), BF16)),
        in_specs=[HBM] * 4,
        out_specs=(VMEM, VMEM),
        scratch_shapes=[pltpu.VMEM((4, 16, 8, BLK), F32), pltpu.SemaphoreType.DMA((4,))],
        compiler_params=params(12),
        name="assemble_start",
    )(*in_hbm(pieces))


def prior_kernel(stack, prior_hbm, pri_hi, pri_lo, out, prior, sems):
    pieces = [pl.ds(i * SEG, SEG) for i in range(16)]
    fetch([prior_hbm.at[p] for p in pieces], [prior.at[p] for p in pieces], sems)
    _, _, _, y, core = place()
    t = y * CORES + core
    on_diag = lax.broadcasted_iota(jnp.int32, (SEG, 128), 1) == lax.rem(t, 4) * SEG + lax.broadcasted_iota(jnp.int32, (SEG, 128), 0)

    def piece(i, diag):
        rows = part_at(i, SEG)
        pltpu.make_async_copy(prior_hbm.at[rows], prior.at[rows], sems.at[i]).wait()
        for cols in BLOCKS:
            pri_hi[rows, cols], pri_lo[rows, cols] = split(prior[rows, cols])
        at = pl.ds(pl.multiple_of(i * BLK + lax.div(t, 4) * 128, 128), 128)
        return diag + jnp.where(on_diag, prior[rows, at], 0.0)

    diag = loop(16, piece, jnp.zeros((SEG, 128), F32))
    against_prior(stack, pri_hi, pri_lo, out)
    out[COLS : COLS + 8, :] = jnp.full((8, OWN), jnp.sum(diag), F32)


def prior_image(stack, prior):
    n = prior.shape[1]
    return pl.pallas_call(
        prior_kernel,
        out_shape=(
            pltpu.VMEM((OWN, n), BF16), pltpu.VMEM((OWN, n), BF16), jax.ShapeDtypeStruct((COLS + 8, OWN), F32),
        ),
        in_specs=[VMEM, HBM],
        out_specs=(VMEM,) * 3,
        scratch_shapes=[pltpu.VMEM((OWN, n), F32), pltpu.SemaphoreType.DMA((16,))],
        compiler_params=params(28),
        cost_estimate=cost(6 * 256 * OWN * n, 8 * OWN * n),
        name="prior_image",
    )(stack, *in_hbm([prior]))


def low_rank(stack, f_hi, f_lo, query, low):
    q = against_factors(stack, f_hi, f_lo)
    query[...] = q
    parts = split(q * (1.0 / f_hi.shape[0]))

    def columns(i, carry):
        for k in range(4):
            at = part_at(4 * i + k, BLK)
            low[:, at] = mm3(parts, (f_hi[:, at], f_lo[:, at]), NN)
        return carry

    loop(4, columns)


def factors_kernel(n0, n1, n2, n3, m0, m1, m2, m3, stack, f_hi, f_lo, query, low, square_out, pieces, sems):
    copies = fetch((n0, n1, n2, n3, m0, m1, m2, m3), [pieces.at[i] for i in range(8)], sems)
    square = jnp.zeros((32, BLK), F32)
    for i in range(8):
        copies[i].wait()
        rows = slice(i * 32, (i + 1) * 32)
        for cols in BLOCKS:
            value = pieces[i, :, cols]
            square = square + value * value
            f_hi[rows, cols], f_lo[rows, cols] = split(value)
    square_out[...] = jnp.full(square_out.shape, jnp.sum(square), F32)
    low_rank(stack, f_hi, f_lo, query, low)


def take_factors(pieces, stack):
    n = stack.shape[1]
    sds = jax.ShapeDtypeStruct
    return pl.pallas_call(
        factors_kernel,
        out_shape=(
            pltpu.VMEM((256, n), BF16), pltpu.VMEM((256, n), BF16),
            sds((COLS, 256), F32), sds((COLS, n), F32), sds((8, 128), F32),
        ),
        in_specs=[HBM] * 8 + [VMEM],
        out_specs=(VMEM,) * 5,
        scratch_shapes=[pltpu.VMEM((8, 32, n), F32), pltpu.SemaphoreType.DMA((8,))],
        compiler_params=params(20),
        cost_estimate=cost(12 * 256 * 256 * n, 8 * 256 * n),
        name="take_factors",
    )(*in_hbm(pieces), stack)


def low_rank_step(stack, f_hi, f_lo):
    n = stack.shape[1]
    sds = jax.ShapeDtypeStruct
    return pl.pallas_call(
        low_rank,
        out_shape=(sds((COLS, 256), F32), sds((COLS, n), F32)),
        in_specs=[VMEM] * 3,
        out_specs=(VMEM,) * 2,
        compiler_params=params(16),
        cost_estimate=cost(12 * 256 * 256 * n, 4 * 256 * n),
        name="low_rank",
    )(stack, f_hi, f_lo)


def arrange(mine, theirs, perm, image):
    _, _, _, y, core = place()
    for d in range(SIDE):
        chip = lax.rem(y + SIDE - d, SIDE) * CORES
        for side, line in ((core, mine), (1 - core, theirs)):
            at = pl.ds(pl.multiple_of((chip + side) * OWN, OWN), OWN)
            perm[:, at] = line[0:COLS, d * OWN : (d + 1) * OWN]
    lane = lax.broadcasted_iota(jnp.int32, (COLS, 128), 1)
    low64 = lane < 64
    even = lax.rem(lane // SEG, 2) == 0
    for high in range(2):
        for g in range(4):
            x = [perm[:, pl.ds(((4 * high + k) * 4 + g) * 128, 128)] for k in range(4)]
            rolled = [pltpu.roll(v, 64, 1) for v in x]
            a0 = jnp.where(low64, x[0], rolled[2])
            a2 = jnp.where(low64, rolled[0], x[2])
            a1 = jnp.where(low64, x[1], rolled[3])
            a3 = jnp.where(low64, rolled[1], x[3])
            result = (
                jnp.where(even, a0, pltpu.roll(a1, SEG, 1)), jnp.where(even, pltpu.roll(a0, 128 - SEG, 1), a1),
                jnp.where(even, a2, pltpu.roll(a3, SEG, 1)), jnp.where(even, pltpu.roll(a2, 128 - SEG, 1), a3),
            )
            for m in range(4):
                first = (4 * g + m) * BLK + high * 128
                image[:, first : first + 128] = result[m]


def own_part(direc):
    _, _, _, y, core = place()
    t = y * CORES + core
    group = lax.broadcasted_iota(jnp.int32, (COLS, 128), 1) // SEG
    parts = []
    for g in range(4):
        value = jnp.zeros((COLS, 128), F32)
        for m in range(4):
            at = pl.ds(pl.multiple_of((4 * g + m) * BLK + lax.div(t, 4) * 128, 128), 128)
            moved = pltpu.roll(direc[:, at], lax.rem((m + 4 - lax.rem(t, 4)) * SEG, 128), 1)
            value = jnp.where(group == m, moved, value)
        parts.append(value)
    return jnp.concatenate(parts, axis=1)


def step_body(pieces, damping, norm, res_in, direc_in, low, query, pri_hi, pri_lo, out, res, direc, stack, perm, image):
    arrange(*pieces, perm, image)
    curve = jnp.zeros((COLS, 1), F32)
    for cols in BLOCKS:
        old = direc_in[:, cols]
        value = image[:, cols] + low[:, cols] + damping * old
        image[:, cols] = value
        curve = curve + rowsum(old * value)
    if norm is None:
        norm = jnp.zeros((COLS, 1), F32)
        for cols in BLOCKS:
            norm = norm + rowsum(res_in[:, cols] * res_in[:, cols])
    alpha = norm / curve
    fresh = jnp.zeros((COLS, 1), F32)
    for cols in BLOCKS:
        value = res_in[:, cols] - alpha * image[:, cols]
        res[:, cols] = value
        fresh = fresh + rowsum(value * value)
    beta = fresh / norm
    for cols in BLOCKS:
        value = res[:, cols] + beta * direc_in[:, cols]
        direc[:, cols] = value
        put(stack, cols, value)
    against_prior(stack, pri_hi, pri_lo, out)
    return alpha, fresh


def first_kernel(
    mine, theirs, start, low, query, square, pri_hi, pri_lo,
    res, direc, stack_out, rr, score, damp, out, stack, perm, image,
):
    pieces = (mine, theirs)
    trace = square[0:1, 0:1] * (1.0 / query.shape[1])
    for piece in pieces:
        for d in range(SIDE):
            trace = trace + piece[COLS : COLS + 1, d * OWN : d * OWN + 1]
    damping = 0.1 * trace / start.shape[1]
    damp[...] = jnp.broadcast_to(damping, damp.shape)
    alpha, fresh = step_body(
        pieces, damping, None, start, start, low, query, pri_hi, pri_lo, out, res, direc, stack, perm, image
    )
    stack_out[...] = stack[...]
    rr[...] = jnp.broadcast_to(fresh, rr.shape)
    score[...] = alpha * query[...]


def step_kernel(
    mine, theirs, res_in, direc_in, rr_in, score_in, damp, low, query, pri_hi, pri_lo,
    res, direc, stack_out, rr, score, out, stack, perm, image,
):
    alpha, fresh = step_body(
        (mine, theirs), damp[0:1, 0:1], rr_in[:, 0:1], res_in, direc_in, low, query, pri_hi, pri_lo,
        out, res, direc, stack, perm, image,
    )
    stack_out[...] = stack[...]
    rr[...] = jnp.broadcast_to(fresh, rr.shape)
    score[...] = score_in[...] + alpha * query[...]


def last_kernel(
    mine, theirs, res_in, direc_in, rr_in, score_in, damp, low, query, pri_hi, pri_lo,
    stack_out, rr, score, known, out, own_image, res, direc, stack, perm, image,
):
    alpha, fresh = step_body(
        (mine, theirs), damp[0:1, 0:1], rr_in[:, 0:1], res_in, direc_in, low, query, pri_hi, pri_lo,
        own_image, res, direc, stack, perm, image,
    )
    out[...] = jnp.broadcast_to(rowsum(own_part(direc) * own_image[...]), out.shape)
    stack_out[...] = stack[...]
    size = jnp.zeros((COLS, 1), F32)
    for cols in BLOCKS:
        size = size + rowsum(direc[:, cols] * direc[:, cols])
    known[...] = jnp.broadcast_to(damp[0:1, 0:1] * size, known.shape)
    rr[...] = jnp.broadcast_to(fresh, rr.shape)
    score[...] = score_in[...] + alpha * query[...]


def cg_call(kernel, operands, outs, extra):
    n = operands[-1].shape[1]
    scratch = ([pltpu.VMEM((COLS, OWN), F32)] if extra else []) + [pltpu.VMEM((COLS, n), F32)] * extra + [
        pltpu.VMEM((2 * COLS, n), BF16), pltpu.VMEM((COLS, n), F32), pltpu.VMEM((COLS, n), F32)
    ]
    return pl.pallas_call(
        kernel,
        out_shape=outs,
        in_specs=[VMEM] * len(operands),
        out_specs=(VMEM,) * len(outs),
        scratch_shapes=scratch,
        compiler_params=params(24),
        name=kernel.__name__[:-7],
    )(*operands)


def iota(shape, axis):
    return lax.broadcasted_iota(jnp.int32, shape, axis)


exact = functools.partial(lax.dot_general, precision=HIGHEST, preferred_element_type=F32)


def own_columns(y, core):
    return (iota((8, COLS), 1) == iota((8, COLS), 0) + 4 * (y * CORES + core)).astype(F32)


def query_kernel(stack, f_hi, f_lo, score, size, own):
    x, z, _, y, core = place()
    q = against_factors(stack, f_hi, f_lo)
    rollouts = q.shape[1]
    size[...] = jnp.broadcast_to(rowsum(q * q) * (1.0 / rollouts), size.shape)
    pick = own_columns(y, core)
    both = jnp.concatenate([exact(pick, q, NN), exact(pick, score[...], NN)], axis=0)
    row = iota((rollouts, rollouts), 0)
    side = lax.rem(core + row // 128, CORES)
    third, second, first, last = row // 32 % 4, row // 8 % 4, row // 2 % 4, row % 2
    even = 1 - side
    dx = even * second + side * third
    dz = even * first + side * second
    dy = even * third + side * first
    home = lax.rem(x + SIDE - dx, SIDE) * SIDE + lax.rem(z + SIDE - dz, SIDE)
    rank = home * 16 + side * 8 + lax.rem(y + SIDE - dy, SIDE) * 2 + last
    own[...] = exact(both, (rank == iota((rollouts, rollouts), 1)).astype(F32), NN)


def last_query(stack, f_hi, f_lo, score):
    return pl.pallas_call(
        query_kernel,
        out_shape=(pltpu.VMEM((COLS, 128), F32), pltpu.VMEM((16, 256), F32)),
        in_specs=[VMEM] * 4,
        out_specs=(VMEM,) * 2,
        compiler_params=params(16),
        cost_estimate=cost(6 * 256 * 256 * f_hi.shape[1], 4 * 256 * f_hi.shape[1]),
        name="last_query",
    )(stack, f_hi, f_lo, score)


def finish_kernel(ours, theirs, known, size, rr, own, out):
    _, _, _, y, core = place()
    curve = (ours[...] + theirs[...]) + known[...] + size[...]
    alpha = exact(own_columns(y, core), rr[...] / curve, NN)[:, 0:1]
    ordered = own[8:16, :] + alpha * own[0:8, :]
    for i in range(16):
        part = ordered[:, i // 8 * 128 : (i // 8 + 1) * 128]
        shift = (128 - i % 8 * 16) % 128
        out[i] = pltpu.roll(part, shift, 1) if shift else part


def finish(ours, theirs, known, size, rr, own):
    return pl.pallas_call(
        finish_kernel,
        out_shape=jax.ShapeDtypeStruct((16, 8, 128), F32),
        in_specs=[VMEM] * 6,
        out_specs=VMEM,
        name="finish",
    )(*in_vmem([ours, theirs, known, size, rr, own]))


def place_kernel(parts, out, rows):
    for i in range(16):
        rows[4 * i : 4 * i + 4, :] = parts[i, 0:4, :]
    pick = lax.broadcasted_iota(jnp.int32, (16, 128), 0) == lax.broadcasted_iota(jnp.int32, (16, 128), 1)
    out[...] = lax.dot_general(pick.astype(F32), rows[...], NT, precision=HIGHEST, preferred_element_type=F32)


def place_scores(parts):
    return pl.pallas_call(
        place_kernel,
        out_shape=jax.ShapeDtypeStruct((16, 64), F32),
        in_specs=[VMEM],
        out_specs=VMEM,
        scratch_shapes=[pltpu.VMEM((64, 128), F32)],
        name="place_scores",
    )(parts)


BOTH = ("dp", "tensor")


def over_stage(value, stage):
    return [value] + [lax.ppermute(value, BOTH, shifted(d, stage)) for d in (1, 2, 3)]


def to_other_core(value):
    return lax.ppermute(value, "tensor", other_core())


def over_y(value):
    return [value] + [lax.ppermute(value, "tensor", along_y(d)) for d in (1, 2, 3)]


def join_image(pieces):
    line = jnp.concatenate(pieces, axis=1)
    return line, to_other_core(line)


def per_device(
    activations, out_grads, lengths, bank_in, index_in, bank_out, index_out, prior_cov, val_grads
):
    _, _, _, _, core = place()
    prior = lax.all_gather(own_slab(prior_cov), "dp", axis=0, tiled=True)

    tokens = (index_in, index_out, activations, out_grads, bank_in.transpose(0, 2, 1), bank_out.transpose(0, 2, 1))
    theirs = project(*tokens, True)
    from_core = to_other_core(theirs)
    mine = project(*tokens, False)
    to_y = [mine[2 * d : 2 * d + 2] + from_core[2 * d : 2 * d + 2] for d in (1, 2, 3)]
    from_y = [lax.ppermute(v, "tensor", along_y(d)) for d, v in zip((1, 2, 3), to_y)]
    own = factor(lengths, [mine[0:2], from_core[0:2], *from_y])
    part = jnp.concatenate(over_stage(own, 0), axis=0)
    part, start_here = lax.optimization_barrier((part, val_grads.T.reshape(16, 4, BLK)))
    moved = over_stage(part, 1)
    start_here = lax.all_to_all(start_here, "dp", 0, 0, tiled=True)
    moved, start_here = lax.optimization_barrier((moved, start_here))
    near = over_stage(jnp.concatenate(moved, axis=0), 2)
    start_there = to_other_core(start_here)
    start_pair = jnp.where(
        core == 0,
        jnp.concatenate([start_here, start_there], axis=1),
        jnp.concatenate([start_there, start_here], axis=1),
    )
    start_pieces = over_y(start_pair)
    near[0], start_pieces = lax.optimization_barrier((near[0], start_pieces))
    near[3], start_pieces = lax.optimization_barrier((near[3], start_pieces))
    start, stack = assemble_start(start_pieces, prior_cov.shape[1])
    near[1], stack = lax.optimization_barrier((near[1], stack))
    near[2], stack = lax.optimization_barrier((near[2], stack))
    far = [to_other_core(piece) for piece in near]
    far, prior = lax.optimization_barrier((far, prior))
    pri_hi, pri_lo, out = prior_image(stack, prior)
    pieces = over_y(out)
    f_hi, f_lo, query, low, square = take_factors(near + far, stack)
    pieces, square = lax.optimization_barrier((pieces, square))
    sds = jax.ShapeDtypeStruct
    n = start.shape[1]
    vector, flat = sds((COLS, n), F32), sds((COLS, 128), F32)
    scores_shape, part_shape = sds((COLS, 256), F32), sds((COLS, OWN), F32)
    state_shapes = (vector, vector, sds((2 * COLS, n), BF16), flat, scores_shape)
    res, direc, stack, rr, score, damp, out = cg_call(
        first_kernel,
        (*join_image(pieces), start, low, query, square, pri_hi, pri_lo),
        (*state_shapes, sds((8, 128), F32), part_shape), 0,
    )
    for iteration in range(1, ITERS - 1):
        pieces = over_y(out)
        query, low = low_rank_step(stack, f_hi, f_lo)
        pieces, query, low = lax.optimization_barrier((pieces, query, low))
        operands = (*join_image(pieces), res, direc, rr, score, damp, low, query, pri_hi, pri_lo)
        if iteration + 2 < ITERS:
            res, direc, stack, rr, score, out = cg_call(step_kernel, operands, (*state_shapes, part_shape), 0)
        else:
            stack, rr, score, known, out = cg_call(
                last_kernel, operands,
                (
                    pltpu.VMEM((2 * COLS, n), BF16), pltpu.VMEM((COLS, 128), F32), pltpu.VMEM((COLS, 256), F32),
                    pltpu.VMEM((COLS, 128), F32), pltpu.VMEM((COLS, 128), F32),
                ),
                2,
            )
    pieces = over_y(out)
    size, own = last_query(stack, f_hi, f_lo, score)
    pieces, size = lax.optimization_barrier((pieces, size))
    ours = (pieces[0] + pieces[1]) + (pieces[2] + pieces[3])
    parts = finish(ours, to_other_core(ours), known, size, rr, own)
    return place_scores(lax.all_to_all(parts, "dp", 0, 0, tiled=True))


def solution(mesh):
    return jax.shard_map(
        per_device,
        mesh=mesh,
        in_specs=(
            P("dp", None, "tensor"),
            P("dp", None, "tensor"),
            P("dp"),
            P(),
            P("tensor"),
            P(),
            P("tensor"),
            P("dp", None),
            P("dp", "tensor"),
        ),
        out_specs=P("dp", "tensor"),
        check_vma=False,
    )
```

```python
import functools

import jax
import jax.numpy as jnp
from jax import lax
from jax.experimental import pallas as pl
from jax.experimental.pallas import tpu as pltpu
from jax.sharding import PartitionSpec as P

ITERS = 6
F32 = jnp.float32
BF16 = jnp.bfloat16
HIGHEST = lax.Precision.HIGHEST

NT = (((1,), (1,)), ((), ()))
NN = (((1,), (0,)), ((), ()))
TN = (((0,), (0,)), ((), ()))

SIDE = 4
CORES = 2
BLK = 256
SEG = 32
OWN = 512
COLS = 32
VMEM = pl.BlockSpec(memory_space=pltpu.VMEM)
SMEM = pl.BlockSpec(memory_space=pltpu.SMEM)
HBM = pl.BlockSpec(memory_space=pltpu.HBM)


def params(mib):
    return pltpu.CompilerParams(vmem_limit_bytes=mib << 20)


def in_vmem(values):
    return [pltpu.with_memory_space_constraint(v, pltpu.VMEM) for v in values]


def in_hbm(values):
    return [pltpu.with_memory_space_constraint(v, pltpu.HBM) for v in values]


def place():
    dp = lax.axis_index("dp").astype(jnp.int32)
    tensor = lax.axis_index("tensor").astype(jnp.int32)
    return lax.div(dp, SIDE), lax.rem(dp, SIDE), dp, lax.div(tensor, CORES), lax.rem(tensor, CORES)


def fetch(sources, targets, sems):
    copies = [pltpu.make_async_copy(a, b, sems.at[i]) for i, (a, b) in enumerate(zip(sources, targets))]
    for copy in copies:
        copy.start()
    return copies


def cost(flops, nbytes):
    return pl.CostEstimate(flops=flops, bytes_accessed=nbytes, transcendentals=0)


def split(value):
    high = value.astype(BF16)
    return high, (value - high.astype(F32)).astype(BF16)


def mm(a, b, dims):
    return lax.dot_general(a, b, dims, preferred_element_type=F32)


def mm3(a, b, dims):
    return mm(a[0], b[0], dims) + mm(a[1], b[0], dims) + mm(a[0], b[1], dims)


def along_z(step):
    return [(i, (i // SIDE) * SIDE + (i + step) % SIDE) for i in range(16)]


def along_x(step):
    return [(i, (i + step * SIDE) % 16) for i in range(16)]


def along_y(step):
    return [(i, (i + step * CORES) % 8) for i in range(8)]


def other_core():
    return [(i, i ^ 1) for i in range(8)]


ORDER = ("yzx", "yxz")


def shifted(step, stage):
    pairs = []
    for dp in range(16):
        for tensor in range(8):
            axis = ORDER[tensor % CORES][stage]
            to_dp = {"x": along_x, "z": along_z}[axis](step)[dp][1] if axis != "y" else dp
            to_tensor = along_y(step)[tensor][1] if axis == "y" else tensor
            pairs.append((dp * 8 + tensor, to_dp * 8 + to_tensor))
    return pairs


def project_kernel(
    idx_in, idx_out, act, grad, bank_in, bank_out, out, acts, grads, proj_in, proj_out, sems, *, flip
):
    _, _, _, y, core = place()
    side = 1 - core if flip else core
    copies = []
    for i, (index, bank, proj) in enumerate(((idx_in, bank_in, proj_in), (idx_out, bank_out, proj_out))):
        blocks = proj.shape[1] // 128
        copies.append(
            fetch(
                [bank.at[index[b]] for b in range(blocks)],
                [proj.at[:, pl.ds(b * 128, 128)] for b in range(blocks)],
                sems.at[pl.ds(16 + 14 * i, blocks)],
            )
        )
    rolls = [side * 8 + lax.rem(y + j // 2, SIDE) * 2 + j % 2 for j in range(8)]
    blocks = []
    for j in range(8):
        blocks.append(fetch((act.at[rolls[j]], grad.at[rolls[j]]), (acts.at[j], grads.at[j]), sems.at[pl.ds(2 * j, 2)]))
    for group in copies:
        for copy in group:
            copy.wait()
    for j in range(8):
        for copy in blocks[j]:
            copy.wait()
        out[j, :, 0:64] = mm(acts[j], proj_in[...], NT)
        out[j, :, 64:128] = mm(grads[j], proj_out[...], NT)


def project(idx_in, idx_out, act, grad, bank_in_t, bank_out_t, flip):
    slots, width, model = act.shape[1], act.shape[2], grad.shape[2]
    return pl.pallas_call(
        functools.partial(project_kernel, flip=flip),
        out_shape=jax.ShapeDtypeStruct((8, slots, 128), F32),
        in_specs=[SMEM] * 2 + [HBM] * 4,
        out_specs=VMEM,
        scratch_shapes=[
            pltpu.VMEM((8, slots, width), BF16), pltpu.VMEM((8, slots, model), BF16),
            pltpu.VMEM((64, width), BF16), pltpu.VMEM((64, model), BF16),
            pltpu.SemaphoreType.DMA((34,)),
        ],
        compiler_params=params(20),
        cost_estimate=cost(16 * slots * (width + model) * 256, 16 * slots * (width + model)),
        name="project",
    )(idx_in, idx_out, *in_hbm([act, grad, bank_in_t, bank_out_t]))


def slab_kernel(prior, out, rows, sems):
    _, _, _, y, core = place()
    first = (y * CORES + core) * SEG
    parts = [pl.ds(i * 8, 8) for i in range(SEG // 8)]
    reads = fetch(
        [prior.at[pl.ds(pl.multiple_of(first + i * 8, 8), 8)] for i in range(SEG // 8)],
        [rows.at[p] for p in parts], sems,
    )
    writes = []
    for i, read in enumerate(reads):
        read.wait()
        writes += fetch([rows.at[parts[i]]], [out.at[parts[i]]], sems.at[pl.ds(SEG // 8 + i, 1)])
    for write in writes:
        write.wait()


def own_slab(prior):
    shape = (SEG, prior.shape[1])
    return pl.pallas_call(
        slab_kernel,
        out_shape=pltpu.HBM(shape, F32),
        in_specs=[HBM],
        out_specs=HBM,
        scratch_shapes=[pltpu.VMEM(shape, F32), pltpu.SemaphoreType.DMA((SEG // 4,))],
        name="own_slab",
    )(*in_hbm([prior]))


def factor_kernel(lens, v0, v1, w1, w2, w3, out):
    _, _, _, y, core = place()
    slots = v0.shape[1]
    for r in range(2):
        total = (v0[r] + v1[r]) + (w1[r] + w2[r]) + w3[r]
        used = lax.broadcasted_iota(jnp.int32, (slots, 64), 0) < lens[core * 8 + y * 2 + r]
        grad = jnp.where(used, total[:, 64:128], 0.0)
        product = mm3(split(grad), split(total[:, 0:64]), TN)
        for k in range(64):
            out[r : r + 1, k * 64 : (k + 1) * 64] = product[k : k + 1, :]


def factor(lens, pieces):
    return pl.pallas_call(
        factor_kernel,
        out_shape=jax.ShapeDtypeStruct((2, 4096), F32),
        in_specs=[SMEM] + [VMEM] * 5,
        out_specs=VMEM,
        name="factor",
    )(lens, *in_vmem(pieces))


def rowsum(value):
    return jnp.sum(value, axis=1, keepdims=True)


def put(stack, cols, value):
    half = stack.shape[0] // 2
    stack[0:half, cols], stack[half:, cols] = split(value)


def loop(count, body, carry=None):
    return lax.fori_loop(0, count, body, carry)


def part_at(i, size):
    return pl.ds(pl.multiple_of(i * size, size), size)


def against_prior(stack, hi, lo, out):
    half = stack.shape[0] // 2

    def rows(i, carry):
        at = part_at(i, 256)
        both = mm(stack[...], hi[at, :], NT)
        out[0:half, at] = both[0:half] + both[half:] + mm(stack[0:half, :], lo[at, :], NT)
        return carry

    loop(hi.shape[0] // 256, rows)


def against_factors(stack, hi, lo):
    half = stack.shape[0] // 2
    size = hi.shape[1] // 2

    def chunk(i, acc):
        at = part_at(i, size)
        both = mm(stack[:, at], hi[:, at], NT)
        return acc + both[0:half] + both[half:] + mm(stack[0:half, at], lo[:, at], NT)

    return loop(2, chunk, jnp.zeros((half, hi.shape[0]), F32))


BLOCKS = [slice(k * BLK, (k + 1) * BLK) for k in range(16)]


def start_kernel(b0, b1, b2, b3, start, stack, pieces, sems):
    begin = fetch((b0, b1, b2, b3), [pieces.at[i] for i in range(4)], sems)
    _, _, _, y, _ = place()
    for d in range(SIDE):
        begin[d].wait()
        at = pl.ds(pl.multiple_of(lax.rem(y + SIDE - d, SIDE) * 8, 8), 8)
        for i in range(16):
            start[at, BLOCKS[i]] = pieces[d, i]
    for cols in BLOCKS:
        put(stack, cols, start[:, cols])


def assemble_start(pieces, n):
    sds = jax.ShapeDtypeStruct
    return pl.pallas_call(
        start_kernel,
        out_shape=(sds((COLS, n), F32), sds((2 * COLS, n), BF16)),
        in_specs=[HBM] * 4,
        out_specs=(VMEM, VMEM),
        scratch_shapes=[pltpu.VMEM((4, 16, 8, BLK), F32), pltpu.SemaphoreType.DMA((4,))],
        compiler_params=params(12),
        name="assemble_start",
    )(*in_hbm(pieces))


def prior_kernel(stack, prior_hbm, pri_hi, pri_lo, out, prior, sems):
    pieces = [pl.ds(i * SEG, SEG) for i in range(16)]
    fetch([prior_hbm.at[p] for p in pieces], [prior.at[p] for p in pieces], sems)
    _, _, _, y, core = place()
    t = y * CORES + core
    on_diag = lax.broadcasted_iota(jnp.int32, (SEG, 128), 1) == lax.rem(t, 4) * SEG + lax.broadcasted_iota(jnp.int32, (SEG, 128), 0)

    def piece(i, diag):
        rows = part_at(i, SEG)
        pltpu.make_async_copy(prior_hbm.at[rows], prior.at[rows], sems.at[i]).wait()
        for cols in BLOCKS:
            pri_hi[rows, cols], pri_lo[rows, cols] = split(prior[rows, cols])
        at = pl.ds(pl.multiple_of(i * BLK + lax.div(t, 4) * 128, 128), 128)
        return diag + jnp.where(on_diag, prior[rows, at], 0.0)

    diag = loop(16, piece, jnp.zeros((SEG, 128), F32))
    against_prior(stack, pri_hi, pri_lo, out)
    out[COLS : COLS + 8, :] = jnp.full((8, OWN), jnp.sum(diag), F32)


def prior_image(stack, prior):
    n = prior.shape[1]
    return pl.pallas_call(
        prior_kernel,
        out_shape=(
            pltpu.VMEM((OWN, n), BF16), pltpu.VMEM((OWN, n), BF16), jax.ShapeDtypeStruct((COLS + 8, OWN), F32),
        ),
        in_specs=[VMEM, HBM],
        out_specs=(VMEM,) * 3,
        scratch_shapes=[pltpu.VMEM((OWN, n), F32), pltpu.SemaphoreType.DMA((16,))],
        compiler_params=params(28),
        cost_estimate=cost(6 * 256 * OWN * n, 8 * OWN * n),
        name="prior_image",
    )(stack, *in_hbm([prior]))


def low_rank(stack, f_hi, f_lo, query, low):
    q = against_factors(stack, f_hi, f_lo)
    query[...] = q
    parts = split(q * (1.0 / f_hi.shape[0]))

    def columns(i, carry):
        for k in range(4):
            at = part_at(4 * i + k, BLK)
            low[:, at] = mm3(parts, (f_hi[:, at], f_lo[:, at]), NN)
        return carry

    loop(4, columns)


def factors_kernel(n0, n1, n2, n3, m0, m1, m2, m3, stack, f_hi, f_lo, query, low, square_out, pieces, sems):
    copies = fetch((n0, n1, n2, n3, m0, m1, m2, m3), [pieces.at[i] for i in range(8)], sems)
    square = jnp.zeros((32, BLK), F32)
    for i in range(8):
        copies[i].wait()
        rows = slice(i * 32, (i + 1) * 32)
        for cols in BLOCKS:
            value = pieces[i, :, cols]
            square = square + value * value
            f_hi[rows, cols], f_lo[rows, cols] = split(value)
    square_out[...] = jnp.full(square_out.shape, jnp.sum(square), F32)
    low_rank(stack, f_hi, f_lo, query, low)


def take_factors(pieces, stack):
    n = stack.shape[1]
    sds = jax.ShapeDtypeStruct
    return pl.pallas_call(
        factors_kernel,
        out_shape=(
            pltpu.VMEM((256, n), BF16), pltpu.VMEM((256, n), BF16),
            sds((COLS, 256), F32), sds((COLS, n), F32), sds((8, 128), F32),
        ),
        in_specs=[HBM] * 8 + [VMEM],
        out_specs=(VMEM,) * 5,
        scratch_shapes=[pltpu.VMEM((8, 32, n), F32), pltpu.SemaphoreType.DMA((8,))],
        compiler_params=params(20),
        cost_estimate=cost(12 * 256 * 256 * n, 8 * 256 * n),
        name="take_factors",
    )(*in_hbm(pieces), stack)


def low_rank_step(stack, f_hi, f_lo):
    n = stack.shape[1]
    sds = jax.ShapeDtypeStruct
    return pl.pallas_call(
        low_rank,
        out_shape=(sds((COLS, 256), F32), sds((COLS, n), F32)),
        in_specs=[VMEM] * 3,
        out_specs=(VMEM,) * 2,
        compiler_params=params(16),
        cost_estimate=cost(12 * 256 * 256 * n, 4 * 256 * n),
        name="low_rank",
    )(stack, f_hi, f_lo)


def arrange(mine, theirs, perm, image):
    _, _, _, y, core = place()
    for d in range(SIDE):
        chip = lax.rem(y + SIDE - d, SIDE) * CORES
        for side, line in ((core, mine), (1 - core, theirs)):
            at = pl.ds(pl.multiple_of((chip + side) * OWN, OWN), OWN)
            perm[:, at] = line[0:COLS, d * OWN : (d + 1) * OWN]
    lane = lax.broadcasted_iota(jnp.int32, (COLS, 128), 1)
    low64 = lane < 64
    even = lax.rem(lane // SEG, 2) == 0
    for high in range(2):
        for g in range(4):
            x = [perm[:, pl.ds(((4 * high + k) * 4 + g) * 128, 128)] for k in range(4)]
            rolled = [pltpu.roll(v, 64, 1) for v in x]
            a0 = jnp.where(low64, x[0], rolled[2])
            a2 = jnp.where(low64, rolled[0], x[2])
            a1 = jnp.where(low64, x[1], rolled[3])
            a3 = jnp.where(low64, rolled[1], x[3])
            result = (
                jnp.where(even, a0, pltpu.roll(a1, SEG, 1)), jnp.where(even, pltpu.roll(a0, 128 - SEG, 1), a1),
                jnp.where(even, a2, pltpu.roll(a3, SEG, 1)), jnp.where(even, pltpu.roll(a2, 128 - SEG, 1), a3),
            )
            for m in range(4):
                first = (4 * g + m) * BLK + high * 128
                image[:, first : first + 128] = result[m]


def own_part(direc):
    _, _, _, y, core = place()
    t = y * CORES + core
    group = lax.broadcasted_iota(jnp.int32, (COLS, 128), 1) // SEG
    parts = []
    for g in range(4):
        value = jnp.zeros((COLS, 128), F32)
        for m in range(4):
            at = pl.ds(pl.multiple_of((4 * g + m) * BLK + lax.div(t, 4) * 128, 128), 128)
            moved = pltpu.roll(direc[:, at], lax.rem((m + 4 - lax.rem(t, 4)) * SEG, 128), 1)
            value = jnp.where(group == m, moved, value)
        parts.append(value)
    return jnp.concatenate(parts, axis=1)


def step_body(pieces, damping, norm, res_in, direc_in, low, query, pri_hi, pri_lo, out, res, direc, stack, perm, image):
    arrange(*pieces, perm, image)
    curve = jnp.zeros((COLS, 1), F32)
    for cols in BLOCKS:
        old = direc_in[:, cols]
        value = image[:, cols] + low[:, cols] + damping * old
        image[:, cols] = value
        curve = curve + rowsum(old * value)
    if norm is None:
        norm = jnp.zeros((COLS, 1), F32)
        for cols in BLOCKS:
            norm = norm + rowsum(res_in[:, cols] * res_in[:, cols])
    alpha = norm / curve
    fresh = jnp.zeros((COLS, 1), F32)
    for cols in BLOCKS:
        value = res_in[:, cols] - alpha * image[:, cols]
        res[:, cols] = value
        fresh = fresh + rowsum(value * value)
    beta = fresh / norm
    for cols in BLOCKS:
        value = res[:, cols] + beta * direc_in[:, cols]
        direc[:, cols] = value
        put(stack, cols, value)
    against_prior(stack, pri_hi, pri_lo, out)
    return alpha, fresh


def first_kernel(
    mine, theirs, start, low, query, square, pri_hi, pri_lo,
    res, direc, stack_out, rr, score, damp, out, stack, perm, image,
):
    pieces = (mine, theirs)
    trace = square[0:1, 0:1] * (1.0 / query.shape[1])
    for piece in pieces:
        for d in range(SIDE):
            trace = trace + piece[COLS : COLS + 1, d * OWN : d * OWN + 1]
    damping = 0.1 * trace / start.shape[1]
    damp[...] = jnp.broadcast_to(damping, damp.shape)
    alpha, fresh = step_body(
        pieces, damping, None, start, start, low, query, pri_hi, pri_lo, out, res, direc, stack, perm, image
    )
    stack_out[...] = stack[...]
    rr[...] = jnp.broadcast_to(fresh, rr.shape)
    score[...] = alpha * query[...]


def step_kernel(
    mine, theirs, res_in, direc_in, rr_in, score_in, damp, low, query, pri_hi, pri_lo,
    res, direc, stack_out, rr, score, out, stack, perm, image,
):
    alpha, fresh = step_body(
        (mine, theirs), damp[0:1, 0:1], rr_in[:, 0:1], res_in, direc_in, low, query, pri_hi, pri_lo,
        out, res, direc, stack, perm, image,
    )
    stack_out[...] = stack[...]
    rr[...] = jnp.broadcast_to(fresh, rr.shape)
    score[...] = score_in[...] + alpha * query[...]


def last_kernel(
    mine, theirs, res_in, direc_in, rr_in, score_in, damp, low, query, pri_hi, pri_lo,
    stack_out, rr, score, known, out, own_image, res, direc, stack, perm, image,
):
    alpha, fresh = step_body(
        (mine, theirs), damp[0:1, 0:1], rr_in[:, 0:1], res_in, direc_in, low, query, pri_hi, pri_lo,
        own_image, res, direc, stack, perm, image,
    )
    out[...] = jnp.broadcast_to(rowsum(own_part(direc) * own_image[...]), out.shape)
    stack_out[...] = stack[...]
    size = jnp.zeros((COLS, 1), F32)
    for cols in BLOCKS:
        size = size + rowsum(direc[:, cols] * direc[:, cols])
    known[...] = jnp.broadcast_to(damp[0:1, 0:1] * size, known.shape)
    rr[...] = jnp.broadcast_to(fresh, rr.shape)
    score[...] = score_in[...] + alpha * query[...]


def cg_call(kernel, operands, outs, extra):
    n = operands[-1].shape[1]
    scratch = ([pltpu.VMEM((COLS, OWN), F32)] if extra else []) + [pltpu.VMEM((COLS, n), F32)] * extra + [
        pltpu.VMEM((2 * COLS, n), BF16), pltpu.VMEM((COLS, n), F32), pltpu.VMEM((COLS, n), F32)
    ]
    return pl.pallas_call(
        kernel,
        out_shape=outs,
        in_specs=[VMEM] * len(operands),
        out_specs=(VMEM,) * len(outs),
        scratch_shapes=scratch,
        compiler_params=params(24),
        name=kernel.__name__[:-7],
    )(*operands)


def iota(shape, axis):
    return lax.broadcasted_iota(jnp.int32, shape, axis)


exact = functools.partial(lax.dot_general, precision=HIGHEST, preferred_element_type=F32)


def own_columns(y, core):
    return (iota((8, COLS), 1) == iota((8, COLS), 0) + 4 * (y * CORES + core)).astype(F32)


def query_kernel(stack, f_hi, f_lo, score, size, own):
    x, z, _, y, core = place()
    q = against_factors(stack, f_hi, f_lo)
    rollouts = q.shape[1]
    size[...] = jnp.broadcast_to(rowsum(q * q) * (1.0 / rollouts), size.shape)
    pick = own_columns(y, core)
    both = jnp.concatenate([exact(pick, q, NN), exact(pick, score[...], NN)], axis=0)
    row = iota((rollouts, rollouts), 0)
    side = lax.rem(core + row // 128, CORES)
    third, second, first, last = row // 32 % 4, row // 8 % 4, row // 2 % 4, row % 2
    even = 1 - side
    dx = even * third + side * second
    dz = even * second + side * third
    dy = first
    home = lax.rem(x + SIDE - dx, SIDE) * SIDE + lax.rem(z + SIDE - dz, SIDE)
    rank = home * 16 + side * 8 + lax.rem(y + SIDE - dy, SIDE) * 2 + last
    own[...] = exact(both, (rank == iota((rollouts, rollouts), 1)).astype(F32), NN)


def last_query(stack, f_hi, f_lo, score):
    return pl.pallas_call(
        query_kernel,
        out_shape=(pltpu.VMEM((COLS, 128), F32), pltpu.VMEM((16, 256), F32)),
        in_specs=[VMEM] * 4,
        out_specs=(VMEM,) * 2,
        compiler_params=params(16),
        cost_estimate=cost(6 * 256 * 256 * f_hi.shape[1], 4 * 256 * f_hi.shape[1]),
        name="last_query",
    )(stack, f_hi, f_lo, score)


def finish_kernel(ours, theirs, known, size, rr, own, out):
    _, _, _, y, core = place()
    curve = (ours[...] + theirs[...]) + known[...] + size[...]
    alpha = exact(own_columns(y, core), rr[...] / curve, NN)[:, 0:1]
    ordered = own[8:16, :] + alpha * own[0:8, :]
    for i in range(16):
        part = ordered[:, i // 8 * 128 : (i // 8 + 1) * 128]
        shift = (128 - i % 8 * 16) % 128
        out[i] = pltpu.roll(part, shift, 1) if shift else part


def finish(ours, theirs, known, size, rr, own):
    return pl.pallas_call(
        finish_kernel,
        out_shape=jax.ShapeDtypeStruct((16, 8, 128), F32),
        in_specs=[VMEM] * 6,
        out_specs=VMEM,
        name="finish",
    )(*in_vmem([ours, theirs, known, size, rr, own]))


def place_kernel(parts, out, rows):
    for i in range(16):
        rows[4 * i : 4 * i + 4, :] = parts[i, 0:4, :]
    pick = lax.broadcasted_iota(jnp.int32, (16, 128), 0) == lax.broadcasted_iota(jnp.int32, (16, 128), 1)
    out[...] = lax.dot_general(pick.astype(F32), rows[...], NT, precision=HIGHEST, preferred_element_type=F32)


def place_scores(parts):
    return pl.pallas_call(
        place_kernel,
        out_shape=jax.ShapeDtypeStruct((16, 64), F32),
        in_specs=[VMEM],
        out_specs=VMEM,
        scratch_shapes=[pltpu.VMEM((64, 128), F32)],
        name="place_scores",
    )(parts)


BOTH = ("dp", "tensor")


def over_stage(value, stage):
    return [value] + [lax.ppermute(value, BOTH, shifted(d, stage)) for d in (1, 2, 3)]


def to_other_core(value):
    return lax.ppermute(value, "tensor", other_core())


def over_y(value):
    return [value] + [lax.ppermute(value, "tensor", along_y(d)) for d in (1, 2, 3)]


def join_image(pieces):
    line = jnp.concatenate(pieces, axis=1)
    return line, to_other_core(line)


def per_device(
    activations, out_grads, lengths, bank_in, index_in, bank_out, index_out, prior_cov, val_grads
):
    _, _, _, _, core = place()
    prior = lax.all_gather(own_slab(prior_cov), "dp", axis=0, tiled=True)

    tokens = (index_in, index_out, activations, out_grads, bank_in.transpose(0, 2, 1), bank_out.transpose(0, 2, 1))
    theirs = project(*tokens, True)
    from_core = to_other_core(theirs)
    mine = project(*tokens, False)
    to_y = [mine[2 * d : 2 * d + 2] + from_core[2 * d : 2 * d + 2] for d in (1, 2, 3)]
    from_y = [lax.ppermute(v, "tensor", along_y(d)) for d, v in zip((1, 2, 3), to_y)]
    own = factor(lengths, [mine[0:2], from_core[0:2], *from_y])
    part = jnp.concatenate(over_stage(own, 0), axis=0)
    part, start_here = lax.optimization_barrier((part, val_grads.T.reshape(16, 4, BLK)))
    moved = over_stage(part, 1)
    start_here = lax.all_to_all(start_here, "dp", 0, 0, tiled=True)
    moved, start_here = lax.optimization_barrier((moved, start_here))
    near = over_stage(jnp.concatenate(moved, axis=0), 2)
    start_there = to_other_core(start_here)
    start_pair = jnp.where(
        core == 0,
        jnp.concatenate([start_here, start_there], axis=1),
        jnp.concatenate([start_there, start_here], axis=1),
    )
    start_pieces = over_y(start_pair)
    near[0], start_pieces = lax.optimization_barrier((near[0], start_pieces))
    near[3], start_pieces = lax.optimization_barrier((near[3], start_pieces))
    start, stack = assemble_start(start_pieces, prior_cov.shape[1])
    near[1], stack = lax.optimization_barrier((near[1], stack))
    near[2], stack = lax.optimization_barrier((near[2], stack))
    far = [to_other_core(piece) for piece in near]
    far, prior = lax.optimization_barrier((far, prior))
    pri_hi, pri_lo, out = prior_image(stack, prior)
    pieces = over_y(out)
    f_hi, f_lo, query, low, square = take_factors(near + far, stack)
    pieces, square = lax.optimization_barrier((pieces, square))
    sds = jax.ShapeDtypeStruct
    n = start.shape[1]
    vector, flat = sds((COLS, n), F32), sds((COLS, 128), F32)
    scores_shape, part_shape = sds((COLS, 256), F32), sds((COLS, OWN), F32)
    state_shapes = (vector, vector, sds((2 * COLS, n), BF16), flat, scores_shape)
    res, direc, stack, rr, score, damp, out = cg_call(
        first_kernel,
        (*join_image(pieces), start, low, query, square, pri_hi, pri_lo),
        (*state_shapes, sds((8, 128), F32), part_shape), 0,
    )
    for iteration in range(1, ITERS - 1):
        pieces = over_y(out)
        query, low = low_rank_step(stack, f_hi, f_lo)
        pieces, query, low = lax.optimization_barrier((pieces, query, low))
        operands = (*join_image(pieces), res, direc, rr, score, damp, low, query, pri_hi, pri_lo)
        if iteration + 2 < ITERS:
            res, direc, stack, rr, score, out = cg_call(step_kernel, operands, (*state_shapes, part_shape), 0)
        else:
            stack, rr, score, known, out = cg_call(
                last_kernel, operands,
                (
                    pltpu.VMEM((2 * COLS, n), BF16), pltpu.VMEM((COLS, 128), F32), pltpu.VMEM((COLS, 256), F32),
                    pltpu.VMEM((COLS, 128), F32), pltpu.VMEM((COLS, 128), F32),
                ),
                2,
            )
    pieces = over_y(out)
    size, own = last_query(stack, f_hi, f_lo, score)
    pieces, size = lax.optimization_barrier((pieces, size))
    ours = (pieces[0] + pieces[1]) + (pieces[2] + pieces[3])
    parts = finish(ours, to_other_core(ours), known, size, rr, own)
    return place_scores(lax.all_to_all(parts, "dp", 0, 0, tiled=True))


def solution(mesh):
    return jax.shard_map(
        per_device,
        mesh=mesh,
        in_specs=(
            P("dp", None, "tensor"),
            P("dp", None, "tensor"),
            P("dp"),
            P(),
            P("tensor"),
            P(),
            P("tensor"),
            P("dp", None),
            P("dp", "tensor"),
        ),
        out_specs=P("dp", "tensor"),
        check_vma=False,
    )
```

```python
import functools

import jax
import jax.numpy as jnp
from jax import lax
from jax.experimental import pallas as pl
from jax.experimental.pallas import tpu as pltpu
from jax.sharding import PartitionSpec as P

ITERS = 6
F32 = jnp.float32
BF16 = jnp.bfloat16
HIGHEST = lax.Precision.HIGHEST

NT = (((1,), (1,)), ((), ()))
NN = (((1,), (0,)), ((), ()))
TN = (((0,), (0,)), ((), ()))

SIDE = 4
CORES = 2
BLK = 256
SEG = 32
OWN = 512
COLS = 32
VMEM = pl.BlockSpec(memory_space=pltpu.VMEM)
SMEM = pl.BlockSpec(memory_space=pltpu.SMEM)
HBM = pl.BlockSpec(memory_space=pltpu.HBM)


def params(mib):
    return pltpu.CompilerParams(vmem_limit_bytes=mib << 20)


def in_vmem(values):
    return [pltpu.with_memory_space_constraint(v, pltpu.VMEM) for v in values]


def in_hbm(values):
    return [pltpu.with_memory_space_constraint(v, pltpu.HBM) for v in values]


def place():
    dp = lax.axis_index("dp").astype(jnp.int32)
    tensor = lax.axis_index("tensor").astype(jnp.int32)
    return lax.div(dp, SIDE), lax.rem(dp, SIDE), dp, lax.div(tensor, CORES), lax.rem(tensor, CORES)


def fetch(sources, targets, sems):
    copies = [pltpu.make_async_copy(a, b, sems.at[i]) for i, (a, b) in enumerate(zip(sources, targets))]
    for copy in copies:
        copy.start()
    return copies


def cost(flops, nbytes):
    return pl.CostEstimate(flops=flops, bytes_accessed=nbytes, transcendentals=0)


def split(value):
    high = value.astype(BF16)
    return high, (value - high.astype(F32)).astype(BF16)


def mm(a, b, dims):
    return lax.dot_general(a, b, dims, preferred_element_type=F32)


def mm3(a, b, dims):
    return mm(a[0], b[0], dims) + mm(a[1], b[0], dims) + mm(a[0], b[1], dims)


def along_z(step):
    return [(i, (i // SIDE) * SIDE + (i + step) % SIDE) for i in range(16)]


def along_x(step):
    return [(i, (i + step * SIDE) % 16) for i in range(16)]


def along_y(step):
    return [(i, (i + step * CORES) % 8) for i in range(8)]


def other_core():
    return [(i, i ^ 1) for i in range(8)]


ORDER = ("yzx", "yxz")


def shifted(step, stage):
    pairs = []
    for dp in range(16):
        for tensor in range(8):
            axis = ORDER[tensor % CORES][stage]
            to_dp = {"x": along_x, "z": along_z}[axis](step)[dp][1] if axis != "y" else dp
            to_tensor = along_y(step)[tensor][1] if axis == "y" else tensor
            pairs.append((dp * 8 + tensor, to_dp * 8 + to_tensor))
    return pairs


def project_kernel(
    idx_in, idx_out, act, grad, bank_in, bank_out, out, acts, grads, proj_in, proj_out, sems, *, flip
):
    _, _, _, y, core = place()
    side = 1 - core if flip else core
    copies = []
    for i, (index, bank, proj) in enumerate(((idx_in, bank_in, proj_in), (idx_out, bank_out, proj_out))):
        blocks = proj.shape[1] // 128
        copies.append(
            fetch(
                [bank.at[index[b]] for b in range(blocks)],
                [proj.at[:, pl.ds(b * 128, 128)] for b in range(blocks)],
                sems.at[pl.ds(16 + 14 * i, blocks)],
            )
        )
    rolls = [side * 8 + lax.rem(y + j // 2, SIDE) * 2 + j % 2 for j in range(8)]
    blocks = []
    for j in range(8):
        blocks.append(fetch((act.at[rolls[j]], grad.at[rolls[j]]), (acts.at[j], grads.at[j]), sems.at[pl.ds(2 * j, 2)]))
    for group in copies:
        for copy in group:
            copy.wait()
    for j in range(8):
        for copy in blocks[j]:
            copy.wait()
        out[j, :, 0:64] = mm(acts[j], proj_in[...], NT)
        out[j, :, 64:128] = mm(grads[j], proj_out[...], NT)


def project(idx_in, idx_out, act, grad, bank_in_t, bank_out_t, flip):
    slots, width, model = act.shape[1], act.shape[2], grad.shape[2]
    return pl.pallas_call(
        functools.partial(project_kernel, flip=flip),
        out_shape=jax.ShapeDtypeStruct((8, slots, 128), F32),
        in_specs=[SMEM] * 2 + [HBM] * 4,
        out_specs=VMEM,
        scratch_shapes=[
            pltpu.VMEM((8, slots, width), BF16), pltpu.VMEM((8, slots, model), BF16),
            pltpu.VMEM((64, width), BF16), pltpu.VMEM((64, model), BF16),
            pltpu.SemaphoreType.DMA((34,)),
        ],
        compiler_params=params(20),
        cost_estimate=cost(16 * slots * (width + model) * 256, 16 * slots * (width + model)),
        name="project",
    )(idx_in, idx_out, *in_hbm([act, grad, bank_in_t, bank_out_t]))


def slab_kernel(prior, out, rows, sems):
    _, _, _, y, core = place()
    first = (y * CORES + core) * SEG
    parts = [pl.ds(i * 8, 8) for i in range(SEG // 8)]
    reads = fetch(
        [prior.at[pl.ds(pl.multiple_of(first + i * 8, 8), 8)] for i in range(SEG // 8)],
        [rows.at[p] for p in parts], sems,
    )
    writes = []
    for i, read in enumerate(reads):
        read.wait()
        writes += fetch([rows.at[parts[i]]], [out.at[parts[i]]], sems.at[pl.ds(SEG // 8 + i, 1)])
    for write in writes:
        write.wait()


def own_slab(prior):
    shape = (SEG, prior.shape[1])
    return pl.pallas_call(
        slab_kernel,
        out_shape=pltpu.HBM(shape, F32),
        in_specs=[HBM],
        out_specs=HBM,
        scratch_shapes=[pltpu.VMEM(shape, F32), pltpu.SemaphoreType.DMA((SEG // 4,))],
        name="own_slab",
    )(*in_hbm([prior]))


def factor_kernel(lens, v0, v1, w1, w2, w3, out):
    _, _, _, y, core = place()
    slots = v0.shape[1]
    for r in range(2):
        total = (v0[r] + v1[r]) + (w1[r] + w2[r]) + w3[r]
        used = lax.broadcasted_iota(jnp.int32, (slots, 64), 0) < lens[core * 8 + y * 2 + r]
        grad = jnp.where(used, total[:, 64:128], 0.0)
        product = mm3(split(grad), split(total[:, 0:64]), TN)
        for k in range(64):
            out[r : r + 1, k * 64 : (k + 1) * 64] = product[k : k + 1, :]


def factor(lens, pieces):
    return pl.pallas_call(
        factor_kernel,
        out_shape=jax.ShapeDtypeStruct((2, 4096), F32),
        in_specs=[SMEM] + [VMEM] * 5,
        out_specs=VMEM,
        name="factor",
    )(lens, *in_vmem(pieces))


def rowsum(value):
    return jnp.sum(value, axis=1, keepdims=True)


def put(stack, cols, value):
    half = stack.shape[0] // 2
    stack[0:half, cols], stack[half:, cols] = split(value)


def loop(count, body, carry=None):
    return lax.fori_loop(0, count, body, carry)


def part_at(i, size):
    return pl.ds(pl.multiple_of(i * size, size), size)


def against_prior(stack, hi, lo, out):
    half = stack.shape[0] // 2

    def rows(i, carry):
        at = part_at(i, 256)
        both = mm(stack[...], hi[at, :], NT)
        out[0:half, at] = both[0:half] + both[half:] + mm(stack[0:half, :], lo[at, :], NT)
        return carry

    loop(hi.shape[0] // 256, rows)


def against_factors(stack, hi, lo):
    half = stack.shape[0] // 2
    size = hi.shape[1] // 2

    def chunk(i, acc):
        at = part_at(i, size)
        both = mm(stack[:, at], hi[:, at], NT)
        return acc + both[0:half] + both[half:] + mm(stack[0:half, at], lo[:, at], NT)

    return loop(2, chunk, jnp.zeros((half, hi.shape[0]), F32))


BLOCKS = [slice(k * BLK, (k + 1) * BLK) for k in range(16)]


def start_kernel(b0, b1, b2, b3, start, stack, pieces, sems):
    begin = fetch((b0, b1, b2, b3), [pieces.at[i] for i in range(4)], sems)
    _, _, _, y, _ = place()
    for d in range(SIDE):
        begin[d].wait()
        at = pl.ds(pl.multiple_of(lax.rem(y + SIDE - d, SIDE) * 8, 8), 8)
        for i in range(16):
            start[at, BLOCKS[i]] = pieces[d, i]
    for cols in BLOCKS:
        put(stack, cols, start[:, cols])


def assemble_start(pieces, n):
    sds = jax.ShapeDtypeStruct
    return pl.pallas_call(
        start_kernel,
        out_shape=(sds((COLS, n), F32), sds((2 * COLS, n), BF16)),
        in_specs=[HBM] * 4,
        out_specs=(VMEM, VMEM),
        scratch_shapes=[pltpu.VMEM((4, 16, 8, BLK), F32), pltpu.SemaphoreType.DMA((4,))],
        compiler_params=params(12),
        name="assemble_start",
    )(*in_hbm(pieces))


def prior_kernel(stack, prior_hbm, pri_hi, pri_lo, out, prior, sems):
    pieces = [pl.ds(i * SEG, SEG) for i in range(16)]
    fetch([prior_hbm.at[p] for p in pieces], [prior.at[p] for p in pieces], sems)
    _, _, _, y, core = place()
    t = y * CORES + core
    on_diag = lax.broadcasted_iota(jnp.int32, (SEG, 128), 1) == lax.rem(t, 4) * SEG + lax.broadcasted_iota(jnp.int32, (SEG, 128), 0)

    def piece(i, diag):
        rows = part_at(i, SEG)
        pltpu.make_async_copy(prior_hbm.at[rows], prior.at[rows], sems.at[i]).wait()
        for cols in BLOCKS:
            pri_hi[rows, cols], pri_lo[rows, cols] = split(prior[rows, cols])
        at = pl.ds(pl.multiple_of(i * BLK + lax.div(t, 4) * 128, 128), 128)
        return diag + jnp.where(on_diag, prior[rows, at], 0.0)

    diag = loop(16, piece, jnp.zeros((SEG, 128), F32))
    against_prior(stack, pri_hi, pri_lo, out)
    out[COLS : COLS + 8, :] = jnp.full((8, OWN), jnp.sum(diag), F32)


def prior_image(stack, prior):
    n = prior.shape[1]
    return pl.pallas_call(
        prior_kernel,
        out_shape=(
            pltpu.VMEM((OWN, n), BF16), pltpu.VMEM((OWN, n), BF16), jax.ShapeDtypeStruct((COLS + 8, OWN), F32),
        ),
        in_specs=[VMEM, HBM],
        out_specs=(VMEM,) * 3,
        scratch_shapes=[pltpu.VMEM((OWN, n), F32), pltpu.SemaphoreType.DMA((16,))],
        compiler_params=params(28),
        cost_estimate=cost(6 * 256 * OWN * n, 8 * OWN * n),
        name="prior_image",
    )(stack, *in_hbm([prior]))


def low_rank(stack, f_hi, f_lo, query, low):
    q = against_factors(stack, f_hi, f_lo)
    query[...] = q
    parts = split(q * (1.0 / f_hi.shape[0]))

    def columns(i, carry):
        for k in range(4):
            at = part_at(4 * i + k, BLK)
            low[:, at] = mm3(parts, (f_hi[:, at], f_lo[:, at]), NN)
        return carry

    loop(4, columns)


def factors_kernel(n0, n1, n2, n3, m0, m1, m2, m3, stack, f_hi, f_lo, query, low, square_out, pieces, sems):
    late = (n1, n2, n3, m2,)
    copies = fetch(late, [pieces.at[i] for i in range(len(late))], sems)
    sources = [n0, m0, m1, m3] + [pieces.at[i] for i in range(len(late))]
    order = (0, 4, 5, 7, 1, 2, 3, 6)
    square = jnp.zeros((32, BLK), F32)
    for position, (i, source) in enumerate(zip(order, sources)):
        if position >= 4:
            copies[position - 4].wait()
        rows = slice(i * 32, (i + 1) * 32)
        for cols in BLOCKS:
            value = source[:, cols]
            square = square + value * value
            f_hi[rows, cols], f_lo[rows, cols] = split(value)
    square_out[...] = jnp.full(square_out.shape, jnp.sum(square), F32)
    low_rank(stack, f_hi, f_lo, query, low)


def take_factors(pieces, stack):
    n = stack.shape[1]
    sds = jax.ShapeDtypeStruct
    return pl.pallas_call(
        factors_kernel,
        out_shape=(
            pltpu.VMEM((256, n), BF16), pltpu.VMEM((256, n), BF16),
            sds((COLS, 256), F32), sds((COLS, n), F32), sds((8, 128), F32),
        ),
        in_specs=[VMEM, HBM, HBM, HBM, VMEM, VMEM, HBM, VMEM, VMEM],
        out_specs=(VMEM,) * 5,
        scratch_shapes=[pltpu.VMEM((4, 32, n), F32), pltpu.SemaphoreType.DMA((4,))],
        compiler_params=params(20),
        cost_estimate=cost(12 * 256 * 256 * n, 8 * 256 * n),
        name="take_factors",
    )(*[(in_vmem if i in (0, 4, 5, 7,) else in_hbm)([v])[0] for i, v in enumerate(pieces)], stack)


def low_rank_step(stack, f_hi, f_lo):
    n = stack.shape[1]
    sds = jax.ShapeDtypeStruct
    return pl.pallas_call(
        low_rank,
        out_shape=(sds((COLS, 256), F32), sds((COLS, n), F32)),
        in_specs=[VMEM] * 3,
        out_specs=(VMEM,) * 2,
        compiler_params=params(16),
        cost_estimate=cost(12 * 256 * 256 * n, 4 * 256 * n),
        name="low_rank",
    )(stack, f_hi, f_lo)


def arrange(mine, theirs, perm, image):
    _, _, _, y, core = place()
    for d in range(SIDE):
        chip = lax.rem(y + SIDE - d, SIDE) * CORES
        for side, line in ((core, mine), (1 - core, theirs)):
            at = pl.ds(pl.multiple_of((chip + side) * OWN, OWN), OWN)
            perm[:, at] = line[0:COLS, d * OWN : (d + 1) * OWN]
    lane = lax.broadcasted_iota(jnp.int32, (COLS, 128), 1)
    low64 = lane < 64
    even = lax.rem(lane // SEG, 2) == 0
    for high in range(2):
        for g in range(4):
            x = [perm[:, pl.ds(((4 * high + k) * 4 + g) * 128, 128)] for k in range(4)]
            rolled = [pltpu.roll(v, 64, 1) for v in x]
            a0 = jnp.where(low64, x[0], rolled[2])
            a2 = jnp.where(low64, rolled[0], x[2])
            a1 = jnp.where(low64, x[1], rolled[3])
            a3 = jnp.where(low64, rolled[1], x[3])
            result = (
                jnp.where(even, a0, pltpu.roll(a1, SEG, 1)), jnp.where(even, pltpu.roll(a0, 128 - SEG, 1), a1),
                jnp.where(even, a2, pltpu.roll(a3, SEG, 1)), jnp.where(even, pltpu.roll(a2, 128 - SEG, 1), a3),
            )
            for m in range(4):
                first = (4 * g + m) * BLK + high * 128
                image[:, first : first + 128] = result[m]


def own_part(direc):
    _, _, _, y, core = place()
    t = y * CORES + core
    group = lax.broadcasted_iota(jnp.int32, (COLS, 128), 1) // SEG
    parts = []
    for g in range(4):
        value = jnp.zeros((COLS, 128), F32)
        for m in range(4):
            at = pl.ds(pl.multiple_of((4 * g + m) * BLK + lax.div(t, 4) * 128, 128), 128)
            moved = pltpu.roll(direc[:, at], lax.rem((m + 4 - lax.rem(t, 4)) * SEG, 128), 1)
            value = jnp.where(group == m, moved, value)
        parts.append(value)
    return jnp.concatenate(parts, axis=1)


def step_body(pieces, damping, norm, res_in, direc_in, low, query, pri_hi, pri_lo, out, res, direc, stack, perm, image):
    arrange(*pieces, perm, image)
    curve = jnp.zeros((COLS, 1), F32)
    for cols in BLOCKS:
        old = direc_in[:, cols]
        value = image[:, cols] + low[:, cols] + damping * old
        image[:, cols] = value
        curve = curve + rowsum(old * value)
    if norm is None:
        norm = jnp.zeros((COLS, 1), F32)
        for cols in BLOCKS:
            norm = norm + rowsum(res_in[:, cols] * res_in[:, cols])
    alpha = norm / curve
    fresh = jnp.zeros((COLS, 1), F32)
    for cols in BLOCKS:
        value = res_in[:, cols] - alpha * image[:, cols]
        res[:, cols] = value
        fresh = fresh + rowsum(value * value)
    beta = fresh / norm
    for cols in BLOCKS:
        value = res[:, cols] + beta * direc_in[:, cols]
        direc[:, cols] = value
        put(stack, cols, value)
    against_prior(stack, pri_hi, pri_lo, out)
    return alpha, fresh


def first_kernel(
    mine, theirs, start, low, query, square, pri_hi, pri_lo,
    res, direc, stack_out, rr, score, damp, out, stack, perm, image,
):
    pieces = (mine, theirs)
    trace = square[0:1, 0:1] * (1.0 / query.shape[1])
    for piece in pieces:
        for d in range(SIDE):
            trace = trace + piece[COLS : COLS + 1, d * OWN : d * OWN + 1]
    damping = 0.1 * trace / start.shape[1]
    damp[...] = jnp.broadcast_to(damping, damp.shape)
    alpha, fresh = step_body(
        pieces, damping, None, start, start, low, query, pri_hi, pri_lo, out, res, direc, stack, perm, image
    )
    stack_out[...] = stack[...]
    rr[...] = jnp.broadcast_to(fresh, rr.shape)
    score[...] = alpha * query[...]


def step_kernel(
    mine, theirs, res_in, direc_in, rr_in, score_in, damp, low, query, pri_hi, pri_lo,
    res, direc, stack_out, rr, score, out, stack, perm, image,
):
    alpha, fresh = step_body(
        (mine, theirs), damp[0:1, 0:1], rr_in[:, 0:1], res_in, direc_in, low, query, pri_hi, pri_lo,
        out, res, direc, stack, perm, image,
    )
    stack_out[...] = stack[...]
    rr[...] = jnp.broadcast_to(fresh, rr.shape)
    score[...] = score_in[...] + alpha * query[...]


def last_kernel(
    mine, theirs, res_in, direc_in, rr_in, score_in, damp, low, query, pri_hi, pri_lo,
    stack_out, rr, score, known, out, own_image, res, direc, stack, perm, image,
):
    alpha, fresh = step_body(
        (mine, theirs), damp[0:1, 0:1], rr_in[:, 0:1], res_in, direc_in, low, query, pri_hi, pri_lo,
        own_image, res, direc, stack, perm, image,
    )
    out[...] = jnp.broadcast_to(rowsum(own_part(direc) * own_image[...]), out.shape)
    stack_out[...] = stack[...]
    size = jnp.zeros((COLS, 1), F32)
    for cols in BLOCKS:
        size = size + rowsum(direc[:, cols] * direc[:, cols])
    known[...] = jnp.broadcast_to(damp[0:1, 0:1] * size, known.shape)
    rr[...] = jnp.broadcast_to(fresh, rr.shape)
    score[...] = score_in[...] + alpha * query[...]


def cg_call(kernel, operands, outs, extra):
    n = operands[-1].shape[1]
    scratch = ([pltpu.VMEM((COLS, OWN), F32)] if extra else []) + [pltpu.VMEM((COLS, n), F32)] * extra + [
        pltpu.VMEM((2 * COLS, n), BF16), pltpu.VMEM((COLS, n), F32), pltpu.VMEM((COLS, n), F32)
    ]
    return pl.pallas_call(
        kernel,
        out_shape=outs,
        in_specs=[VMEM] * len(operands),
        out_specs=(VMEM,) * len(outs),
        scratch_shapes=scratch,
        compiler_params=params(24),
        name=kernel.__name__[:-7],
    )(*operands)


def iota(shape, axis):
    return lax.broadcasted_iota(jnp.int32, shape, axis)


exact = functools.partial(lax.dot_general, precision=HIGHEST, preferred_element_type=F32)


def own_columns(y, core):
    return (iota((8, COLS), 1) == iota((8, COLS), 0) + 4 * (y * CORES + core)).astype(F32)


def query_kernel(stack, f_hi, f_lo, score, size, own):
    x, z, _, y, core = place()
    q = against_factors(stack, f_hi, f_lo)
    rollouts = q.shape[1]
    size[...] = jnp.broadcast_to(rowsum(q * q) * (1.0 / rollouts), size.shape)
    pick = own_columns(y, core)
    both = jnp.concatenate([exact(pick, q, NN), exact(pick, score[...], NN)], axis=0)
    row = iota((rollouts, rollouts), 0)
    side = lax.rem(core + row // 128, CORES)
    third, second, first, last = row // 32 % 4, row // 8 % 4, row // 2 % 4, row % 2
    even = 1 - side
    dx = even * third + side * second
    dz = even * second + side * third
    dy = first
    home = lax.rem(x + SIDE - dx, SIDE) * SIDE + lax.rem(z + SIDE - dz, SIDE)
    rank = home * 16 + side * 8 + lax.rem(y + SIDE - dy, SIDE) * 2 + last
    own[...] = exact(both, (rank == iota((rollouts, rollouts), 1)).astype(F32), NN)


def last_query(stack, f_hi, f_lo, score):
    return pl.pallas_call(
        query_kernel,
        out_shape=(pltpu.VMEM((COLS, 128), F32), pltpu.VMEM((16, 256), F32)),
        in_specs=[VMEM] * 4,
        out_specs=(VMEM,) * 2,
        compiler_params=params(16),
        cost_estimate=cost(6 * 256 * 256 * f_hi.shape[1], 4 * 256 * f_hi.shape[1]),
        name="last_query",
    )(stack, f_hi, f_lo, score)


def finish_kernel(ours, theirs, known, size, rr, own, out):
    _, _, _, y, core = place()
    curve = (ours[...] + theirs[...]) + known[...] + size[...]
    alpha = exact(own_columns(y, core), rr[...] / curve, NN)[:, 0:1]
    ordered = own[8:16, :] + alpha * own[0:8, :]
    for i in range(16):
        part = ordered[:, i // 8 * 128 : (i // 8 + 1) * 128]
        shift = (128 - i % 8 * 16) % 128
        out[i] = pltpu.roll(part, shift, 1) if shift else part


def finish(ours, theirs, known, size, rr, own):
    return pl.pallas_call(
        finish_kernel,
        out_shape=jax.ShapeDtypeStruct((16, 8, 128), F32),
        in_specs=[VMEM] * 6,
        out_specs=VMEM,
        name="finish",
    )(*in_vmem([ours, theirs, known, size, rr, own]))


def place_kernel(parts, out, rows):
    for i in range(16):
        rows[4 * i : 4 * i + 4, :] = parts[i, 0:4, :]
    pick = lax.broadcasted_iota(jnp.int32, (16, 128), 0) == lax.broadcasted_iota(jnp.int32, (16, 128), 1)
    out[...] = lax.dot_general(pick.astype(F32), rows[...], NT, precision=HIGHEST, preferred_element_type=F32)


def place_scores(parts):
    return pl.pallas_call(
        place_kernel,
        out_shape=jax.ShapeDtypeStruct((16, 64), F32),
        in_specs=[VMEM],
        out_specs=VMEM,
        scratch_shapes=[pltpu.VMEM((64, 128), F32)],
        name="place_scores",
    )(parts)


BOTH = ("dp", "tensor")


def over_stage(value, stage):
    return [value] + [lax.ppermute(value, BOTH, shifted(d, stage)) for d in (1, 2, 3)]


def to_other_core(value):
    return lax.ppermute(value, "tensor", other_core())


def over_y(value):
    return [value] + [lax.ppermute(value, "tensor", along_y(d)) for d in (1, 2, 3)]


def join_image(pieces):
    line = jnp.concatenate(pieces, axis=1)
    return line, to_other_core(line)


def per_device(
    activations, out_grads, lengths, bank_in, index_in, bank_out, index_out, prior_cov, val_grads
):
    _, _, _, _, core = place()
    prior = lax.all_gather(own_slab(prior_cov), "dp", axis=0, tiled=True)

    tokens = (index_in, index_out, activations, out_grads, bank_in.transpose(0, 2, 1), bank_out.transpose(0, 2, 1))
    theirs = project(*tokens, True)
    from_core = to_other_core(theirs)
    mine = project(*tokens, False)
    to_y = [mine[2 * d : 2 * d + 2] + from_core[2 * d : 2 * d + 2] for d in (1, 2, 3)]
    from_y = [lax.ppermute(v, "tensor", along_y(d)) for d, v in zip((1, 2, 3), to_y)]
    own = factor(lengths, [mine[0:2], from_core[0:2], *from_y])
    part = jnp.concatenate(over_stage(own, 0), axis=0)
    part, start_here = lax.optimization_barrier((part, val_grads.T.reshape(16, 4, BLK)))
    moved = over_stage(part, 1)
    start_here = lax.all_to_all(start_here, "dp", 0, 0, tiled=True)
    moved, start_here = lax.optimization_barrier((moved, start_here))
    near = over_stage(jnp.concatenate(moved, axis=0), 2)
    start_there = to_other_core(start_here)
    start_pair = jnp.where(
        core == 0,
        jnp.concatenate([start_here, start_there], axis=1),
        jnp.concatenate([start_there, start_here], axis=1),
    )
    start_pieces = over_y(start_pair)
    near[0], start_pieces = lax.optimization_barrier((near[0], start_pieces))
    near[3], start_pieces = lax.optimization_barrier((near[3], start_pieces))
    start, stack = assemble_start(start_pieces, prior_cov.shape[1])
    near[1], stack = lax.optimization_barrier((near[1], stack))
    near[2], stack = lax.optimization_barrier((near[2], stack))
    far = [to_other_core(piece) for piece in near]
    far, prior = lax.optimization_barrier((far, prior))
    pri_hi, pri_lo, out = prior_image(stack, prior)
    pieces = over_y(out)
    f_hi, f_lo, query, low, square = take_factors(near + far, stack)
    pieces, square = lax.optimization_barrier((pieces, square))
    sds = jax.ShapeDtypeStruct
    n = start.shape[1]
    vector, flat = sds((COLS, n), F32), sds((COLS, 128), F32)
    scores_shape, part_shape = sds((COLS, 256), F32), sds((COLS, OWN), F32)
    state_shapes = (vector, vector, sds((2 * COLS, n), BF16), flat, scores_shape)
    res, direc, stack, rr, score, damp, out = cg_call(
        first_kernel,
        (*join_image(pieces), start, low, query, square, pri_hi, pri_lo),
        (*state_shapes, sds((8, 128), F32), part_shape), 0,
    )
    for iteration in range(1, ITERS - 1):
        pieces = over_y(out)
        query, low = low_rank_step(stack, f_hi, f_lo)
        pieces, query, low = lax.optimization_barrier((pieces, query, low))
        operands = (*join_image(pieces), res, direc, rr, score, damp, low, query, pri_hi, pri_lo)
        if iteration + 2 < ITERS:
            res, direc, stack, rr, score, out = cg_call(step_kernel, operands, (*state_shapes, part_shape), 0)
        else:
            stack, rr, score, known, out = cg_call(
                last_kernel, operands,
                (
                    pltpu.VMEM((2 * COLS, n), BF16), pltpu.VMEM((COLS, 128), F32), pltpu.VMEM((COLS, 256), F32),
                    pltpu.VMEM((COLS, 128), F32), pltpu.VMEM((COLS, 128), F32),
                ),
                2,
            )
    pieces = over_y(out)
    size, own = last_query(stack, f_hi, f_lo, score)
    pieces, size = lax.optimization_barrier((pieces, size))
    ours = (pieces[0] + pieces[1]) + (pieces[2] + pieces[3])
    parts = finish(ours, to_other_core(ours), known, size, rr, own)
    return place_scores(lax.all_to_all(parts, "dp", 0, 0, tiled=True))


def solution(mesh):
    return jax.shard_map(
        per_device,
        mesh=mesh,
        in_specs=(
            P("dp", None, "tensor"),
            P("dp", None, "tensor"),
            P("dp"),
            P(),
            P("tensor"),
            P(),
            P("tensor"),
            P("dp", None),
            P("dp", "tensor"),
        ),
        out_specs=P("dp", "tensor"),
        check_vma=False,
    )
```
